32 devices in a mesh: dom: 32 (over z, y, x, core).
Axes of the slice: x: 2, y: 2, z: 4, core: 2. Of those that a mesh axis runs over, the one named last changes fastest.
Arguments:
- right_side: float32 [8, 524288], P(None, 'dom'), may hold values from -24 to 24, as said below
- stiffness: float32 [3, 125, 8192], P(None, None, 'dom'), may hold values from 0.005 to 0.05
- mass: float32 [125, 8192], P(None, 'dom'), may hold values from 0.5 to 2
- region: int32 [8192], P('dom'), may hold values from 0 to 2
- density: float32 [3], replicated, may hold values from 0.5 to 2
- elem_nodes: int32 [125, 8192], P(None, 'dom'), may hold values from 0 to 20479, as said below
- peer_rank: int32 [32, 5], P('dom'), may hold values from 0 to 31, as said below
- send_nodes: int32 [32, 5, 128], P('dom'), may hold values from 0 to 16383, as said below
Outputs:
- solution: float32 [8, 524288], P(None, 'dom')
- residual: float32 [8, 524288], P(None, 'dom')
The draws below stay inside these ranges and needn't reach their ends.
Inputs may be any that keep to these rules, and one draw needn't show every extreme that they name: `right_side`: A mean scale that rises along the partitions. `peer_rank`: the peers of partition r, in a drawn order: r + 1 and r - 1 modulo 32, and r XOR 2**k for 3 bit positions k between 1 and log2(32) - 1 that are the same for every partition, the highest one among them. Peers are mutual. `send_nodes`: repeats are possible within one list. `elem_nodes`: A value 16384 + s * 128 + c names slot c of what peer s shares with this partition. Elements 2 g and 2 g + 1 of a partition name own nodes only from 128 g to 128 g + 127, each of them at least once. List the received slots of a partition in the order of its peer_rank slots, slot c fastest, and repeat that list cyclically: for g < 64 the elements 2 g and 2 g + 1 also name exactly the entries g * 10 to (g + 1) * 10 - 1 of it, each once; other elements name no received slot.
All inputs are finite; a program needn't handle non-finite values.
Results may differ from the reference program's by a relative error of at most 0.0003.
Values sent between devices are 32-bit elements; how exact they have to be, the bound alone decides.
No kernel may reach another device: no remote copies, remote signals or barrier semaphores. Data moves between devices by JAX's collectives and lax.ppermute only.
A program may use at most 128 MiB of HBM per device.

```python
import math
import jax
import jax.numpy as jnp
import numpy as np
from jax import lax

NV = 8
NPE = 125
ELEM_DEV = 256
BND_DEV = 128
NODE_DEV = 16384
CAP = 128
NXOR = 3
NPEER = 5
GHOST_RUN = 10
ITERS = 2
ELEMS = 8192
NODES = 524288
N_DOM = 32


def peer_table(key):
    levels = N_DOM.bit_length() - 1
    inner_bits = jax.random.permutation(jax.random.fold_in(key, 11), levels - 2).astype(jnp.int32) + 1
    bit_list = jnp.concatenate([inner_bits[:NXOR - 1], jnp.array([levels - 1], jnp.int32)])
    rank_list = jnp.arange(N_DOM, dtype=jnp.int32)
    columns = [(rank_list + 1) % N_DOM, (rank_list + N_DOM - 1) % N_DOM]
    for position in range(NXOR):
        columns.append(jnp.bitwise_xor(rank_list, jnp.left_shift(jnp.int32(1), bit_list[position])))
    peer_grid = jnp.stack(columns, axis=1).astype(jnp.int32)
    slot_keys = jax.random.split(jax.random.fold_in(key, 12), N_DOM)
    slot_order = jax.vmap(lambda slot_key: jax.random.permutation(slot_key, NPEER))(slot_keys).astype(jnp.int32)
    return jnp.take_along_axis(peer_grid, slot_order, axis=1).astype(jnp.int32)


def draw_peer_rank(key, part):
    return peer_table(key)


def draw_send_nodes(key, part):
    lists = jax.random.randint(jax.random.fold_in(key, 21), (N_DOM, NPEER, CAP), 0, NODE_DEV, dtype=jnp.int32)
    lists = lists.at[0, 0, 0].set(0)
    return lists.at[N_DOM - 1, NPEER - 1, CAP - 1].set(NODE_DEV - 1)


def draw_elem_nodes(key, part):
    peers = peer_table(key)
    pair_total = ELEM_DEV // 2
    edge_pairs = BND_DEV // 2
    window = NODE_DEV // pair_total
    live = NPEER * CAP

    def one_device(device_key, peer_row):
        slot_range = jnp.arange(CAP, dtype=jnp.int32)
        ghost_pool = (NODE_DEV + peer_row[:, None] * CAP + slot_range[None, :]).reshape(-1).astype(jnp.int32)
        runs = jnp.take(ghost_pool, jnp.arange(edge_pairs * GHOST_RUN, dtype=jnp.int32) % live).reshape(edge_pairs, GHOST_RUN)

        def edge_pair(pair_index, run):
            pair_key = jax.random.fold_in(device_key, pair_index)
            fill = jax.random.randint(jax.random.fold_in(pair_key, 1), (2 * NPE - GHOST_RUN - window,), 0, window, dtype=jnp.int32)
            own = pair_index * window + jnp.concatenate([jnp.arange(window, dtype=jnp.int32), fill])
            refs = jax.random.permutation(jax.random.fold_in(pair_key, 2), jnp.concatenate([own, run]))
            return refs.reshape(2, NPE).T

        def inner_pair(pair_index):
            pair_key = jax.random.fold_in(device_key, pair_index)
            fill = jax.random.randint(jax.random.fold_in(pair_key, 1), (2 * NPE - window,), 0, window, dtype=jnp.int32)
            own = pair_index * window + jnp.concatenate([jnp.arange(window, dtype=jnp.int32), fill])
            refs = jax.random.permutation(jax.random.fold_in(pair_key, 2), own)
            return refs.reshape(2, NPE).T
        edge_blocks = jax.vmap(edge_pair)(jnp.arange(edge_pairs, dtype=jnp.int32), runs)
        inner_blocks = jax.vmap(inner_pair)(jnp.arange(edge_pairs, pair_total, dtype=jnp.int32))
        all_pairs = jnp.concatenate([edge_blocks, inner_blocks], axis=0)
        return jnp.transpose(all_pairs, (1, 0, 2)).reshape(NPE, ELEM_DEV).astype(jnp.int32)
    device_keys = jax.random.split(jax.random.fold_in(key, 31), N_DOM)
    blocks = jax.vmap(one_device)(device_keys, peers)
    return jnp.transpose(blocks, (1, 0, 2)).reshape(NPE, N_DOM * ELEM_DEV).astype(jnp.int32)


def draw_right_side(key, part):
    node_ids = jnp.arange(NODES, dtype=jnp.int32)
    device_of = (node_ids // NODE_DEV).astype(jnp.float32)
    rising = jnp.exp(jnp.log(3.0) * device_of / (N_DOM - 1))
    values = jnp.clip(jax.random.normal(key, (NV, NODES), jnp.float32), -5.0, 5.0) * rising[None, :]
    return values


def with_ends(values, key, smallest, largest):
    spot = [jax.random.randint(jax.random.fold_in(key, axis), (), 0, length) for axis, length in enumerate(values.shape)]
    longest = values.shape.index(max(values.shape))
    beside = spot[:longest] + [(spot[longest] + 1) % values.shape[longest]] + spot[longest + 1:]
    return values.at[tuple(spot)].set(smallest).at[tuple(beside)].set(largest)


def steps_of(rng, extent, shards, least, high):
    factor_of = 1.0
    for dim, shards_of in shards:
        heights = jax.random.uniform(jax.random.fold_in(jax.random.fold_in(rng, 6), dim), (shards_of,), jnp.float32, least / len(shards), high / len(shards))
        factor_of = factor_of * jnp.repeat(jnp.exp(heights), extent[dim] // shards_of).reshape((-1,) + (1,) * (len(extent) - 1 - dim))
    return factor_of


def setup_inputs(seed: int = 0) -> dict:
    key_list = jax.random.split(jax.random.key(seed), 9)
    right_side = draw_right_side(jax.random.fold_in(key_list[8], 71), 0)
    stiffness = jnp.clip(jnp.exp(math.log(0.05) - 2.3025851 * jax.random.uniform(key_list[1], (3, NPE, ELEMS), jnp.float32) ** steps_of(key_list[1], (3, NPE, ELEMS), ((2, 32),), -0.2, 0.2)), 0.005, 0.05)
    mass = jnp.clip(jnp.exp(math.log(2.0) - 1.3862944 * jax.random.uniform(key_list[2], (NPE, ELEMS), jnp.float32) ** steps_of(key_list[2], (NPE, ELEMS), ((1, 32),), -0.2, 0.2)), 0.5, 2.0)
    region = with_ends(jax.random.randint(key_list[3], (ELEMS,), 0, 3), jax.random.fold_in(key_list[3], 1), 0, 2).astype(jnp.int32)
    density = jnp.clip(jnp.exp(jax.random.uniform(key_list[4], (3,), jnp.float32, math.log(0.5), math.log(2.0))), 0.5, 2.0)
    elem_nodes = draw_elem_nodes(jax.random.fold_in(key_list[8], 71), 0)
    peer_rank = draw_peer_rank(jax.random.fold_in(key_list[8], 71), 0)
    send_nodes = draw_send_nodes(jax.random.fold_in(key_list[8], 71), 0)
    return {"right_side": right_side, "stiffness": stiffness, "mass": mass, "region": region, "density": density, "elem_nodes": elem_nodes, "peer_rank": peer_rank, "send_nodes": send_nodes}


precise = lax.Precision.HIGHEST

def gll_matrix():
    points = np.array([-1.0, -np.sqrt(3.0 / 7.0), 0.0, np.sqrt(3.0 / 7.0), 1.0])
    weights = np.array([1.0 / np.prod([points[column] - points[other] for other in range(5) if other != column]) for column in range(5)])
    matrix = np.zeros((5, 5))
    for row_index in range(5):
        for column in range(5):
            if row_index != column:
                matrix[row_index, column] = weights[column] / weights[row_index] / (points[row_index] - points[column])
        matrix[row_index, row_index] = -np.sum(matrix[row_index])
    return matrix

def element_apply(gathered, stiff_grid, mass_grid, derivative):
    grad_first = jnp.einsum('ai,vijke->vajke', derivative, gathered, precision=precise)
    result = jnp.einsum('ai,vajke->vijke', derivative, stiff_grid[0] * grad_first, precision=precise)
    grad_second = jnp.einsum('bj,vijke->vibke', derivative, gathered, precision=precise)
    result = result + jnp.einsum('bj,vibke->vijke', derivative, stiff_grid[1] * grad_second, precision=precise)
    grad_third = jnp.einsum('ck,vijke->vijce', derivative, gathered, precision=precise)
    result = result + jnp.einsum('ck,vijce->vijke', derivative, stiff_grid[2] * grad_third, precision=precise)
    return result + mass_grid * gathered

def element_diagonal(stiff_grid, mass_grid, derivative):
    square = derivative * derivative
    first = jnp.einsum('ai,ajke->ijke', square, stiff_grid[0], precision=precise)
    second = jnp.einsum('bj,ibke->ijke', square, stiff_grid[1], precision=precise)
    third = jnp.einsum('ck,ijce->ijke', square, stiff_grid[2], precision=precise)
    return first + second + third + mass_grid

def reference(right_side, stiffness, mass, region, density, elem_nodes, peer_rank, send_nodes):
    derivative = jnp.asarray(gll_matrix(), jnp.float32)
    sources = jnp.broadcast_to(jnp.arange(N_DOM, dtype=jnp.int32)[:, None], peer_rank.shape)
    offsets = (jnp.arange(N_DOM, dtype=jnp.int32)[:, None, None] * NODE_DEV + send_nodes).astype(jnp.int32)
    table = jnp.zeros((N_DOM, N_DOM, CAP), jnp.int32).at[peer_rank, sources].set(offsets)
    table = table.reshape(N_DOM, N_DOM * CAP)
    blocks = elem_nodes.reshape(NPE, N_DOM, ELEM_DEV).transpose(1, 0, 2)

    def globalize(device, block_list, table_row):
        own_global = device * NODE_DEV + block_list
        remote = jnp.take(table_row, jnp.clip(block_list - NODE_DEV, 0, N_DOM * CAP - 1))
        return jnp.where(block_list < NODE_DEV, own_global, remote).astype(jnp.int32)
    global_nodes = jax.vmap(globalize)(jnp.arange(N_DOM, dtype=jnp.int32), blocks, table)
    mass_term = jnp.take(density, region)[None, :] * mass
    diag_terms = element_diagonal(stiffness.reshape(3, 5, 5, 5, ELEMS), mass_term.reshape(5, 5, 5, ELEMS), derivative)
    diag_terms = diag_terms.reshape(NPE, N_DOM, ELEM_DEV).transpose(1, 0, 2)
    diagonal = jnp.zeros((NODES,), jnp.float32).at[global_nodes.reshape(-1)].add(diag_terms.reshape(-1))

    def operator(vector_field):

        def one_block(device, summed):
            node_list = lax.dynamic_index_in_dim(global_nodes, device, 0, keepdims=False).reshape(-1)
            start = (device * ELEM_DEV).astype(jnp.int32)
            stiff_grid = lax.dynamic_slice_in_dim(stiffness, start, ELEM_DEV, 2).reshape(3, 5, 5, 5, ELEM_DEV)
            mass_block = lax.dynamic_slice_in_dim(mass_term, start, ELEM_DEV, 1).reshape(5, 5, 5, ELEM_DEV)
            gathered = jnp.take(vector_field, node_list, axis=1).reshape(NV, 5, 5, 5, ELEM_DEV)
            result = element_apply(gathered, stiff_grid, mass_block, derivative)
            return summed.at[:, node_list].add(result.reshape(NV, -1))
        return lax.fori_loop(0, N_DOM, one_block, jnp.zeros_like(vector_field))
    solution = jnp.zeros_like(right_side)
    residual = right_side
    precond = residual / diagonal[None, :]
    direction = precond
    product_now = lax.optimization_barrier(jnp.sum(residual * precond, axis=1))
    for iteration in range(ITERS):
        applied = operator(direction)
        step_size = product_now / lax.optimization_barrier(jnp.sum(direction * applied, axis=1))
        solution = solution + step_size[:, None] * direction
        residual = residual - step_size[:, None] * applied
        precond = residual / diagonal[None, :]
        product_next = lax.optimization_barrier(jnp.sum(residual * precond, axis=1))
        direction = precond + (product_next / product_now)[:, None] * direction
        product_now = product_next
    return (solution, residual)
```

```python
import functools

import jax
import jax.numpy as jnp
import numpy as np
from jax import lax
from jax.experimental import pallas as pl
from jax.experimental.pallas import tpu as pltpu
from jax.sharding import PartitionSpec as P

ITERS = 2
LANES = 128
ROWS = 8
NONE = 255
SIDE = 5
NPE = SIDE**3


def gll_matrix():
    points = np.array([-1.0, -np.sqrt(3.0 / 7.0), 0.0, np.sqrt(3.0 / 7.0), 1.0])
    weights = np.array(
        [
            1.0 / np.prod([points[column] - points[other] for other in range(5) if other != column])
            for column in range(5)
        ]
    )
    matrix = np.zeros((5, 5))
    for row_index in range(5):
        for column in range(5):
            if row_index != column:
                matrix[row_index, column] = (
                    weights[column] / weights[row_index] / (points[row_index] - points[column])
                )
        matrix[row_index, row_index] = -np.sum(matrix[row_index])
    return matrix


def direction_matrices():
    base = np.asarray(gll_matrix(), np.float32)
    eye = np.eye(SIDE, dtype=np.float32)
    return [
        np.einsum("ai,bj,ck->abcijk", *factors).reshape(NPE, NPE)
        for factors in ((base, eye, eye), (eye, base, eye), (eye, eye, base))
    ]


def split_np(values):
    high = values.astype(jnp.bfloat16)
    low = (values - high.astype(np.float32)).astype(jnp.bfloat16)
    return high, low


def constant_operands():
    mats = direction_matrices()
    grad = np.zeros((LANES, 3 * LANES), np.float32)
    for d in range(3):
        grad[:NPE, d * LANES : d * LANES + NPE] = mats[d].T
    high, low = split_np(grad)
    first = np.block([[high, low], [high, np.zeros_like(low)]])
    back_high, back_low = high.T, low.T
    second = np.block([[back_high, back_low], [back_high, back_low]])
    squares = np.stack([(m.T * m.T) for m in mats])
    return jnp.asarray(first), jnp.asarray(second), jnp.asarray(squares)


def take(values, index):
    numbers = lax.GatherDimensionNumbers(
        offset_dims=(),
        collapsed_slice_dims=(1,),
        start_index_map=(1,),
        operand_batching_dims=(0,),
        start_indices_batching_dims=(0,),
    )
    return lax.gather(
        values, index[..., None], numbers, (1, 1), mode=lax.GatherScatterMode.PROMISE_IN_BOUNDS
    )


def iota(shape, axis):
    return lax.broadcasted_iota(jnp.int32, shape, axis)


def spread(row, rows=ROWS):
    return jnp.broadcast_to(row, (rows, row.shape[-1]))


def codes_of(nodes, lane_offset, peer_ref, own_count, peer_count, window):
    pair = (iota(nodes.shape, 1) + lane_offset) >> 1
    own = nodes - pair * window
    ref = nodes - own_count
    sender = ref // LANES
    slot = jnp.zeros_like(ref)
    for p in range(1, peer_count):
        slot = jnp.where(sender == peer_ref[0, p], p, slot)
    return jnp.where(ref >= 0, window + slot * LANES + (ref & (LANES - 1)), own)


def vmem():
    return pl.BlockSpec(memory_space=pltpu.VMEM)


def smem():
    return pl.BlockSpec(memory_space=pltpu.SMEM)


def call(body, name, in_specs, outs, out_specs=None, scratch=()):
    return pl.pallas_call(
        body,
        name=name,
        in_specs=in_specs,
        out_specs=tuple(out_specs or [vmem()] * len(outs)),
        out_shape=tuple(jax.ShapeDtypeStruct(shape, dtype) for shape, dtype in outs),
        scratch_shapes=list(scratch),
    )


def ghost_diag_body(cfg, peer, density, nodes, stiff, mass, region, squares, send, diag, mass_out, pos):
    run = cfg["run"]
    tag = region[...]
    dens = jnp.where(tag == 0, density[0], jnp.where(tag == 1, density[1], density[2]))
    term = mass[...] * dens
    mass_out[...] = term
    total = term
    for d in range(3):
        total = total + jnp.dot(
            squares[d], stiff[d], precision=lax.Precision.HIGHEST, preferred_element_type=jnp.float32
        )
    diag[...] = total
    edge = total[:, :LANES]
    code = codes_of(nodes[:, :LANES], 0, peer, cfg["own"], cfg["peers"], cfg["window"])
    lane = iota(code.shape, 1)
    base = code - (cfg["window"] + run * (lane >> 1))
    place = iota(code.shape, 0) + LANES * (lane & 1)
    flat = iota((ROWS, LANES), 0) * LANES + iota((ROWS, LANES), 1)
    pair = (flat * cfg["magic"]) >> 16
    hop = flat - pair * run
    pair_lane = jnp.minimum(2 * pair, LANES - 1)
    got = jnp.zeros((ROWS, LANES), jnp.float32)
    where_at = jnp.zeros((ROWS, LANES), jnp.int32)
    for h in range(run):
        hit = base == h
        position = jnp.sum(jnp.where(hit, place, 0), axis=0, keepdims=True)
        value = jnp.sum(jnp.where(hit, edge, 0.0), axis=0, keepdims=True)
        position, value = spread(position), spread(value)
        position = position + pltpu.roll(position, LANES - 1, 1)
        value = value + pltpu.roll(value, LANES - 1, 1)
        got = jnp.where(hop == h, take(value, pair_lane), got)
        where_at = jnp.where(hop == h, take(position, pair_lane), where_at)
    pos[...] = where_at
    send[...] = jnp.zeros(send.shape, jnp.float32)
    for p in range(cfg["peers"]):
        send[peer[0, p]] = got[p : p + 1]


def tables_body(
    cfg, peer, nodes, stiff, diag, mass, idx, st, mt, first, next0, next1, own_diag, trips,
    code_pad, value_pad, order, links,
):
    lane = iota((LANES, LANES), 1)
    row_id = iota((LANES, LANES), 0)
    code_pad[...] = jnp.full(code_pad.shape, 4096, jnp.int32)
    value_pad[...] = jnp.zeros(value_pad.shape, jnp.float32)
    links[...] = jnp.full(links.shape, NONE, jnp.int32)
    for b in range(2):
        cols = slice(b * LANES, (b + 1) * LANES)
        code_pad[:NPE, cols] = codes_of(
            nodes[:, cols], b * LANES, peer, cfg["own"], cfg["peers"], cfg["window"]
        )
        idx[cols, :] = jnp.where(lane < NPE, code_pad[:, cols].T, 0)

    def deal(ref, parity):
        source = (2 * lane + parity) & (LANES - 1)
        return jnp.where(
            lane < LANES // 2, take(ref[:, :LANES], source), take(ref[:, LANES:], source)
        )

    order[:LANES] = deal(code_pad, 0)
    order[LANES:] = deal(code_pad, 1)
    heads = jnp.full((LANES, LANES), NONE, jnp.int32)
    for parity in (1, 0):

        def link(step, heads, parity=parity):
            at = parity * LANES + NPE - 1 - step
            hit = row_id == order[pl.ds(at, 1), :]
            links[pl.ds(at, 1), :] = jnp.sum(jnp.where(hit, heads, 0), axis=0, keepdims=True)
            return jnp.where(hit, at, heads)

        heads = lax.fori_loop(0, NPE, link, heads)
    first[...] = heads.T
    next0[...] = links[:LANES].T
    next1[...] = links[LANES:].T
    for d in range(3):
        value_pad[:NPE] = stiff[d]
        for b in range(2):
            cols = slice(b * LANES, (b + 1) * LANES)
            st[cols, d * LANES : (d + 1) * LANES] = value_pad[:, cols].T
    value_pad[:NPE] = mass[...]
    for b in range(2):
        cols = slice(b * LANES, (b + 1) * LANES)
        mt[cols, :] = value_pad[:, cols].T
    value_pad[:NPE] = diag[...]
    even = deal(value_pad, 0).T
    odd = deal(value_pad, 1).T
    n0, n1 = next0[...], next1[...]

    def more(carry):
        return carry[3] > 0

    def walk(carry):
        pos, total, count, _ = carry
        low = pos & (LANES - 1)
        near = pos < LANES
        total = total + jnp.where(near, take(even, low), take(odd, low))
        pos = jnp.where(near, take(n0, low), take(n1, low))
        return pos, total, count + 1, (jnp.min(pos) < NONE).astype(jnp.int32)

    _, total, count, _ = lax.while_loop(
        more, walk, (first[...], jnp.zeros((LANES, LANES), jnp.float32), jnp.int32(0), jnp.int32(1))
    )
    own_diag[...] = total
    trips[0, 0] = count


def pick(cfg, field, peer, send_s, send_v, out):
    lane = iota((ROWS, LANES), 1)
    for p in range(cfg["peers"]):
        low = spread(send_v[0, p : p + 1, :] & (LANES - 1))

        def body(c, got, p=p, low=low):
            base = pl.multiple_of((send_s[0, p, c] >> 7) * LANES, LANES)
            return jnp.where(lane == c, take(field[:, pl.ds(base, LANES)], low), got)

        got = lax.fori_loop(0, LANES, body, jnp.zeros((ROWS, LANES), jnp.float32), unroll=16)
        out[peer[0, p]] = got


def start_body(cfg, peer, send_s, send_v, recv, own_diag, right, inverse, z, out, energy):
    peers, windows = cfg["peers"], cfg["pairs"]
    total = own_diag[...]
    for p in range(peers):
        node = send_v[0, p : p + 1, :]
        value = recv[peer[0, p]]
        left = jnp.where(iota((windows, LANES), 0) == (node >> 7), spread(value, windows), 0.0)
        hot = (iota((LANES, LANES), 0) == (node & (LANES - 1))).astype(jnp.float32)
        total = total + lax.dot_general(
            left, hot, (((1,), (1,)), ((), ())), precision=lax.Precision.HIGHEST,
            preferred_element_type=jnp.float32,
        )
    inverse[...] = 1.0 / total
    acc = jnp.zeros((ROWS, LANES), jnp.float32)
    for g in range(windows):
        cols = slice(g * LANES, (g + 1) * LANES)
        scaled = right[:, cols] * spread(inverse[g : g + 1, :])
        z[:, cols] = scaled
        acc = acc + right[:, cols] * scaled
    energy[...] = acc
    out[...] = jnp.zeros(out.shape, jnp.float32)
    pick(cfg, z, peer, send_s, send_v, out)


def apply_rows(values, st, mt, weights1, weights2):
    count = values.shape[0] // ROWS

    def halves(x):
        high = x.astype(jnp.bfloat16)
        return jnp.concatenate([high, (x - high.astype(jnp.float32)).astype(jnp.bfloat16)], axis=1)

    both = jnp.dot(halves(values), weights1[...], preferred_element_type=jnp.float32)
    wide = 3 * LANES
    grad = (both[:, :wide] + both[:, wide:]).reshape(count, ROWS, wide)
    flux = (grad * st[:, None, :]).reshape(count * ROWS, wide)
    both = jnp.dot(halves(flux), weights2[...], preferred_element_type=jnp.float32)
    lumped = (values.reshape(count, ROWS, LANES) * mt[:, None, :]).reshape(count * ROWS, LANES)
    return both[:, :LANES] + both[:, LANES:] + lumped


CHUNK = 64


def apply_half(values, result, st, mt, weights1, weights2, first_element):
    acc = jnp.zeros((ROWS, LANES), jnp.float32)
    for c in range(values.shape[0] // (ROWS * CHUNK)):
        rows = slice(c * CHUNK * ROWS, (c + 1) * CHUNK * ROWS)
        elems = slice(first_element + c * CHUNK, first_element + (c + 1) * CHUNK)
        v = values[rows]
        r = apply_rows(v, st[elems], mt[elems], weights1, weights2)
        result[rows] = r
        acc = acc + jnp.sum((v * r).reshape(CHUNK, ROWS, LANES), axis=0)
    return acc


def scatter_half(cfg, result, first, next0, next1, trips, out, first_pair, pair_count):
    for group in range(pair_count // ROWS):
        rows = slice(first_pair + group * ROWS, first_pair + (group + 1) * ROWS)
        n0, n1 = next0[rows], next1[rows]

        def walk(_, carry, group=group, n0=n0, n1=n1):
            pos, sums = carry
            low = pos & (LANES - 1)
            near = pos < LANES
            added = []
            for i in range(ROWS):
                e = 2 * (group * ROWS + i) * ROWS
                at = spread(low[i : i + 1])
                value = jnp.where(
                    spread(pos[i : i + 1]) < LANES,
                    take(result[e : e + ROWS], at),
                    take(result[e + ROWS : e + 2 * ROWS], at),
                )
                added.append(sums[i] + value)
            return jnp.where(near, take(n0, low), take(n1, low)), tuple(added)

        zero = jnp.zeros((ROWS, LANES), jnp.float32)
        _, sums = lax.fori_loop(0, trips[0, 0], walk, (first[rows], (zero,) * ROWS))
        for i in range(ROWS):
            cols = slice((group * ROWS + i) * LANES, (group * ROWS + i + 1) * LANES)
            out[:, cols] = sums[i]


def inner_body(cfg, trips, z, idx, st, mt, first, next0, next1, w1, w2, out, curve, values, result):
    edge, pairs = cfg["edge_pairs"], cfg["pairs"]
    for g in range(edge, pairs):
        window = z[:, g * LANES : (g + 1) * LANES]
        for parity in range(2):
            e = 2 * g + parity
            at = (e - 2 * edge) * ROWS
            values[at : at + ROWS] = take(window, spread(idx[e : e + 1, :]))
    curve[...] = apply_half(values, result, st, mt, w1, w2, 2 * edge)
    scatter_half(cfg, result, first, next0, next1, trips, out, edge, pairs - edge)


def edge_body(cfg, peer, recv, z, idx, st, mt, pos, w1, w2, energy, curve, result, out, values, ghosts):
    run, edge, peers = cfg["run"], cfg["edge_pairs"], cfg["peers"]
    for p in range(peers):
        ghosts[p] = recv[peer[0, p]]
    spans = []
    for g in range(edge):
        low, high = run * g // LANES, (run * (g + 1) - 1) // LANES
        spans.append((low, high))
        window = z[:, g * LANES : (g + 1) * LANES]
        for parity in range(2):
            e = 2 * g + parity
            code = spread(idx[e : e + 1, :])
            at = code & (LANES - 1)
            got = take(ghosts[low], at)
            if high > low:
                got = jnp.where(code < LANES * (high + 1), got, take(ghosts[high], at))
            values[e * ROWS : (e + 1) * ROWS] = jnp.where(code < LANES, take(window, at), got)
    acc = apply_half(values, result, st, mt, w1, w2, 0) + curve[...]
    lane = iota((ROWS, LANES), 1)
    sums = [jnp.zeros((ROWS, LANES), jnp.float32) for _ in range(peers)]
    for g in range(edge):
        for p in range(spans[g][0], spans[g][1] + 1):
            place = spread(pos[p : p + 1, :])
            at = place & (LANES - 1)
            e = 2 * g * ROWS
            value = jnp.where(
                place < LANES, take(result[e : e + ROWS], at), take(result[e + ROWS : e + 2 * ROWS], at)
            )
            begin, end = run * g - p * LANES, run * (g + 1) - p * LANES
            sums[p] = jnp.where((lane >= begin) & (lane < end), value, sums[p])
    parts = jnp.where(
        lane == 0,
        jnp.sum(energy[...], axis=1, keepdims=True),
        jnp.where(lane == 1, jnp.sum(acc, axis=1, keepdims=True), 0.0),
    )
    out[:, :ROWS, :] = jnp.zeros((out.shape[0], ROWS, LANES), jnp.float32)
    for n in range(out.shape[0]):
        out[n, ROWS:, :] = parts
    for p in range(peers):
        out[peer[0, p], :ROWS, :] = sums[p]


def edge_scatter_body(cfg, trips, result, first, next0, next1, out):
    scatter_half(cfg, result, first, next0, next1, trips, out, 0, cfg["edge_pairs"])


def returned_sums(cfg, peer, send_v, recv, left, hot):
    peers, windows = cfg["peers"], cfg["pairs"]
    wide = peers * LANES
    node = jnp.concatenate([send_v[0, p : p + 1, :] for p in range(peers)], axis=1)
    value = jnp.concatenate([recv[peer[0, p], :ROWS, :] for p in range(peers)], axis=1)
    high = value.astype(jnp.bfloat16).astype(jnp.float32)
    low = value - high
    lanes = (iota((LANES, wide), 0) == (node & (LANES - 1))).astype(jnp.bfloat16)
    hot[:, :wide] = lanes
    hot[:, wide:] = lanes
    block = spread(node >> 7)
    for g in range(0, windows, 2):
        rows = slice(g * ROWS, (g + 2) * ROWS)
        even, odd = block == g, block == g + 1
        left[rows, :wide] = jnp.concatenate(
            [jnp.where(even, high, 0.0), jnp.where(odd, high, 0.0)], axis=0
        ).astype(jnp.bfloat16)
        left[rows, wide:] = jnp.concatenate(
            [jnp.where(even, low, 0.0), jnp.where(odd, low, 0.0)], axis=0
        ).astype(jnp.bfloat16)
    return lax.dot_general(
        left[...], hot[...], (((1,), (1,)), ((), ())), preferred_element_type=jnp.float32
    )


def dot_totals(recv):
    total = recv[0, ROWS:, :]
    for n in range(1, recv.shape[0]):
        total = total + recv[n, ROWS:, :]
    lane = iota((ROWS, LANES), 1)
    return [
        jnp.broadcast_to(jnp.sum(jnp.where(lane == k, total, 0.0), axis=1, keepdims=True), (ROWS, LANES))
        for k in range(2)
    ]


def step_body(
    cfg, peer, send_s, send_v, recv, w_edge, w_inner, right, inverse,
    w, r1, z1, out, energy, coefs, left, hot, sums,
):
    windows, edge = cfg["pairs"], cfg["edge_pairs"]
    sums[...] = returned_sums(cfg, peer, send_v, recv, left, hot)
    energy_now, curve_now = dot_totals(recv)
    alpha = energy_now / curve_now
    coefs[0] = alpha
    coefs[1] = energy_now
    acc = jnp.zeros((ROWS, LANES), jnp.float32)
    for g in range(windows):
        cols = slice(g * LANES, (g + 1) * LANES)
        half = w_edge if g < edge else w_inner
        base = (g if g < edge else g - edge) * LANES
        image = half[:, base : base + LANES] + sums[g * ROWS : (g + 1) * ROWS]
        w[:, cols] = image
        left_over = right[:, cols] - alpha * image
        r1[:, cols] = left_over
        scaled = left_over * spread(inverse[g : g + 1, :])
        z1[:, cols] = scaled
        acc = acc + left_over * scaled
    energy[...] = acc
    out[...] = jnp.zeros(out.shape, jnp.float32)
    pick(cfg, z1, peer, send_s, send_v, out)


def last_body(
    cfg, peer, send_v, recv, y_edge, y_inner, w, r1, z1, z0, coefs, solution, residual, left, hot, sums
):
    windows, edge = cfg["pairs"], cfg["edge_pairs"]
    sums[...] = returned_sums(cfg, peer, send_v, recv, left, hot)
    energy_next, curve_next = dot_totals(recv)
    alpha, energy_now = coefs[0], coefs[1]
    beta = energy_next / energy_now
    step = energy_next / (curve_next - beta * energy_next / alpha)
    for g in range(windows):
        cols = slice(g * LANES, (g + 1) * LANES)
        half = y_edge if g < edge else y_inner
        base = (g if g < edge else g - edge) * LANES
        image = half[:, base : base + LANES] + sums[g * ROWS : (g + 1) * ROWS]
        residual[:, cols] = r1[:, cols] - step * (image + beta * w[:, cols])
        solution[:, cols] = alpha * z0[:, cols] + step * (z1[:, cols] + beta * z0[:, cols])


def on_device(right_side, stiffness, mass, region, density, elem_nodes, peer_rank, send_nodes):
    vectors, own_count = right_side.shape
    elem_count = elem_nodes.shape[1]
    pairs = elem_count // 2
    edge_pairs = pairs // 2
    peers, slots = send_nodes.shape[1], send_nodes.shape[2]
    devices = lax.axis_size("dom")
    run = peers * slots // edge_pairs
    magic = (1 << 16) // run + 1
    flat = np.arange(ROWS * LANES)
    if (
        vectors != ROWS or own_count != pairs * LANES or slots != LANES or pairs != LANES
        or peers * slots != run * edge_pairs or peers > ROWS or run > LANES
        or ((flat * magic) >> 16 != flat // run).any()
    ):
        raise ValueError("unsupported sizes")
    cfg = dict(
        own=own_count, pairs=pairs, edge_pairs=edge_pairs, peers=peers, run=run, magic=magic,
        window=own_count // pairs,
    )
    f32, i32 = jnp.float32, jnp.int32
    weights1, weights2, squares = constant_operands()
    V, S = vmem(), smem()
    field = ((vectors, own_count), f32)
    half_field = ((vectors, own_count // 2), f32)
    tile = ((ROWS, LANES), f32)
    square = ((LANES, LANES), f32)
    square_i = ((LANES, LANES), i32)
    half_rows = ((elem_count // 2 * ROWS, LANES), f32)

    def bind(body):
        return functools.partial(body, cfg)

    def exchange(values):
        return lax.all_to_all(values, "dom", split_axis=0, concat_axis=0, tiled=True)

    send, diag, mass_term, pos = call(
        bind(ghost_diag_body), "ghost_diag", [S, S, V, V, V, V, V],
        [((devices, 1, LANES), f32), ((NPE, elem_count), f32), ((NPE, elem_count), f32), ((ROWS, LANES), i32)],
    )(peer_rank, density, elem_nodes, stiffness, mass, region.reshape(1, elem_count), squares)
    recv = exchange(send)
    idx, st, mt, first, next0, next1, own_diag, trips = call(
        bind(tables_body), "tables", [S, V, V, V, V],
        [
            ((elem_count, LANES), i32), ((elem_count, 3 * LANES), f32), ((elem_count, LANES), f32),
            square_i, square_i, square_i, square, ((1, 1), i32),
        ],
        [V] * 7 + [S],
        [
            pltpu.VMEM((LANES, elem_count), i32), pltpu.VMEM((LANES, elem_count), f32),
            pltpu.VMEM((elem_count, LANES), i32), pltpu.VMEM((elem_count, LANES), i32),
        ],
    )(peer_rank, elem_nodes, stiffness, diag, mass_term)

    inverse, z0, send, energy = call(
        bind(start_body), "start", [S, S, V, V, V, V],
        [square, field, ((devices, ROWS, LANES), f32), tile],
    )(peer_rank, send_nodes, send_nodes, recv, own_diag, right_side)

    def operator(z, send, energy):
        recv = exchange(send)
        inner, curve = call(
            bind(inner_body), "inner", [S] + [V] * 9, [half_field, tile],
            scratch=[pltpu.VMEM(*half_rows), pltpu.VMEM(*half_rows)],
        )(trips, z, idx, st, mt, first, next0, next1, weights1, weights2)
        result, send = call(
            bind(edge_body), "edge", [S] + [V] * 10, [half_rows, ((devices, 2 * ROWS, LANES), f32)],
            scratch=[pltpu.VMEM(*half_rows), pltpu.VMEM((peers, ROWS, LANES), f32)],
        )(peer_rank, recv, z, idx, st, mt, pos, weights1, weights2, energy, curve)
        recv = exchange(send)
        (edge,) = call(bind(edge_scatter_body), "edge_scatter", [S] + [V] * 4, [half_field])(
            trips, result, first, next0, next1
        )
        return recv, edge, inner

    wide = 2 * peers * LANES
    scratch = [
        pltpu.VMEM((vectors * pairs, wide), jnp.bfloat16), pltpu.VMEM((LANES, wide), jnp.bfloat16),
        pltpu.VMEM((vectors * pairs, LANES), f32),
    ]
    recv, w_edge, w_inner = operator(z0, send, energy)
    w, r1, z1, send, energy, coefs = call(
        bind(step_body), "step", [S, S] + [V] * 6,
        [field, field, field, ((devices, ROWS, LANES), f32), tile, ((2, ROWS, LANES), f32)],
        scratch=scratch,
    )(peer_rank, send_nodes, send_nodes, recv, w_edge, w_inner, right_side, inverse)
    recv, y_edge, y_inner = operator(z1, send, energy)
    return call(bind(last_body), "last", [S] + [V] * 9, [field, field], scratch=scratch)(
        peer_rank, send_nodes, recv, y_edge, y_inner, w, r1, z1, z0, coefs
    )


def solution(mesh):
    placed = (
        P(None, "dom"),
        P(None, None, "dom"),
        P(None, "dom"),
        P("dom"),
        P(),
        P(None, "dom"),
        P("dom", None),
        P("dom", None, None),
    )
    return jax.shard_map(
        on_device,
        mesh=mesh,
        in_specs=placed,
        out_specs=(P(None, "dom"), P(None, "dom")),
        check_vma=False,
    )
```

```python
import functools

import jax
import jax.numpy as jnp
import numpy as np
from jax import lax
from jax.experimental import pallas as pl
from jax.experimental.pallas import tpu as pltpu
from jax.sharding import PartitionSpec as P

ITERS = 2
LANES = 128
ROWS = 8
NONE = 255
SIDE = 5
NPE = SIDE**3


def gll_matrix():
    points = np.array([-1.0, -np.sqrt(3.0 / 7.0), 0.0, np.sqrt(3.0 / 7.0), 1.0])
    weights = np.array(
        [
            1.0 / np.prod([points[column] - points[other] for other in range(5) if other != column])
            for column in range(5)
        ]
    )
    matrix = np.zeros((5, 5))
    for row_index in range(5):
        for column in range(5):
            if row_index != column:
                matrix[row_index, column] = (
                    weights[column] / weights[row_index] / (points[row_index] - points[column])
                )
        matrix[row_index, row_index] = -np.sum(matrix[row_index])
    return matrix


def direction_matrices():
    base = np.asarray(gll_matrix(), np.float32)
    eye = np.eye(SIDE, dtype=np.float32)
    return [
        np.einsum("ai,bj,ck->abcijk", *factors).reshape(NPE, NPE)
        for factors in ((base, eye, eye), (eye, base, eye), (eye, eye, base))
    ]


def split_np(values):
    high = values.astype(jnp.bfloat16)
    low = (values - high.astype(np.float32)).astype(jnp.bfloat16)
    return high, low


def constant_operands():
    mats = direction_matrices()
    grad = np.zeros((LANES, 3 * LANES), np.float32)
    for d in range(3):
        grad[:NPE, d * LANES : d * LANES + NPE] = mats[d].T
    high, low = split_np(grad)
    first = np.block([[high, low], [high, np.zeros_like(low)]])
    back_high, back_low = high.T, low.T
    second = np.block([[back_high, back_low], [back_high, back_low]])
    squares = np.stack(split_np(np.stack([m.T * m.T for m in mats])))
    return jnp.asarray(first), jnp.asarray(second), jnp.asarray(squares)


def take(values, index):
    numbers = lax.GatherDimensionNumbers(
        offset_dims=(),
        collapsed_slice_dims=(1,),
        start_index_map=(1,),
        operand_batching_dims=(0,),
        start_indices_batching_dims=(0,),
    )
    return lax.gather(
        values, index[..., None], numbers, (1, 1), mode=lax.GatherScatterMode.PROMISE_IN_BOUNDS
    )


def iota(shape, axis):
    return lax.broadcasted_iota(jnp.int32, shape, axis)


def spread(row, rows=ROWS):
    return jnp.broadcast_to(row, (rows, row.shape[-1]))


def codes_of(nodes, lane_offset, peer_ref, own_count, peer_count, window):
    pair = (iota(nodes.shape, 1) + lane_offset) >> 1
    own = nodes - pair * window
    ref = nodes - own_count
    sender = ref // LANES
    slot = jnp.zeros_like(ref)
    for p in range(1, peer_count):
        slot = jnp.where(sender == peer_ref[0, p], p, slot)
    return jnp.where(ref >= 0, window + slot * LANES + (ref & (LANES - 1)), own)


def vmem():
    return pl.BlockSpec(memory_space=pltpu.VMEM)


def smem():
    return pl.BlockSpec(memory_space=pltpu.SMEM)


def hbm():
    return pl.BlockSpec(memory_space=pltpu.HBM)


def call(body, name, in_specs, outs, stay, scratch=(), resident=(), grid=()):
    kernel = pl.pallas_call(
        body,
        name=name,
        grid=grid,
        in_specs=in_specs,
        out_specs=tuple(vmem() for _ in outs),
        out_shape=tuple(
            pltpu.VMEM(shape, dtype) if k in stay else jax.ShapeDtypeStruct(shape, dtype)
            for k, (shape, dtype) in enumerate(outs)
        ),
        scratch_shapes=list(scratch),
        compiler_params=pltpu.CompilerParams(vmem_limit_bytes=24 << 20),
    )

    def run(*operands):
        return kernel(
            *[
                pltpu.with_memory_space_constraint(operand, pltpu.VMEM if k in resident else pltpu.HBM)
                for k, operand in enumerate(operands)
            ]
        )

    return run


def element_sums(mass, region, density, stiff, squares):
    dens = jnp.where(region == 0, density[0], jnp.where(region == 1, density[1], density[2]))
    term = mass * dens
    total = term
    for d in range(3):
        high = stiff[d].astype(jnp.bfloat16)
        low = (stiff[d] - high.astype(jnp.float32)).astype(jnp.bfloat16)
        for weight, part in ((squares[0, d], high), (squares[0, d], low), (squares[1, d], high)):
            total = total + jnp.dot(weight, part, preferred_element_type=jnp.float32)
    return term, total


def ghost_diag_body(cfg, peer, density, nodes, stiff, mass, region, squares, send, pos):
    run = cfg["run"]
    _, edge = element_sums(mass[...], region[...], density, stiff, squares)
    code = codes_of(nodes[...], 0, peer, cfg["own"], cfg["peers"], cfg["window"])
    lane = iota(code.shape, 1)
    base = code - (cfg["window"] + run * (lane >> 1))
    place = iota(code.shape, 0) + LANES * (lane & 1)
    flat = iota((ROWS, LANES), 0) * LANES + iota((ROWS, LANES), 1)
    pair = (flat * cfg["magic"]) >> 16
    hop = flat - pair * run
    pair_lane = jnp.minimum(2 * pair, LANES - 1)
    got = jnp.zeros((ROWS, LANES), jnp.float32)
    where_at = jnp.zeros((ROWS, LANES), jnp.int32)
    for h in range(run):
        hit = base == h
        position = jnp.sum(jnp.where(hit, place, 0), axis=0, keepdims=True)
        value = jnp.sum(jnp.where(hit, edge, 0.0), axis=0, keepdims=True)
        position, value = spread(position), spread(value)
        position = position + pltpu.roll(position, LANES - 1, 1)
        value = value + pltpu.roll(value, LANES - 1, 1)
        got = jnp.where(hop == h, take(value, pair_lane), got)
        where_at = jnp.where(hop == h, take(position, pair_lane), where_at)
    pos[...] = where_at
    send[...] = jnp.zeros(send.shape, jnp.float32)
    for p in range(cfg["peers"]):
        send[peer[0, p]] = got[p : p + 1]


def tables_body(
    cfg, peer, density, nodes, stiff, mass, region, squares, send_s, send_v, right,
    idx, st_edge, mt_edge, st_inner, mt_inner, own_diag, right_at, diag_at, same,
    code_pad, value_pad, rows,
):
    code_pad[...] = jnp.full(code_pad.shape, NONE, jnp.int32)
    value_pad[...] = jnp.zeros(value_pad.shape, jnp.float32)

    def turned(ref):
        return jnp.concatenate([ref[:, :LANES].T, ref[:, LANES:].T], axis=0)

    for b in range(2):
        cols = slice(b * LANES, (b + 1) * LANES)
        code_pad[:NPE, cols] = codes_of(
            nodes[:, cols], b * LANES, peer, cfg["own"], cfg["peers"], cfg["window"]
        )
    idx[...] = turned(code_pad)
    term, diag = element_sums(mass[...], region[...], density, stiff, squares)
    value_pad[:NPE] = diag
    rows[...] = turned(value_pad)
    for g in range(cfg["pairs"]):
        row = jnp.concatenate([rows[2 * g : 2 * g + 1, :], rows[2 * g + 1 : 2 * g + 2, :]], axis=1)
        own_diag[g : g + 1, :] = scatter_rows(spread(row), idx, g)[:1]
    for d in range(3):
        value_pad[:NPE] = stiff[d]
        cols = slice(d * LANES, (d + 1) * LANES)
        st_edge[:, cols] = value_pad[:, :LANES].T
        st_inner[:, cols] = value_pad[:, LANES:].T
    value_pad[:NPE] = term
    mt_edge[...] = value_pad[:, :LANES].T
    mt_inner[...] = value_pad[:, LANES:].T
    pick(cfg, right, send_s, send_v, right_at)
    node = slot_nodes(cfg, send_v)
    wide = node.shape[1]
    hot = jnp.where(iota((LANES, wide), 0) == (node & (LANES - 1)), 1.0, 0.0).astype(jnp.bfloat16)
    here = iota((LANES, wide), 0) == (node >> 7)
    at_slots = jnp.zeros((1, wide), jnp.float32)
    for part in reversed(parts_of(own_diag[...], 3)):
        seen = jnp.dot(part.astype(jnp.bfloat16), hot, preferred_element_type=jnp.float32)
        at_slots = at_slots + jnp.sum(jnp.where(here, seen, 0.0), axis=0, keepdims=True)
    diag_at[...] = spread(at_slots)
    for p in range(cfg["peers"]):
        column = jnp.broadcast_to(send_v[p], (LANES, LANES)).T
        for q in range(cfg["peers"]):
            same[p * LANES : (p + 1) * LANES, q * LANES : (q + 1) * LANES] = jnp.where(
                column == send_v[q], 1.0, 0.0
            ).astype(jnp.bfloat16)


def scatter_rows(rows, idx, g):
    node = iota((LANES, LANES), 0)
    spots = jnp.concatenate(
        [jnp.where(node == idx[2 * g + k : 2 * g + k + 1, :], 1.0, 0.0) for k in range(2)], axis=1
    ).astype(jnp.bfloat16)
    high = rows.astype(jnp.bfloat16).astype(jnp.float32)
    both = jnp.concatenate([high, rows - high], axis=0).astype(jnp.bfloat16)
    sums = lax.dot_general(both, spots, (((1,), (1,)), ((), ())), preferred_element_type=jnp.float32)
    return sums[:ROWS] + sums[ROWS:]


def pick(cfg, field, send_s, send_v, out):
    lane = iota((ROWS, LANES), 1)
    for p in range(cfg["peers"]):
        low = spread(send_v[p] & (LANES - 1))
        got = jnp.zeros((ROWS, LANES), jnp.float32)
        for c in range(LANES):
            base = pl.multiple_of((send_s[p, 0, c] >> 7) * LANES, LANES)
            got = jnp.where(lane == c, take(field[:, pl.ds(base, LANES)], low), got)
        out[:, p * LANES : (p + 1) * LANES] = got


def slot_nodes(cfg, send_v):
    return jnp.concatenate([send_v[p] for p in range(cfg["peers"])], axis=1)


def nt_dot(left, right):
    return lax.dot_general(left, right, (((1,), (1,)), ((), ())), preferred_element_type=jnp.float32)


def parts_of(values, count):
    parts = []
    for _ in range(count):
        part = values.astype(jnp.bfloat16).astype(jnp.float32)
        parts.append(part)
        values = values - part
    return parts


def received_diag(cfg, peer, recv):
    return jnp.concatenate([recv[peer[0, p]] for p in range(cfg["peers"])], axis=1)


def received_rows(cfg, peer, recv):
    blocks = []
    for p in range(cfg["peers"]):
        first = peer[0, p] * (ROWS + 1)
        blocks.append(jnp.concatenate([recv[first + v] for v in range(ROWS)], axis=0))
    return jnp.concatenate(blocks, axis=1)


def put_slots(cfg, peer, values, out):
    for p in range(cfg["peers"]):
        out[peer[0, p]] = values[:, p * LANES : (p + 1) * LANES]


def start_body(cfg, peer, recv, right_at, diag_at, same, out, inverse_at):
    got = spread(received_diag(cfg, peer, recv))
    top, middle, bottom = parts_of(got, 3)
    both = jnp.concatenate([top, middle], axis=0).astype(jnp.bfloat16)
    more = jnp.concatenate([bottom, bottom], axis=0).astype(jnp.bfloat16)
    first = nt_dot(both, same[...])
    total = diag_at[...] + (first[:ROWS] + (first[ROWS:] + nt_dot(more, same[...])[:ROWS]))
    inverse = 1.0 / total
    inverse_at[...] = inverse
    out[...] = jnp.zeros(out.shape, jnp.float32)
    put_slots(cfg, peer, right_at[...] * inverse, out)


def first_fields_body(cfg, peer, send_v, recv, own_diag, right_hbm, inverse, z, energy, right, arrived):
    fetch = pltpu.make_async_copy(right_hbm, right, arrived)
    fetch.start()
    windows = cfg["pairs"]
    node, got = slot_nodes(cfg, send_v), received_diag(cfg, peer, recv)
    here = iota((windows, got.shape[1]), 0) == (node >> 7)
    hot = jnp.where(iota((LANES, got.shape[1]), 0) == (node & (LANES - 1)), 1.0, 0.0).astype(jnp.bfloat16)
    total = own_diag[...]
    for part in parts_of(got, 3):
        total = total + nt_dot(jnp.where(here, spread(part, windows), 0.0).astype(jnp.bfloat16), hot)
    inverse[...] = 1.0 / total
    fetch.wait()
    acc = jnp.zeros((ROWS, LANES), jnp.float32)
    for g in range(windows):
        cols = slice(g * LANES, (g + 1) * LANES)
        scaled = right[:, cols] * spread(inverse[g : g + 1, :])
        z[:, cols] = scaled
        acc = acc + right[:, cols] * scaled
    energy[...] = acc


def apply_rows(values, st, mt, weights1, weights2):
    count = values.shape[0] // ROWS

    def halves(x):
        high = x.astype(jnp.bfloat16)
        return jnp.concatenate([high, (x - high.astype(jnp.float32)).astype(jnp.bfloat16)], axis=1)

    both = jnp.dot(halves(values), weights1[...], preferred_element_type=jnp.float32)
    wide = 3 * LANES
    grad = (both[:, :wide] + both[:, wide:]).reshape(count, ROWS, wide)
    flux = (grad * st[:, None, :]).reshape(count * ROWS, wide)
    both = jnp.dot(halves(flux), weights2[...], preferred_element_type=jnp.float32)
    lumped = (values.reshape(count, ROWS, LANES) * mt[:, None, :]).reshape(count * ROWS, LANES)
    return both[:, :LANES] + both[:, LANES:] + lumped


CHUNK = 64


def apply_half(values, result, st, mt, weights1, weights2):
    acc = jnp.zeros((ROWS, LANES), jnp.float32)
    for c in range(values.shape[0] // (ROWS * CHUNK)):
        rows = slice(c * CHUNK * ROWS, (c + 1) * CHUNK * ROWS)
        elems = slice(c * CHUNK, (c + 1) * CHUNK)
        v = values[rows]
        r = apply_rows(v, st[elems], mt[elems], weights1, weights2)
        result[rows] = r
        acc = acc + jnp.sum((v * r).reshape(CHUNK, ROWS, LANES), axis=0)
    return acc


def scatter_half(result, idx, out, first_pair, pair_count):
    for g in range(pair_count):
        e = 2 * g * ROWS
        rows = jnp.concatenate([result[e : e + ROWS], result[e + ROWS : e + 2 * ROWS]], axis=1)
        out[:, g * LANES : (g + 1) * LANES] = scatter_rows(rows, idx, first_pair + g)


def inner_body(cfg, z, idx, st, mt, w1, w2, out, curve, values, result):
    edge, pairs = cfg["edge_pairs"], cfg["pairs"]
    for g in range(edge, pairs):
        window = z[:, g * LANES : (g + 1) * LANES]
        for parity in range(2):
            e = 2 * g + parity
            at = (e - 2 * edge) * ROWS
            values[at : at + ROWS] = take(window, spread(idx[e : e + 1, :] & (LANES - 1)))
    curve[...] = apply_half(values, result, st, mt, w1, w2)
    scatter_half(result, idx, out, edge, pairs - edge)


def edge_body(cfg, peer, recv, z, idx, st, mt, pos, w1, w2, energy, curve, result, out, values, ghosts):
    run, edge, peers = cfg["run"], cfg["edge_pairs"], cfg["peers"]
    for p in range(peers):
        ghosts[p] = recv[peer[0, p]]
    spans = []
    for g in range(edge):
        low, high = run * g // LANES, (run * (g + 1) - 1) // LANES
        spans.append((low, high))
        window = z[:, g * LANES : (g + 1) * LANES]
        for parity in range(2):
            e = 2 * g + parity
            code = spread(idx[e : e + 1, :])
            at = code & (LANES - 1)
            got = take(ghosts[low], at)
            if high > low:
                got = jnp.where(code < LANES * (high + 1), got, take(ghosts[high], at))
            values[e * ROWS : (e + 1) * ROWS] = jnp.where(code < LANES, take(window, at), got)
    acc = apply_half(values, result, st, mt, w1, w2) + curve[...]
    lane = iota((ROWS, LANES), 1)
    sums = [jnp.zeros((ROWS, LANES), jnp.float32) for _ in range(peers)]
    for g in range(edge):
        for p in range(spans[g][0], spans[g][1] + 1):
            place = spread(pos[p : p + 1, :])
            at = place & (LANES - 1)
            e = 2 * g * ROWS
            value = jnp.where(
                place < LANES, take(result[e : e + ROWS], at), take(result[e + ROWS : e + 2 * ROWS], at)
            )
            begin, end = run * g - p * LANES, run * (g + 1) - p * LANES
            sums[p] = jnp.where((lane >= begin) & (lane < end), value, sums[p])
    row = iota((ROWS, LANES), 0)
    dots = jnp.where(lane == row, jnp.sum(energy[...], axis=1, keepdims=True), 0.0)
    dots = jnp.where(lane == row + ROWS, jnp.sum(acc, axis=1, keepdims=True), dots)
    dots = jnp.sum(dots, axis=0, keepdims=True)
    out[...] = jnp.zeros(out.shape, jnp.float32)
    for n in range(out.shape[0] // (ROWS + 1)):
        out[n * (ROWS + 1) + ROWS] = dots
    for p in range(peers):
        for v in range(ROWS):
            out[peer[0, p] * (ROWS + 1) + v] = sums[p][v : v + 1]


def edge_scatter_body(cfg, result, idx, inner, out):
    split = cfg["edge_pairs"] * LANES
    scatter_half(result, idx, out, 0, cfg["edge_pairs"])
    out[:, split:] = inner[...]


def edge_scatter_pick_body(cfg, send_s, send_v, result, idx, inner, out, at_slots):
    edge_scatter_body(cfg, result, idx, inner, out)
    pick(cfg, out, send_s, send_v, at_slots)


def returned_sums(cfg, peer, send_v, recv, left, hot):
    windows = cfg["pairs"]
    node, value = slot_nodes(cfg, send_v), received_rows(cfg, peer, recv)
    wide = node.shape[1]
    high, low = parts_of(value, 2)
    lanes = jnp.where(iota((LANES, wide), 0) == (node & (LANES - 1)), 1.0, 0.0).astype(jnp.bfloat16)
    hot[:, :wide] = lanes
    hot[:, wide:] = lanes
    block = spread(node >> 7)
    for g in range(0, windows, 2):
        rows = slice(g * ROWS, (g + 2) * ROWS)
        even, odd = block == g, block == g + 1
        left[rows, :wide] = jnp.concatenate(
            [jnp.where(even, high, 0.0), jnp.where(odd, high, 0.0)], axis=0
        ).astype(jnp.bfloat16)
        left[rows, wide:] = jnp.concatenate(
            [jnp.where(even, low, 0.0), jnp.where(odd, low, 0.0)], axis=0
        ).astype(jnp.bfloat16)
    return nt_dot(left[...], hot[...])


def dot_totals(recv):
    total = recv[ROWS]
    for n in range(1, recv.shape[0] // (ROWS + 1)):
        total = total + recv[n * (ROWS + 1) + ROWS]
    total = spread(total)
    lane, row = iota((ROWS, LANES), 1), iota((ROWS, LANES), 0)
    return [
        jnp.broadcast_to(
            jnp.sum(jnp.where(lane == row + k * ROWS, total, 0.0), axis=1, keepdims=True), (ROWS, LANES)
        )
        for k in range(2)
    ]


def step_body(cfg, peer, recv, right_at, inverse_at, image_at, same, out, coefs):
    energy_now, curve_now = dot_totals(recv)
    alpha = energy_now / curve_now
    coefs[0] = alpha
    coefs[1] = energy_now
    both = jnp.concatenate(parts_of(received_rows(cfg, peer, recv), 2), axis=0).astype(jnp.bfloat16)
    got = nt_dot(both, same[...])
    image = image_at[...] + (got[:ROWS] + got[ROWS:])
    left_over = right_at[...] - spread_lanes(alpha, image.shape[1]) * image
    out[...] = jnp.zeros(out.shape, jnp.float32)
    put_slots(cfg, peer, left_over * inverse_at[...], out)


def spread_lanes(tile, wide):
    return jnp.concatenate([tile] * (wide // LANES), axis=1)


def next_fields_body(
    cfg, peer, send_v, recv, own, right_hbm, inverse, coefs, w, z1, energy, left, hot, sums, right, arrived
):
    fetch = pltpu.make_async_copy(right_hbm, right, arrived)
    fetch.start()
    windows = cfg["pairs"]
    sums[...] = returned_sums(cfg, peer, send_v, recv, left, hot)
    alpha = coefs[0]
    fetch.wait()
    acc = jnp.zeros((ROWS, LANES), jnp.float32)
    for g in range(windows):
        cols = slice(g * LANES, (g + 1) * LANES)
        image = own[:, cols] + sums[g * ROWS : (g + 1) * ROWS]
        w[:, cols] = image
        left_over = right[:, cols] - alpha * image
        scaled = left_over * spread(inverse[g : g + 1, :])
        z1[:, cols] = scaled
        acc = acc + left_over * scaled
    energy[...] = acc


def last_body(
    cfg, peer, send_v, recv, own, right_hbm, inverse, w, z1, coefs,
    solution, residual, left, hot, sums, right, arrived,
):
    fetch = pltpu.make_async_copy(right_hbm, right, arrived)
    fetch.start()
    windows = cfg["pairs"]
    sums[...] = returned_sums(cfg, peer, send_v, recv, left, hot)
    energy_next, curve_next = dot_totals(recv)
    alpha, energy_now = coefs[0], coefs[1]
    beta = energy_next / energy_now
    step = energy_next / (curve_next - beta * energy_next / alpha)
    fetch.wait()
    for g in range(windows):
        cols = slice(g * LANES, (g + 1) * LANES)
        image = own[:, cols] + sums[g * ROWS : (g + 1) * ROWS]
        start, before = right[:, cols], w[:, cols]
        z0 = start * spread(inverse[g : g + 1, :])
        residual[:, cols] = (start - alpha * before) - step * (image + beta * before)
        solution[:, cols] = alpha * z0 + step * (z1[:, cols] + beta * z0)


def on_device(right_side, stiffness, mass, region, density, elem_nodes, peer_rank, send_nodes):
    vectors, own_count = right_side.shape
    elem_count = elem_nodes.shape[1]
    pairs = elem_count // 2
    edge_pairs = pairs // 2
    peers, slots = send_nodes.shape[1], send_nodes.shape[2]
    devices = lax.axis_size("dom")
    run = peers * slots // edge_pairs
    magic = (1 << 16) // run + 1
    flat = np.arange(ROWS * LANES)
    if (
        vectors != ROWS or own_count != pairs * LANES or slots != LANES or pairs != LANES
        or peers * slots != run * edge_pairs or peers > ROWS or run > LANES
        or ((flat * magic) >> 16 != flat // run).any()
    ):
        raise ValueError("unsupported sizes")
    cfg = dict(
        own=own_count, pairs=pairs, edge_pairs=edge_pairs, peers=peers, run=run, magic=magic,
        window=own_count // pairs,
    )
    f32, i32 = jnp.float32, jnp.int32
    weights1, weights2, squares = constant_operands()
    V, S = vmem(), smem()
    field = ((vectors, own_count), f32)
    half_field = ((vectors, own_count // 2), f32)
    tile = ((ROWS, LANES), f32)
    square = ((LANES, LANES), f32)
    half_rows = ((elem_count // 2 * ROWS, LANES), f32)

    def bind(body):
        return functools.partial(body, cfg)

    def exchange(values):
        return lax.all_to_all(values, "dom", split_axis=0, concat_axis=0, tiled=True)

    regions = region.reshape(1, elem_count)
    half_specs = [
        pl.BlockSpec((NPE, LANES), lambda _: (0, 0)),
        pl.BlockSpec((3, NPE, LANES), lambda _: (0, 0, 0)),
        pl.BlockSpec((NPE, LANES), lambda _: (0, 0)),
        pl.BlockSpec((1, LANES), lambda _: (0, 0)),
    ]
    send, pos = call(
        bind(ghost_diag_body), "ghost_diag", [S, S, *half_specs, V],
        [((devices, 1, LANES), f32), ((ROWS, LANES), i32)], (1,), grid=(1,),
    )(peer_rank, density, elem_nodes, stiffness, mass, regions, squares)
    recv = exchange(send)
    shared = jnp.transpose(send_nodes, (1, 0, 2))
    slots_all = ((vectors, peers * slots), f32)
    edge_count = elem_count // 2
    idx, st_edge, mt_edge, st_inner, mt_inner, own_diag, right_at, diag_at, same = call(
        bind(tables_body), "tables", [S, S] + [V] * 5 + [S, V, V],
        [
            ((elem_count, LANES), i32),
            ((edge_count, 3 * LANES), f32), ((edge_count, LANES), f32),
            ((elem_count - edge_count, 3 * LANES), f32), ((elem_count - edge_count, LANES), f32),
            square, slots_all, slots_all, ((peers * slots, peers * slots), jnp.bfloat16),
        ],
        (0, 1, 2, 5, 6, 7, 8),
        [
            pltpu.VMEM((LANES, elem_count), i32), pltpu.VMEM((LANES, elem_count), f32),
            pltpu.VMEM((elem_count, LANES), f32),
        ],
    )(peer_rank, density, elem_nodes, stiffness, mass, regions, squares, shared, shared, right_side)

    send_shape = ((devices, ROWS, LANES), f32)
    copied = [pltpu.VMEM(*field), pltpu.SemaphoreType.DMA(())]
    send, inverse_at = call(
        bind(start_body), "start", [S] + [V] * 4, [send_shape, slots_all], (1,), (), (1, 2, 3, 4)
    )(peer_rank, recv, right_at, diag_at, same)
    diag_recv = recv
    recv = exchange(send)
    inverse, z, energy = call(
        bind(first_fields_body), "first_fields", [S, V, V, V, hbm()], [square, field, tile], range(3),
        copied, (2, 3),
    )(peer_rank, shared, diag_recv, own_diag, right_side)

    def inner_part(z):
        return call(
            bind(inner_body), "inner", [V] * 6, [half_field, tile], range(2),
            [pltpu.VMEM(*half_rows), pltpu.VMEM(*half_rows)], (0, 1, 4, 5),
        )(z, idx, st_inner, mt_inner, weights1, weights2)

    def edge_part(recv, z, energy, curve):
        return call(
            bind(edge_body), "edge", [S] + [V] * 10,
            [half_rows, ((devices * (ROWS + 1), 1, LANES), f32)], (0,),
            [pltpu.VMEM(*half_rows), pltpu.VMEM((peers, ROWS, LANES), f32)], range(1, 11),
        )(peer_rank, recv, z, idx, st_edge, mt_edge, pos, weights1, weights2, energy, curve)

    wide = 2 * peers * slots
    scratch = [
        pltpu.VMEM((vectors * pairs, wide), jnp.bfloat16), pltpu.VMEM((LANES, wide), jnp.bfloat16),
        pltpu.VMEM((vectors * pairs, LANES), f32), *copied,
    ]
    inner, curve = inner_part(z)
    result, send = edge_part(recv, z, energy, curve)
    recv = exchange(send)
    own, image_at = call(
        bind(edge_scatter_pick_body), "edge_scatter_pick", [S] + [V] * 4, [field, slots_all], range(2), (),
        (2, 3, 4),
    )(shared, shared, result, idx, inner)
    send, coefs = call(
        bind(step_body), "step", [S] + [V] * 5, [send_shape, ((2, ROWS, LANES), f32)], (1,), (),
        range(1, 6),
    )(peer_rank, recv, right_at, inverse_at, image_at, same)
    sum_recv = recv
    recv = exchange(send)
    w, z, energy = call(
        bind(next_fields_body), "next_fields", [S] + [V] * 3 + [hbm()] + [V] * 2, [field, field, tile],
        range(3), scratch, (2, 3, 5, 6),
    )(peer_rank, shared, sum_recv, own, right_side, inverse, coefs)
    inner, curve = inner_part(z)
    result, send = edge_part(recv, z, energy, curve)
    recv = exchange(send)
    (own,) = call(bind(edge_scatter_body), "edge_scatter", [V] * 3, [field], (0,), (), range(3))(
        result, idx, inner
    )
    return call(
        bind(last_body), "last", [S] + [V] * 3 + [hbm()] + [V] * 4, [field, field], (), scratch,
        (2, 3, 5, 6, 7, 8),
    )(peer_rank, shared, recv, own, right_side, inverse, w, z, coefs)


def solution(mesh):
    placed = (
        P(None, "dom"),
        P(None, None, "dom"),
        P(None, "dom"),
        P("dom"),
        P(),
        P(None, "dom"),
        P("dom", None),
        P("dom", None, None),
    )
    return jax.shard_map(
        on_device,
        mesh=mesh,
        in_specs=placed,
        out_specs=(P(None, "dom"), P(None, "dom")),
        check_vma=False,
    )
```

```python
import functools

import jax
import jax.numpy as jnp
import numpy as np
from jax import lax
from jax.experimental import pallas as pl
from jax.experimental.pallas import tpu as pltpu
from jax.sharding import PartitionSpec as P

ITERS = 2
LANES = 128
ROWS = 8
NONE = 255
SIDE = 5
NPE = SIDE**3


def gll_matrix():
    points = np.array([-1.0, -np.sqrt(3.0 / 7.0), 0.0, np.sqrt(3.0 / 7.0), 1.0])
    weights = np.array(
        [
            1.0 / np.prod([points[column] - points[other] for other in range(5) if other != column])
            for column in range(5)
        ]
    )
    matrix = np.zeros((5, 5))
    for row_index in range(5):
        for column in range(5):
            if row_index != column:
                matrix[row_index, column] = (
                    weights[column] / weights[row_index] / (points[row_index] - points[column])
                )
        matrix[row_index, row_index] = -np.sum(matrix[row_index])
    return matrix


def direction_matrices():
    base = np.asarray(gll_matrix(), np.float32)
    eye = np.eye(SIDE, dtype=np.float32)
    return [
        np.einsum("ai,bj,ck->abcijk", *factors).reshape(NPE, NPE)
        for factors in ((base, eye, eye), (eye, base, eye), (eye, eye, base))
    ]


def split_np(values):
    high = values.astype(jnp.bfloat16)
    low = (values - high.astype(np.float32)).astype(jnp.bfloat16)
    return high, low


def constant_operands():
    mats = direction_matrices()
    grad = np.zeros((LANES, 3 * LANES), np.float32)
    for d in range(3):
        grad[:NPE, d * LANES : d * LANES + NPE] = mats[d].T
    high, low = split_np(grad)
    first = np.concatenate([high, low], axis=1)
    second = np.concatenate([high.T, low.T], axis=1)
    squares = np.stack(split_np(np.stack([m.T * m.T for m in mats])))
    return jnp.asarray(first), jnp.asarray(second), jnp.asarray(squares)


def take(values, index):
    numbers = lax.GatherDimensionNumbers(
        offset_dims=(),
        collapsed_slice_dims=(1,),
        start_index_map=(1,),
        operand_batching_dims=(0,),
        start_indices_batching_dims=(0,),
    )
    return lax.gather(
        values, index[..., None], numbers, (1, 1), mode=lax.GatherScatterMode.PROMISE_IN_BOUNDS
    )


def iota(shape, axis):
    return lax.broadcasted_iota(jnp.int32, shape, axis)


def spread(row, rows=ROWS):
    return jnp.broadcast_to(row, (rows, row.shape[-1]))


def codes_of(nodes, lane_offset, peer_ref, own_count, peer_count, window):
    pair = (iota(nodes.shape, 1) + lane_offset) >> 1
    own = nodes - pair * window
    ref = nodes - own_count
    sender = ref // LANES
    slot = jnp.zeros_like(ref)
    for p in range(1, peer_count):
        slot = jnp.where(sender == peer_ref[0, p], p, slot)
    return jnp.where(ref >= 0, window + slot * LANES + (ref & (LANES - 1)), own)


def vmem():
    return pl.BlockSpec(memory_space=pltpu.VMEM)


def smem():
    return pl.BlockSpec(memory_space=pltpu.SMEM)


def hbm():
    return pl.BlockSpec(memory_space=pltpu.HBM)


def call(body, name, in_specs, outs, stay, scratch=(), resident=(), grid=(), out_specs=None):
    kernel = pl.pallas_call(
        body,
        name=name,
        grid=grid,
        in_specs=in_specs,
        out_specs=out_specs or tuple(vmem() for _ in outs),
        out_shape=tuple(
            (pltpu.VMEM if k in stay else pltpu.HBM)(shape, dtype)
            for k, (shape, dtype) in enumerate(outs)
        ),
        scratch_shapes=list(scratch),
        compiler_params=pltpu.CompilerParams(vmem_limit_bytes=24 << 20),
    )

    def run(*operands):
        return kernel(
            *[
                pltpu.with_memory_space_constraint(operand, pltpu.VMEM if k in resident else pltpu.HBM)
                for k, operand in enumerate(operands)
            ]
        )

    return run


def element_sums(mass, region, density, stiff, squares):
    dens = jnp.where(region == 0, density[0], jnp.where(region == 1, density[1], density[2]))
    term = mass * dens
    total = term
    for d in range(3):
        high = stiff[d].astype(jnp.bfloat16)
        low = (stiff[d] - high.astype(jnp.float32)).astype(jnp.bfloat16)
        for weight, part in ((squares[0, d], high), (squares[0, d], low), (squares[1, d], high)):
            total = total + jnp.dot(weight, part, preferred_element_type=jnp.float32)
    return term, total


def ghost_diag_body(
    cfg, peer, density, nodes, stiff, mass, region, squares, shared, send, pos, peer_row, base, node_row
):
    lanes = iota((1, LANES), 1)
    row = jnp.zeros((1, LANES), jnp.int32)
    for p in range(cfg["peers"]):
        row = jnp.where(lanes == p, peer[0, p], row)
        base[p] = shared[p] & (-LANES)
        node_row[:, p * LANES : (p + 1) * LANES] = shared[p]
    peer_row[...] = row
    run = cfg["run"]
    _, edge = element_sums(mass[...], region[...], density, stiff, squares)
    code = codes_of(nodes[...], 0, peer, cfg["own"], cfg["peers"], cfg["window"])
    lane = iota(code.shape, 1)
    base = code - (cfg["window"] + run * (lane >> 1))
    place = iota(code.shape, 0) + LANES * (lane & 1)
    flat = iota((ROWS, LANES), 0) * LANES + iota((ROWS, LANES), 1)
    pair = (flat * cfg["magic"]) >> 16
    hop = flat - pair * run
    pair_lane = jnp.minimum(2 * pair, LANES - 1)
    got = jnp.zeros((ROWS, LANES), jnp.float32)
    where_at = jnp.zeros((ROWS, LANES), jnp.int32)
    for h in range(run):
        hit = base == h
        position = jnp.sum(jnp.where(hit, place, 0), axis=0, keepdims=True)
        value = jnp.sum(jnp.where(hit, edge, 0.0), axis=0, keepdims=True)
        position, value = spread(position), spread(value)
        position = position + pltpu.roll(position, LANES - 1, 1)
        value = value + pltpu.roll(value, LANES - 1, 1)
        got = jnp.where(hop == h, take(value, pair_lane), got)
        where_at = jnp.where(hop == h, take(position, pair_lane), where_at)
    pos[...] = where_at
    send[...] = jnp.zeros(send.shape, jnp.float32)
    for p in range(cfg["peers"]):
        send[peer[0, p]] = got[p : p + 1]


def tables_body(
    cfg, peer, density, nodes, stiff, mass, region, squares, base_s, node_row, right,
    idx, st_edge, mt_edge, st_inner, mt_inner, own_diag, right_at, diag_at, same,
    code_pad, value_pad, rows,
):
    code_pad[...] = jnp.full(code_pad.shape, NONE, jnp.int32)
    value_pad[...] = jnp.zeros(value_pad.shape, jnp.float32)

    def turned(ref):
        return jnp.concatenate([ref[:, :LANES].T, ref[:, LANES:].T], axis=0)

    for b in range(2):
        cols = slice(b * LANES, (b + 1) * LANES)
        code_pad[:NPE, cols] = codes_of(
            nodes[:, cols], b * LANES, peer, cfg["own"], cfg["peers"], cfg["window"]
        )
    idx[...] = turned(code_pad)
    term, diag = element_sums(mass[...], region[...], density, stiff, squares)
    value_pad[:NPE] = diag
    rows[...] = turned(value_pad)
    for g in range(cfg["pairs"]):
        row = jnp.concatenate([rows[2 * g : 2 * g + 1, :], rows[2 * g + 1 : 2 * g + 2, :]], axis=1)
        own_diag[g : g + 1, :] = scatter_rows(spread(row), idx, g)[:1]
    for d in range(3):
        value_pad[:NPE] = stiff[d]
        cols = slice(d * LANES, (d + 1) * LANES)
        st_edge[:, cols] = value_pad[:, :LANES].T
        st_inner[:, cols] = value_pad[:, LANES:].T
    value_pad[:NPE] = term
    mt_edge[...] = value_pad[:, :LANES].T
    mt_inner[...] = value_pad[:, LANES:].T
    pick(cfg, right, base_s, node_row, right_at)
    node = node_row[...]
    wide = node.shape[1]
    hot = jnp.where(iota((LANES, wide), 0) == (node & (LANES - 1)), 1.0, 0.0).astype(jnp.bfloat16)
    here = iota((LANES, wide), 0) == (node >> 7)
    at_slots = jnp.zeros((1, wide), jnp.float32)
    for part in reversed(parts_of(own_diag[...], 3)):
        seen = jnp.dot(part.astype(jnp.bfloat16), hot, preferred_element_type=jnp.float32)
        at_slots = at_slots + jnp.sum(jnp.where(here, seen, 0.0), axis=0, keepdims=True)
    diag_at[...] = spread(at_slots)
    for p in range(cfg["peers"]):
        column = jnp.broadcast_to(node[:, p * LANES : (p + 1) * LANES], (LANES, LANES)).T
        for q in range(cfg["peers"]):
            same[p * LANES : (p + 1) * LANES, q * LANES : (q + 1) * LANES] = jnp.where(
                column == node[:, q * LANES : (q + 1) * LANES], 1.0, 0.0
            ).astype(jnp.bfloat16)


def scatter_rows(rows, idx, g):
    node = iota((LANES, LANES), 0)
    spots = jnp.concatenate(
        [jnp.where(node == idx[2 * g + k : 2 * g + k + 1, :], 1.0, 0.0) for k in range(2)], axis=1
    ).astype(jnp.bfloat16)
    high = rows.astype(jnp.bfloat16).astype(jnp.float32)
    both = jnp.concatenate([high, rows - high], axis=0).astype(jnp.bfloat16)
    sums = lax.dot_general(both, spots, (((1,), (1,)), ((), ())), preferred_element_type=jnp.float32)
    return sums[:ROWS] + sums[ROWS:]


def peers_of(cfg, peer_row):
    lane = iota((1, LANES), 1)
    return [jnp.max(jnp.where(lane == p, peer_row[...], 0)) for p in range(cfg["peers"])]


def pick(cfg, field, base_s, node_row, out):
    lane = iota((ROWS, LANES), 1)
    for p in range(cfg["peers"]):
        low = spread(node_row[:, p * LANES : (p + 1) * LANES] & (LANES - 1))
        got = jnp.zeros((ROWS, LANES), jnp.float32)
        for c in range(LANES):
            base = pl.multiple_of(base_s[p, 0, c], LANES)
            got = jnp.where(lane == c, take(field[:, pl.ds(base, LANES)], low), got)
        out[:, p * LANES : (p + 1) * LANES] = got


def nt_dot(left, right):
    return lax.dot_general(left, right, (((1,), (1,)), ((), ())), preferred_element_type=jnp.float32)


def parts_of(values, count):
    parts = []
    for _ in range(count):
        part = values.astype(jnp.bfloat16).astype(jnp.float32)
        parts.append(part)
        values = values - part
    return parts


def received_diag(cfg, peer, recv):
    return jnp.concatenate([recv[peer[p]] for p in range(cfg["peers"])], axis=1)


def received_rows(cfg, peer, recv):
    blocks = []
    for p in range(cfg["peers"]):
        first = peer[p] * (ROWS + 1)
        blocks.append(jnp.concatenate([recv[first + v] for v in range(ROWS)], axis=0))
    return jnp.concatenate(blocks, axis=1)


def put_slots(cfg, peer, values, out):
    for p in range(cfg["peers"]):
        out[peer[p]] = values[:, p * LANES : (p + 1) * LANES]


def start_body(cfg, peer_row, recv, right_at, diag_at, same, out, inverse_at):
    peer = peers_of(cfg, peer_row)
    got = spread(received_diag(cfg, peer, recv))
    top, middle, bottom = parts_of(got, 3)
    both = jnp.concatenate([top, middle], axis=0).astype(jnp.bfloat16)
    more = jnp.concatenate([bottom, bottom], axis=0).astype(jnp.bfloat16)
    first = nt_dot(both, same[...])
    total = diag_at[...] + (first[:ROWS] + (first[ROWS:] + nt_dot(more, same[...])[:ROWS]))
    inverse = 1.0 / total
    inverse_at[...] = inverse
    out[...] = jnp.zeros(out.shape, jnp.float32)
    put_slots(cfg, peer, right_at[...] * inverse, out)


def first_fields_body(cfg, peer_row, node_row, recv, own_diag, right, inverse, z, energy):
    peer = peers_of(cfg, peer_row)
    windows = cfg["pairs"]
    node, got = node_row[...], received_diag(cfg, peer, recv)
    here = iota((windows, got.shape[1]), 0) == (node >> 7)
    hot = jnp.where(iota((LANES, got.shape[1]), 0) == (node & (LANES - 1)), 1.0, 0.0).astype(jnp.bfloat16)
    total = own_diag[...]
    for part in parts_of(got, 3):
        total = total + nt_dot(jnp.where(here, spread(part, windows), 0.0).astype(jnp.bfloat16), hot)
    inverse[...] = 1.0 / total
    acc = jnp.zeros((ROWS, LANES), jnp.float32)
    for g in range(windows):
        cols = slice(g * LANES, (g + 1) * LANES)
        scaled = right[:, cols] * spread(inverse[g : g + 1, :])
        z[:, cols] = scaled
        acc = acc + right[:, cols] * scaled
    energy[...] = acc


def apply_rows(values, st, mt, weights1, weights2):
    count = values.shape[0] // ROWS

    def halves(x):
        high = x.astype(jnp.bfloat16)
        return jnp.concatenate([high, (x - high.astype(jnp.float32)).astype(jnp.bfloat16)], axis=1)

    both = jnp.dot(halves(values), weights1[...], preferred_element_type=jnp.float32)
    wide = 3 * LANES
    grad = (both[:, :wide] + both[:, wide:]).reshape(count, ROWS, wide)
    flux = (grad * st[:, None, :]).reshape(count * ROWS, wide)
    both = jnp.dot(halves(flux), weights2[...], preferred_element_type=jnp.float32)
    lumped = (values.reshape(count, ROWS, LANES) * mt[:, None, :]).reshape(count * ROWS, LANES)
    return both[:, :LANES] + both[:, LANES:] + lumped


def fill_weights(weights1, weights2, both1, both2):
    wide = 3 * LANES
    both1[:LANES] = weights1[...]
    both1[LANES:, :wide] = weights1[:, :wide]
    both1[LANES:, wide:] = jnp.zeros((LANES, wide), jnp.bfloat16)
    both2[:wide] = weights2[...]
    both2[wide:] = weights2[...]


CHUNK = 64


def apply_half(values, result, st, mt, weights1, weights2):
    acc = jnp.zeros((ROWS, LANES), jnp.float32)
    for c in range(values.shape[0] // (ROWS * CHUNK)):
        rows = slice(c * CHUNK * ROWS, (c + 1) * CHUNK * ROWS)
        elems = slice(c * CHUNK, (c + 1) * CHUNK)
        v = values[rows]
        r = apply_rows(v, st[elems], mt[elems], weights1, weights2)
        result[rows] = r
        acc = acc + jnp.sum((v * r).reshape(CHUNK, ROWS, LANES), axis=0)
    return acc


def scatter_half(edge, inner, idx, out):
    count = edge.shape[0] // (2 * ROWS)
    for g in range(idx.shape[0] // 2):
        half, e = (edge, 2 * g * ROWS) if g < count else (inner, 2 * (g - count) * ROWS)
        rows = jnp.concatenate([half[e : e + ROWS], half[e + ROWS : e + 2 * ROWS]], axis=1)
        out[:, g * LANES : (g + 1) * LANES] = scatter_rows(rows, idx, g)


def inner_body(cfg, z, idx, st, mt, w1, w2, result, curve, values, both1, both2):
    fill_weights(w1, w2, both1, both2)
    edge, pairs = cfg["edge_pairs"], cfg["pairs"]
    for g in range(edge, pairs):
        window = z[:, g * LANES : (g + 1) * LANES]
        for parity in range(2):
            e = 2 * g + parity
            at = (e - 2 * edge) * ROWS
            values[at : at + ROWS] = take(window, spread(idx[e : e + 1, :] & (LANES - 1)))
    curve[...] = apply_half(values, result, st, mt, both1, both2)


def edge_body(
    cfg, peer_row, recv, z, idx, st, mt, pos, w1, w2, energy, curve, result, out, values, ghosts, both1, both2
):
    peer = peers_of(cfg, peer_row)
    fill_weights(w1, w2, both1, both2)
    run, edge, peers = cfg["run"], cfg["edge_pairs"], cfg["peers"]
    for p in range(peers):
        ghosts[p] = recv[peer[p]]
    spans = []
    for g in range(edge):
        low, high = run * g // LANES, (run * (g + 1) - 1) // LANES
        spans.append((low, high))
        window = z[:, g * LANES : (g + 1) * LANES]
        for parity in range(2):
            e = 2 * g + parity
            code = spread(idx[e : e + 1, :])
            at = code & (LANES - 1)
            got = take(ghosts[low], at)
            if high > low:
                got = jnp.where(code < LANES * (high + 1), got, take(ghosts[high], at))
            values[e * ROWS : (e + 1) * ROWS] = jnp.where(code < LANES, take(window, at), got)
    acc = apply_half(values, result, st, mt, both1, both2) + curve[...]
    lane = iota((ROWS, LANES), 1)
    sums = [jnp.zeros((ROWS, LANES), jnp.float32) for _ in range(peers)]
    for g in range(edge):
        for p in range(spans[g][0], spans[g][1] + 1):
            place = spread(pos[p : p + 1, :])
            at = place & (LANES - 1)
            e = 2 * g * ROWS
            value = jnp.where(
                place < LANES, take(result[e : e + ROWS], at), take(result[e + ROWS : e + 2 * ROWS], at)
            )
            begin, end = run * g - p * LANES, run * (g + 1) - p * LANES
            sums[p] = jnp.where((lane >= begin) & (lane < end), value, sums[p])
    row = iota((ROWS, LANES), 0)
    dots = jnp.where(lane == row, jnp.sum(energy[...], axis=1, keepdims=True), 0.0)
    dots = jnp.where(lane == row + ROWS, jnp.sum(acc, axis=1, keepdims=True), dots)
    dots = jnp.sum(dots, axis=0, keepdims=True)
    out[...] = jnp.zeros(out.shape, jnp.float32)
    for n in range(out.shape[0] // (ROWS + 1)):
        out[n * (ROWS + 1) + ROWS] = dots
    for p in range(peers):
        for v in range(ROWS):
            out[peer[p] * (ROWS + 1) + v] = sums[p][v : v + 1]


def edge_scatter_body(cfg, result, idx, inner, out):
    scatter_half(result, inner, idx, out)


def edge_scatter_pick_body(cfg, base_s, node_row, result, idx, inner, out, at_slots):
    edge_scatter_body(cfg, result, idx, inner, out)
    pick(cfg, out, base_s, node_row, at_slots)


def returned_sums(cfg, peer, node_row, recv, left, hot):
    windows = cfg["pairs"]
    node, value = node_row[...], received_rows(cfg, peer, recv)
    wide = node.shape[1]
    high, low = parts_of(value, 2)
    lanes = jnp.where(iota((LANES, wide), 0) == (node & (LANES - 1)), 1.0, 0.0).astype(jnp.bfloat16)
    hot[:, :wide] = lanes
    hot[:, wide:] = lanes
    block = spread(node >> 7)
    for g in range(0, windows, 2):
        rows = slice(g * ROWS, (g + 2) * ROWS)
        even, odd = block == g, block == g + 1
        left[rows, :wide] = jnp.concatenate(
            [jnp.where(even, high, 0.0), jnp.where(odd, high, 0.0)], axis=0
        ).astype(jnp.bfloat16)
        left[rows, wide:] = jnp.concatenate(
            [jnp.where(even, low, 0.0), jnp.where(odd, low, 0.0)], axis=0
        ).astype(jnp.bfloat16)
    return nt_dot(left[...], hot[...])


def dot_totals(recv):
    total = recv[ROWS]
    for n in range(1, recv.shape[0] // (ROWS + 1)):
        total = total + recv[n * (ROWS + 1) + ROWS]
    total = spread(total)
    lane, row = iota((ROWS, LANES), 1), iota((ROWS, LANES), 0)
    return [
        jnp.broadcast_to(
            jnp.sum(jnp.where(lane == row + k * ROWS, total, 0.0), axis=1, keepdims=True), (ROWS, LANES)
        )
        for k in range(2)
    ]


def step_body(cfg, peer_row, recv, right_at, inverse_at, image_at, same, out, coefs):
    peer = peers_of(cfg, peer_row)
    energy_now, curve_now = dot_totals(recv)
    alpha = energy_now / curve_now
    coefs[0] = alpha
    coefs[1] = energy_now
    both = jnp.concatenate(parts_of(received_rows(cfg, peer, recv), 2), axis=0).astype(jnp.bfloat16)
    got = nt_dot(both, same[...])
    image = image_at[...] + (got[:ROWS] + got[ROWS:])
    left_over = right_at[...] - spread_lanes(alpha, image.shape[1]) * image
    out[...] = jnp.zeros(out.shape, jnp.float32)
    put_slots(cfg, peer, left_over * inverse_at[...], out)


def spread_lanes(tile, wide):
    return jnp.concatenate([tile] * (wide // LANES), axis=1)


def next_fields_body(
    cfg, peer_row, node_row, recv, own_hbm, right_hbm, inverse, coefs, w, z1, energy, left, hot, sums, right, own, arrived
):
    fetches = [
        pltpu.make_async_copy(there, here, arrived.at[k]) for k, (there, here) in enumerate(((right_hbm, right), (own_hbm, own)))
    ]
    for fetch in fetches:
        fetch.start()
    peer = peers_of(cfg, peer_row)
    windows = cfg["pairs"]
    sums[...] = returned_sums(cfg, peer, node_row, recv, left, hot)
    alpha = coefs[0]
    for fetch in fetches:
        fetch.wait()
    acc = jnp.zeros((ROWS, LANES), jnp.float32)
    for g in range(windows):
        cols = slice(g * LANES, (g + 1) * LANES)
        image = own[:, cols] + sums[g * ROWS : (g + 1) * ROWS]
        w[:, cols] = image
        left_over = right[:, cols] - alpha * image
        scaled = left_over * spread(inverse[g : g + 1, :])
        z1[:, cols] = scaled
        acc = acc + left_over * scaled
    energy[...] = acc


LAST_STEP = 32


def last_body(
    cfg, peer_row, node_row, recv, own, right_hbm, inverse, w_hbm, z1, coefs,
    solution_hbm, residual_hbm, left, hot, sums, right, w, arrived, solution, residual, sent,
):
    fetches = [
        pltpu.make_async_copy(there, here, arrived.at[k]) for k, (there, here) in enumerate(((right_hbm, right), (w_hbm, w)))
    ]
    for fetch in fetches:
        fetch.start()
    peer = peers_of(cfg, peer_row)
    windows = cfg["pairs"]
    sums[...] = returned_sums(cfg, peer, node_row, recv, left, hot)
    energy_next, curve_next = dot_totals(recv)
    alpha, energy_now = coefs[0], coefs[1]
    beta = energy_next / energy_now
    step = energy_next / (curve_next - beta * energy_next / alpha)
    copies = []
    for fetch in fetches:
        fetch.wait()
    for g in range(windows):
        cols = slice(g * LANES, (g + 1) * LANES)
        image = own[:, cols] + sums[g * ROWS : (g + 1) * ROWS]
        start, before = right[:, cols], w[:, cols]
        z0 = start * spread(inverse[g : g + 1, :])
        residual[:, cols] = (start - alpha * before) - step * (image + beta * before)
        solution[:, cols] = alpha * z0 + step * (z1[:, cols] + beta * z0)
        if (g + 1) % LAST_STEP == 0:
            done = slice((g + 1 - LAST_STEP) * LANES, (g + 1) * LANES)
            for k, (here, there) in enumerate(((solution, solution_hbm), (residual, residual_hbm))):
                copies.append(
                    pltpu.make_async_copy(here.at[:, done], there.at[:, done], sent.at[g // LAST_STEP, k])
                )
                copies[-1].start()
    for copy in copies:
        copy.wait()


def on_device(right_side, stiffness, mass, region, density, elem_nodes, peer_rank, send_nodes):
    vectors, own_count = right_side.shape
    elem_count = elem_nodes.shape[1]
    pairs = elem_count // 2
    edge_pairs = pairs // 2
    peers, slots = send_nodes.shape[1], send_nodes.shape[2]
    devices = lax.axis_size("dom")
    run = peers * slots // edge_pairs
    magic = (1 << 16) // run + 1
    flat = np.arange(ROWS * LANES)
    if (
        vectors != ROWS or own_count != pairs * LANES or slots != LANES or pairs != LANES
        or peers * slots != run * edge_pairs or peers > ROWS or run > LANES
        or ((flat * magic) >> 16 != flat // run).any()
    ):
        raise ValueError("unsupported sizes")
    cfg = dict(
        own=own_count, pairs=pairs, edge_pairs=edge_pairs, peers=peers, run=run, magic=magic,
        window=own_count // pairs,
    )
    f32, i32 = jnp.float32, jnp.int32
    weights1, weights2, squares = constant_operands()
    V, S = vmem(), smem()
    field = ((vectors, own_count), f32)
    tile = ((ROWS, LANES), f32)
    square = ((LANES, LANES), f32)
    half_rows = ((elem_count // 2 * ROWS, LANES), f32)

    def bind(body):
        return functools.partial(body, cfg)

    def exchange(values):
        return lax.all_to_all(values, "dom", split_axis=0, concat_axis=0, tiled=True)

    regions = region.reshape(1, elem_count)
    half_specs = [
        pl.BlockSpec((NPE, LANES), lambda _: (0, 0)),
        pl.BlockSpec((3, NPE, LANES), lambda _: (0, 0, 0)),
        pl.BlockSpec((NPE, LANES), lambda _: (0, 0)),
        pl.BlockSpec((1, LANES), lambda _: (0, 0)),
    ]
    shared = jnp.transpose(send_nodes, (1, 0, 2))
    send, pos, peer_row, base, node_row = call(
        bind(ghost_diag_body), "ghost_diag", [S, S, *half_specs, V, V],
        [
            ((devices, 1, LANES), f32), ((ROWS, LANES), i32), ((1, LANES), i32), ((peers, 1, slots), i32),
            ((1, peers * slots), i32),
        ],
        (1, 2, 4), grid=(1,),
    )(peer_rank, density, elem_nodes, stiffness, mass, regions, squares, shared)
    recv = exchange(send)
    slots_all = ((vectors, peers * slots), f32)
    edge_count = elem_count // 2
    idx, st_edge, mt_edge, st_inner, mt_inner, own_diag, right_at, diag_at, same = call(
        bind(tables_body), "tables", [S, S] + [V] * 5 + [S, V, V],
        [
            ((elem_count, LANES), i32),
            ((edge_count, 3 * LANES), f32), ((edge_count, LANES), f32),
            ((elem_count - edge_count, 3 * LANES), f32), ((elem_count - edge_count, LANES), f32),
            square, slots_all, slots_all, ((peers * slots, peers * slots), jnp.bfloat16),
        ],
        (0, 1, 2, 5, 6, 7, 8),
        [
            pltpu.VMEM((LANES, elem_count), i32), pltpu.VMEM((LANES, elem_count), f32),
            pltpu.VMEM((elem_count, LANES), f32),
        ],
        (8,),
    )(peer_rank, density, elem_nodes, stiffness, mass, regions, squares, base, node_row, right_side)

    send_shape = ((devices, ROWS, LANES), f32)
    send, inverse_at = call(
        bind(start_body), "start", [V] * 5, [send_shape, slots_all], (1,), (), range(5)
    )(peer_row, recv, right_at, diag_at, same)
    diag_recv = recv
    recv = exchange(send)
    inverse, z, energy = call(
        bind(first_fields_body), "first_fields", [V] * 5, [square, field, tile], range(3), (), range(5),
    )(peer_row, node_row, diag_recv, own_diag, right_side)

    weight_rows = [
        pltpu.VMEM((2 * LANES, 6 * LANES), jnp.bfloat16), pltpu.VMEM((6 * LANES, 2 * LANES), jnp.bfloat16)
    ]

    def inner_part(z):
        return call(
            bind(inner_body), "inner", [V] * 6, [half_rows, tile], range(2),
            [pltpu.VMEM(*half_rows), *weight_rows], (0, 1, 4, 5),
        )(z, idx, st_inner, mt_inner, weights1, weights2)

    def edge_part(recv, z, energy, curve):
        return call(
            bind(edge_body), "edge", [V] * 11,
            [half_rows, ((devices * (ROWS + 1), 1, LANES), f32)], (0,),
            [pltpu.VMEM(*half_rows), pltpu.VMEM((peers, ROWS, LANES), f32), *weight_rows], range(11),
        )(peer_row, recv, z, idx, st_edge, mt_edge, pos, weights1, weights2, energy, curve)

    wide = 2 * peers * slots
    scratch = [
        pltpu.VMEM((vectors * pairs, wide), jnp.bfloat16), pltpu.VMEM((LANES, wide), jnp.bfloat16),
        pltpu.VMEM((vectors * pairs, LANES), f32), pltpu.VMEM(*field), pltpu.VMEM(*field),
        pltpu.SemaphoreType.DMA((2,)),
    ]
    inner, curve = inner_part(z)
    result, send = edge_part(recv, z, energy, curve)
    recv = exchange(send)
    own, image_at = call(
        bind(edge_scatter_pick_body), "edge_scatter_pick", [S] + [V] * 4, [field, slots_all], (1,), (),
        (1, 2, 3, 4),
    )(base, node_row, result, idx, inner)
    send, coefs = call(
        bind(step_body), "step", [V] * 6, [send_shape, ((2, ROWS, LANES), f32)], (1,), (),
        range(6),
    )(peer_row, recv, right_at, inverse_at, image_at, same)
    sum_recv = recv
    recv = exchange(send)
    w, z, energy = call(
        bind(next_fields_body), "next_fields", [V] * 3 + [hbm(), hbm()] + [V] * 2, [field, field, tile], (1, 2), scratch,
        (0, 1, 2, 5, 6),
    )(peer_row, node_row, sum_recv, own, right_side, inverse, coefs)
    inner, curve = inner_part(z)
    result, send = edge_part(recv, z, energy, curve)
    recv = exchange(send)
    (own,) = call(bind(edge_scatter_body), "edge_scatter", [V] * 3, [field], (0,), (), range(3))(
        result, idx, inner
    )
    return call(
        bind(last_body), "last", [V] * 4 + [hbm(), V, hbm()] + [V] * 2, [field, field], (),
        scratch + [
            pltpu.VMEM(*field), pltpu.VMEM(*field), pltpu.SemaphoreType.DMA((pairs // LAST_STEP, 2)),
        ],
        (0, 1, 2, 3, 5, 7, 8), out_specs=(hbm(), hbm()),
    )(peer_row, node_row, recv, own, right_side, inverse, w, z, coefs)


def solution(mesh):
    placed = (
        P(None, "dom"),
        P(None, None, "dom"),
        P(None, "dom"),
        P("dom"),
        P(),
        P(None, "dom"),
        P("dom", None),
        P("dom", None, None),
    )
    return jax.shard_map(
        on_device,
        mesh=mesh,
        in_specs=placed,
        out_specs=(P(None, "dom"), P(None, "dom")),
        check_vma=False,
    )
```

```python
import functools

import jax
import jax.numpy as jnp
import numpy as np
from jax import lax
from jax.experimental import pallas as pl
from jax.experimental.pallas import tpu as pltpu
from jax.sharding import PartitionSpec as P

ITERS = 2
LANES = 128
ROWS = 8
NONE = 255
SIDE = 5
NPE = SIDE**3


def gll_matrix():
    points = np.array([-1.0, -np.sqrt(3.0 / 7.0), 0.0, np.sqrt(3.0 / 7.0), 1.0])
    weights = np.array(
        [
            1.0 / np.prod([points[column] - points[other] for other in range(5) if other != column])
            for column in range(5)
        ]
    )
    matrix = np.zeros((5, 5))
    for row_index in range(5):
        for column in range(5):
            if row_index != column:
                matrix[row_index, column] = (
                    weights[column] / weights[row_index] / (points[row_index] - points[column])
                )
        matrix[row_index, row_index] = -np.sum(matrix[row_index])
    return matrix


def direction_matrices():
    base = np.asarray(gll_matrix(), np.float32)
    eye = np.eye(SIDE, dtype=np.float32)
    return [
        np.einsum("ai,bj,ck->abcijk", *factors).reshape(NPE, NPE)
        for factors in ((base, eye, eye), (eye, base, eye), (eye, eye, base))
    ]


def split_np(values):
    high = values.astype(jnp.bfloat16)
    low = (values - high.astype(np.float32)).astype(jnp.bfloat16)
    return high, low


def constant_operands():
    mats = direction_matrices()
    grad = np.zeros((LANES, 3 * LANES), np.float32)
    for d in range(3):
        grad[:NPE, d * LANES : d * LANES + NPE] = mats[d].T
    high, low = split_np(grad)
    first = np.concatenate([high, low], axis=1)
    second = np.concatenate([high.T, low.T], axis=1)
    squares = np.stack(split_np(np.stack([m.T * m.T for m in mats])))
    return jnp.asarray(first), jnp.asarray(second), jnp.asarray(squares)


def take(values, index):
    numbers = lax.GatherDimensionNumbers(
        offset_dims=(),
        collapsed_slice_dims=(1,),
        start_index_map=(1,),
        operand_batching_dims=(0,),
        start_indices_batching_dims=(0,),
    )
    return lax.gather(
        values, index[..., None], numbers, (1, 1), mode=lax.GatherScatterMode.PROMISE_IN_BOUNDS
    )


def iota(shape, axis):
    return lax.broadcasted_iota(jnp.int32, shape, axis)


def spread(row, rows=ROWS):
    return jnp.broadcast_to(row, (rows, row.shape[-1]))


def codes_of(nodes, lane_offset, peer_ref, own_count, peer_count, window):
    pair = (iota(nodes.shape, 1) + lane_offset) >> 1
    own = nodes - pair * window
    ref = nodes - own_count
    sender = ref // LANES
    slot = jnp.zeros_like(ref)
    for p in range(1, peer_count):
        slot = jnp.where(sender == peer_ref[0, p], p, slot)
    return jnp.where(ref >= 0, window + slot * LANES + (ref & (LANES - 1)), own)


def vmem():
    return pl.BlockSpec(memory_space=pltpu.VMEM)


def smem():
    return pl.BlockSpec(memory_space=pltpu.SMEM)


def hbm():
    return pl.BlockSpec(memory_space=pltpu.HBM)


def call(body, name, in_specs, outs, stay, scratch=(), resident=(), grid=(), out_specs=None):
    kernel = pl.pallas_call(
        body,
        name=name,
        grid=grid,
        in_specs=in_specs,
        out_specs=out_specs or tuple(vmem() for _ in outs),
        out_shape=tuple(
            (pltpu.VMEM if k in stay else pltpu.HBM)(shape, dtype)
            for k, (shape, dtype) in enumerate(outs)
        ),
        scratch_shapes=list(scratch),
        compiler_params=pltpu.CompilerParams(vmem_limit_bytes=24 << 20),
    )

    def run(*operands):
        return kernel(
            *[
                pltpu.with_memory_space_constraint(operand, pltpu.VMEM if k in resident else pltpu.HBM)
                for k, operand in enumerate(operands)
            ]
        )

    return run


def element_sums(mass, region, density, stiff, squares):
    dens = jnp.where(region == 0, density[0], jnp.where(region == 1, density[1], density[2]))
    term = mass * dens
    total = term
    for d in range(3):
        high = stiff[d].astype(jnp.bfloat16)
        low = (stiff[d] - high.astype(jnp.float32)).astype(jnp.bfloat16)
        for weight, part in ((squares[0, d], high), (squares[0, d], low), (squares[1, d], high)):
            total = total + jnp.dot(weight, part, preferred_element_type=jnp.float32)
    return term, total


def ghost_diag_body(
    cfg, peer, density, nodes, stiff, mass, region, squares, shared, send, pos, peer_row, base, node_row
):
    lanes = iota((1, LANES), 1)
    row = jnp.zeros((1, LANES), jnp.int32)
    for p in range(cfg["peers"]):
        row = jnp.where(lanes == p, peer[0, p], row)
        base[p] = shared[p] & (-LANES)
        node_row[:, p * LANES : (p + 1) * LANES] = shared[p]
    peer_row[...] = row
    run = cfg["run"]
    _, edge = element_sums(mass[...], region[...], density, stiff, squares)
    code = codes_of(nodes[...], 0, peer, cfg["own"], cfg["peers"], cfg["window"])
    lane = iota(code.shape, 1)
    base = code - (cfg["window"] + run * (lane >> 1))
    place = iota(code.shape, 0) + LANES * (lane & 1)
    flat = iota((ROWS, LANES), 0) * LANES + iota((ROWS, LANES), 1)
    pair = (flat * cfg["magic"]) >> 16
    hop = flat - pair * run
    pair_lane = jnp.minimum(2 * pair, LANES - 1)
    got = jnp.zeros((ROWS, LANES), jnp.float32)
    where_at = jnp.zeros((ROWS, LANES), jnp.int32)
    for h in range(run):
        hit = base == h
        position = jnp.sum(jnp.where(hit, place, 0), axis=0, keepdims=True)
        value = jnp.sum(jnp.where(hit, edge, 0.0), axis=0, keepdims=True)
        position, value = spread(position), spread(value)
        position = position + pltpu.roll(position, LANES - 1, 1)
        value = value + pltpu.roll(value, LANES - 1, 1)
        got = jnp.where(hop == h, take(value, pair_lane), got)
        where_at = jnp.where(hop == h, take(position, pair_lane), where_at)
    pos[...] = where_at
    send[...] = jnp.zeros(send.shape, jnp.float32)
    for p in range(cfg["peers"]):
        send[peer[0, p]] = got[p : p + 1]


def tables_body(
    cfg, peer, density, nodes, stiff, mass, region, squares, base_s, node_row, right,
    idx, st_edge, mt_edge, st_inner, mt_inner, own_diag, right_at, diag_at, same,
    code_pad, value_pad, rows,
):
    code_pad[...] = jnp.full(code_pad.shape, NONE, jnp.int32)
    value_pad[...] = jnp.zeros(value_pad.shape, jnp.float32)

    def turned(ref):
        return jnp.concatenate([ref[:, :LANES].T, ref[:, LANES:].T], axis=0)

    for b in range(2):
        cols = slice(b * LANES, (b + 1) * LANES)
        code_pad[:NPE, cols] = codes_of(
            nodes[:, cols], b * LANES, peer, cfg["own"], cfg["peers"], cfg["window"]
        )
    idx[...] = turned(code_pad)
    term, diag = element_sums(mass[...], region[...], density, stiff, squares)
    value_pad[:NPE] = diag
    rows[...] = turned(value_pad)
    for g in range(0, cfg["pairs"], 2):
        lines = [
            spread(jnp.concatenate([rows[2 * k : 2 * k + 1, :], rows[2 * k + 1 : 2 * k + 2, :]], axis=1))
            for k in (g, g + 1)
        ]
        for k, sums in enumerate(scatter_pairs(lines, idx, g)):
            own_diag[g + k : g + k + 1, :] = sums[:1]
    for d in range(3):
        value_pad[:NPE] = stiff[d]
        cols = slice(d * LANES, (d + 1) * LANES)
        st_edge[:, cols] = value_pad[:, :LANES].T
        st_inner[:, cols] = value_pad[:, LANES:].T
    value_pad[:NPE] = term
    mt_edge[...] = value_pad[:, :LANES].T
    mt_inner[...] = value_pad[:, LANES:].T
    pick(cfg, right, base_s, node_row, right_at)
    node = node_row[...]
    wide = node.shape[1]
    hot = jnp.where(iota((LANES, wide), 0) == (node & (LANES - 1)), 1.0, 0.0).astype(jnp.bfloat16)
    here = iota((LANES, wide), 0) == (node >> 7)
    at_slots = jnp.zeros((1, wide), jnp.float32)
    for part in reversed(parts_of(own_diag[...], 3)):
        seen = jnp.dot(part.astype(jnp.bfloat16), hot, preferred_element_type=jnp.float32)
        at_slots = at_slots + jnp.sum(jnp.where(here, seen, 0.0), axis=0, keepdims=True)
    diag_at[...] = spread(at_slots)
    for p in range(cfg["peers"]):
        column = jnp.broadcast_to(node[:, p * LANES : (p + 1) * LANES], (LANES, LANES)).T
        for q in range(cfg["peers"]):
            same[p * LANES : (p + 1) * LANES, q * LANES : (q + 1) * LANES] = jnp.where(
                column == node[:, q * LANES : (q + 1) * LANES], 1.0, 0.0
            ).astype(jnp.bfloat16)


def scatter_rows(rows, idx, g):
    node = iota((LANES, LANES), 0)
    spots = jnp.concatenate(
        [jnp.where(node == idx[2 * g + k : 2 * g + k + 1, :], 1.0, 0.0) for k in range(2)], axis=1
    ).astype(jnp.bfloat16)
    high = rows.astype(jnp.bfloat16).astype(jnp.float32)
    both = jnp.concatenate([high, rows - high], axis=0).astype(jnp.bfloat16)
    sums = lax.dot_general(both, spots, (((1,), (1,)), ((), ())), preferred_element_type=jnp.float32)
    return sums[:ROWS] + sums[ROWS:]


def scatter_pairs(rows, idx, g):
    node = iota((LANES, LANES), 0)
    spots = [
        jnp.concatenate(
            [jnp.where(node == idx[e : e + 1, :], 1.0, 0.0) for e in (2 * pair, 2 * pair + 1)], axis=1
        ).astype(jnp.bfloat16)
        for pair in (g, g + 1)
    ]
    parts = []
    for values in rows:
        high = values.astype(jnp.bfloat16).astype(jnp.float32)
        parts += [high, values - high]
    sums = nt_dot(jnp.concatenate(parts, axis=0).astype(jnp.bfloat16), jnp.concatenate(spots, axis=0))
    own = (sums[: 2 * ROWS, :LANES], sums[2 * ROWS :, LANES:])
    return [x[:ROWS] + x[ROWS:] for x in own]


def peers_of(cfg, peer_row):
    lane = iota((1, LANES), 1)
    return [jnp.max(jnp.where(lane == p, peer_row[...], 0)) for p in range(cfg["peers"])]


def pick(cfg, field, base_s, node_row, out):
    lane = iota((ROWS, LANES), 1)
    for p in range(cfg["peers"]):
        low = spread(node_row[:, p * LANES : (p + 1) * LANES] & (LANES - 1))
        got = jnp.zeros((ROWS, LANES), jnp.float32)
        for c in range(LANES):
            base = pl.multiple_of(base_s[p, 0, c], LANES)
            got = jnp.where(lane == c, take(field[:, pl.ds(base, LANES)], low), got)
        out[:, p * LANES : (p + 1) * LANES] = got


def nt_dot(left, right):
    return lax.dot_general(left, right, (((1,), (1,)), ((), ())), preferred_element_type=jnp.float32)


def parts_of(values, count):
    parts = []
    for _ in range(count):
        part = values.astype(jnp.bfloat16).astype(jnp.float32)
        parts.append(part)
        values = values - part
    return parts


def received_diag(cfg, peer, recv):
    return jnp.concatenate([recv[peer[p]] for p in range(cfg["peers"])], axis=1)


def received_rows(cfg, peer, recv):
    blocks = []
    for p in range(cfg["peers"]):
        first = peer[p] * (ROWS + 1)
        blocks.append(jnp.concatenate([recv[first + v] for v in range(ROWS)], axis=0))
    return jnp.concatenate(blocks, axis=1)


def put_slots(cfg, peer, values, out):
    for p in range(cfg["peers"]):
        out[peer[p]] = values[:, p * LANES : (p + 1) * LANES]


def start_body(cfg, peer_row, recv, right_at, diag_at, same, out, inverse_at):
    peer = peers_of(cfg, peer_row)
    got = spread(received_diag(cfg, peer, recv))
    top, middle, bottom = parts_of(got, 3)
    both = jnp.concatenate([top, middle], axis=0).astype(jnp.bfloat16)
    more = jnp.concatenate([bottom, bottom], axis=0).astype(jnp.bfloat16)
    first = nt_dot(both, same[...])
    total = diag_at[...] + (first[:ROWS] + (first[ROWS:] + nt_dot(more, same[...])[:ROWS]))
    inverse = 1.0 / total
    inverse_at[...] = inverse
    out[...] = jnp.zeros(out.shape, jnp.float32)
    put_slots(cfg, peer, right_at[...] * inverse, out)


def first_fields_body(cfg, peer_row, node_row, recv, own_diag, right, inverse, z, energy):
    peer = peers_of(cfg, peer_row)
    windows = cfg["pairs"]
    node, got = node_row[...], received_diag(cfg, peer, recv)
    here = iota((windows, got.shape[1]), 0) == (node >> 7)
    hot = jnp.where(iota((LANES, got.shape[1]), 0) == (node & (LANES - 1)), 1.0, 0.0).astype(jnp.bfloat16)
    total = own_diag[...]
    for part in parts_of(got, 3):
        total = total + nt_dot(jnp.where(here, spread(part, windows), 0.0).astype(jnp.bfloat16), hot)
    inverse[...] = 1.0 / total
    acc = jnp.zeros((ROWS, LANES), jnp.float32)
    for g in range(windows):
        cols = slice(g * LANES, (g + 1) * LANES)
        scaled = right[:, cols] * spread(inverse[g : g + 1, :])
        z[:, cols] = scaled
        acc = acc + right[:, cols] * scaled
    energy[...] = acc


def apply_rows(values, st, mt, weights1, weights2):
    count = values.shape[0] // ROWS

    def halves(x):
        high = x.astype(jnp.bfloat16)
        return jnp.concatenate([high, (x - high.astype(jnp.float32)).astype(jnp.bfloat16)], axis=1)

    both = jnp.dot(halves(values), weights1[...], preferred_element_type=jnp.float32)
    wide = 3 * LANES
    grad = (both[:, :wide] + both[:, wide:]).reshape(count, ROWS, wide)
    flux = (grad * st[:, None, :]).reshape(count * ROWS, wide)
    both = jnp.dot(halves(flux), weights2[...], preferred_element_type=jnp.float32)
    lumped = (values.reshape(count, ROWS, LANES) * mt[:, None, :]).reshape(count * ROWS, LANES)
    return both[:, :LANES] + both[:, LANES:] + lumped


def fill_weights(weights1, weights2, both1, both2):
    wide = 3 * LANES
    both1[:LANES] = weights1[...]
    both1[LANES:, :wide] = weights1[:, :wide]
    both1[LANES:, wide:] = jnp.zeros((LANES, wide), jnp.bfloat16)
    both2[:wide] = weights2[...]
    both2[wide:] = weights2[...]


CHUNK = 16


def apply_half(values, result, st, mt, weights1, weights2):
    acc = jnp.zeros((ROWS, LANES), jnp.float32)
    for c in range(values.shape[0] // (ROWS * CHUNK)):
        rows = slice(c * CHUNK * ROWS, (c + 1) * CHUNK * ROWS)
        elems = slice(c * CHUNK, (c + 1) * CHUNK)
        v = values[rows]
        r = apply_rows(v, st[elems], mt[elems], weights1, weights2)
        result[rows] = r
        acc = acc + jnp.sum((v * r).reshape(CHUNK, ROWS, LANES), axis=0)
    return acc


def scatter_half(edge, inner, idx, out):
    count = edge.shape[0] // (2 * ROWS)
    for g in range(idx.shape[0] // 2):
        half, e = (edge, 2 * g * ROWS) if g < count else (inner, 2 * (g - count) * ROWS)
        rows = jnp.concatenate([half[e : e + ROWS], half[e + ROWS : e + 2 * ROWS]], axis=1)
        out[:, g * LANES : (g + 1) * LANES] = scatter_rows(rows, idx, g)


def inner_body(cfg, z, idx, st, mt, w1, w2, result, curve, values, both1, both2):
    fill_weights(w1, w2, both1, both2)
    edge, pairs = cfg["edge_pairs"], cfg["pairs"]
    for g in range(edge, pairs):
        window = z[:, g * LANES : (g + 1) * LANES]
        for parity in range(2):
            e = 2 * g + parity
            at = (e - 2 * edge) * ROWS
            values[at : at + ROWS] = take(window, spread(idx[e : e + 1, :] & (LANES - 1)))
    curve[...] = apply_half(values, result, st, mt, both1, both2)


def edge_body(
    cfg, peer_row, recv, z, idx, st, mt, pos, w1, w2, energy, curve, result, out, values, ghosts, both1, both2
):
    peer = peers_of(cfg, peer_row)
    fill_weights(w1, w2, both1, both2)
    run, edge, peers = cfg["run"], cfg["edge_pairs"], cfg["peers"]
    for p in range(peers):
        ghosts[p] = recv[peer[p]]
    spans = []
    for g in range(edge):
        low, high = run * g // LANES, (run * (g + 1) - 1) // LANES
        spans.append((low, high))
        window = z[:, g * LANES : (g + 1) * LANES]
        for parity in range(2):
            e = 2 * g + parity
            code = spread(idx[e : e + 1, :])
            at = code & (LANES - 1)
            got = take(ghosts[low], at)
            if high > low:
                got = jnp.where(code < LANES * (high + 1), got, take(ghosts[high], at))
            values[e * ROWS : (e + 1) * ROWS] = jnp.where(code < LANES, take(window, at), got)
    acc = apply_half(values, result, st, mt, both1, both2) + curve[...]
    lane = iota((ROWS, LANES), 1)
    sums = [jnp.zeros((ROWS, LANES), jnp.float32) for _ in range(peers)]
    for g in range(edge):
        for p in range(spans[g][0], spans[g][1] + 1):
            place = spread(pos[p : p + 1, :])
            at = place & (LANES - 1)
            e = 2 * g * ROWS
            value = jnp.where(
                place < LANES, take(result[e : e + ROWS], at), take(result[e + ROWS : e + 2 * ROWS], at)
            )
            begin, end = run * g - p * LANES, run * (g + 1) - p * LANES
            sums[p] = jnp.where((lane >= begin) & (lane < end), value, sums[p])
    row = iota((ROWS, LANES), 0)
    dots = jnp.where(lane == row, jnp.sum(energy[...], axis=1, keepdims=True), 0.0)
    dots = jnp.where(lane == row + ROWS, jnp.sum(acc, axis=1, keepdims=True), dots)
    dots = jnp.sum(dots, axis=0, keepdims=True)
    out[...] = jnp.zeros(out.shape, jnp.float32)
    for n in range(out.shape[0] // (ROWS + 1)):
        out[n * (ROWS + 1) + ROWS] = dots
    for p in range(peers):
        for v in range(ROWS):
            out[peer[p] * (ROWS + 1) + v] = sums[p][v : v + 1]


def edge_scatter_body(cfg, result, idx, inner, out):
    scatter_half(result, inner, idx, out)


def edge_scatter_pick_body(cfg, base_s, node_row, result, idx, inner, out, at_slots):
    edge_scatter_body(cfg, result, idx, inner, out)
    pick(cfg, out, base_s, node_row, at_slots)


RETURN_STEP = 32


def returned_sums(cfg, peer, node_row, recv, left, hot):
    windows = cfg["pairs"]
    node, value = node_row[...], received_rows(cfg, peer, recv)
    wide = node.shape[1]
    high, low = parts_of(value, 2)
    lanes = jnp.where(iota((LANES, wide), 0) == (node & (LANES - 1)), 1.0, 0.0).astype(jnp.bfloat16)
    hot[:, :wide] = lanes
    hot[:, wide:] = lanes
    block = spread(node >> 7)
    for start in range(0, windows, RETURN_STEP):
        for g in range(start, start + RETURN_STEP, 2):
            rows = slice(g * ROWS, (g + 2) * ROWS)
            even, odd = block == g, block == g + 1
            left[rows, :wide] = jnp.concatenate(
                [jnp.where(even, high, 0.0), jnp.where(odd, high, 0.0)], axis=0
            ).astype(jnp.bfloat16)
            left[rows, wide:] = jnp.concatenate(
                [jnp.where(even, low, 0.0), jnp.where(odd, low, 0.0)], axis=0
            ).astype(jnp.bfloat16)
        yield start, nt_dot(left[start * ROWS : (start + RETURN_STEP) * ROWS], hot[...])


def dot_totals(recv):
    total = recv[ROWS]
    for n in range(1, recv.shape[0] // (ROWS + 1)):
        total = total + recv[n * (ROWS + 1) + ROWS]
    total = spread(total)
    lane, row = iota((ROWS, LANES), 1), iota((ROWS, LANES), 0)
    return [
        jnp.broadcast_to(
            jnp.sum(jnp.where(lane == row + k * ROWS, total, 0.0), axis=1, keepdims=True), (ROWS, LANES)
        )
        for k in range(2)
    ]


def step_body(cfg, peer_row, recv, right_at, inverse_at, image_at, same, out, coefs):
    peer = peers_of(cfg, peer_row)
    energy_now, curve_now = dot_totals(recv)
    alpha = energy_now / curve_now
    coefs[0] = alpha
    coefs[1] = energy_now
    both = jnp.concatenate(parts_of(received_rows(cfg, peer, recv), 2), axis=0).astype(jnp.bfloat16)
    got = nt_dot(both, same[...])
    image = image_at[...] + (got[:ROWS] + got[ROWS:])
    left_over = right_at[...] - spread_lanes(alpha, image.shape[1]) * image
    out[...] = jnp.zeros(out.shape, jnp.float32)
    put_slots(cfg, peer, left_over * inverse_at[...], out)


def spread_lanes(tile, wide):
    return jnp.concatenate([tile] * (wide // LANES), axis=1)


def window_sums(*operands):
    for start, sums in returned_sums(*operands):
        for k in range(RETURN_STEP):
            yield start + k, sums[k * ROWS : (k + 1) * ROWS]


def next_fields_body(
    cfg, peer_row, node_row, recv, own_hbm, right_hbm, inverse, coefs, w, z1, energy, left, hot, right, own, arrived
):
    fetches = [
        pltpu.make_async_copy(there, here, arrived.at[k]) for k, (there, here) in enumerate(((right_hbm, right), (own_hbm, own)))
    ]
    for fetch in fetches:
        fetch.start()
    peer = peers_of(cfg, peer_row)
    alpha = coefs[0]
    for fetch in fetches:
        fetch.wait()
    acc = jnp.zeros((ROWS, LANES), jnp.float32)
    for g, sums in window_sums(cfg, peer, node_row, recv, left, hot):
        cols = slice(g * LANES, (g + 1) * LANES)
        image = own[:, cols] + sums
        w[:, cols] = image
        left_over = right[:, cols] - alpha * image
        scaled = left_over * spread(inverse[g : g + 1, :])
        z1[:, cols] = scaled
        acc = acc + left_over * scaled
    energy[...] = acc


LAST_STEP = 32


def last_body(
    cfg, peer_row, node_row, recv, own, right_hbm, inverse, w_hbm, z1, coefs,
    solution_hbm, residual_hbm, left, hot, right, w, arrived, solution, residual, sent,
):
    fetches = [
        pltpu.make_async_copy(there, here, arrived.at[k]) for k, (there, here) in enumerate(((right_hbm, right), (w_hbm, w)))
    ]
    for fetch in fetches:
        fetch.start()
    peer = peers_of(cfg, peer_row)
    windows = cfg["pairs"]
    energy_next, curve_next = dot_totals(recv)
    alpha, energy_now = coefs[0], coefs[1]
    beta = energy_next / energy_now
    step = energy_next / (curve_next - beta * energy_next / alpha)
    copies = []
    for fetch in fetches:
        fetch.wait()
    for g, sums in window_sums(cfg, peer, node_row, recv, left, hot):
        cols = slice(g * LANES, (g + 1) * LANES)
        image = own[:, cols] + sums
        start, before = right[:, cols], w[:, cols]
        z0 = start * spread(inverse[g : g + 1, :])
        residual[:, cols] = (start - alpha * before) - step * (image + beta * before)
        solution[:, cols] = alpha * z0 + step * (z1[:, cols] + beta * z0)
        if (g + 1) % LAST_STEP == 0:
            done = slice((g + 1 - LAST_STEP) * LANES, (g + 1) * LANES)
            for k, (here, there) in enumerate(((solution, solution_hbm), (residual, residual_hbm))):
                copies.append(
                    pltpu.make_async_copy(here.at[:, done], there.at[:, done], sent.at[g // LAST_STEP, k])
                )
                copies[-1].start()
    for copy in copies:
        copy.wait()


def on_device(right_side, stiffness, mass, region, density, elem_nodes, peer_rank, send_nodes):
    vectors, own_count = right_side.shape
    elem_count = elem_nodes.shape[1]
    pairs = elem_count // 2
    edge_pairs = pairs // 2
    peers, slots = send_nodes.shape[1], send_nodes.shape[2]
    devices = lax.axis_size("dom")
    run = peers * slots // edge_pairs
    magic = (1 << 16) // run + 1
    flat = np.arange(ROWS * LANES)
    if (
        vectors != ROWS or own_count != pairs * LANES or slots != LANES or pairs != LANES
        or peers * slots != run * edge_pairs or peers > ROWS or run > LANES
        or ((flat * magic) >> 16 != flat // run).any()
    ):
        raise ValueError("unsupported sizes")
    cfg = dict(
        own=own_count, pairs=pairs, edge_pairs=edge_pairs, peers=peers, run=run, magic=magic,
        window=own_count // pairs,
    )
    f32, i32 = jnp.float32, jnp.int32
    weights1, weights2, squares = constant_operands()
    V, S = vmem(), smem()
    field = ((vectors, own_count), f32)
    tile = ((ROWS, LANES), f32)
    square = ((LANES, LANES), f32)
    half_rows = ((elem_count // 2 * ROWS, LANES), f32)

    def bind(body):
        return functools.partial(body, cfg)

    def exchange(values):
        return lax.all_to_all(values, "dom", split_axis=0, concat_axis=0, tiled=True)

    regions = region.reshape(1, elem_count)
    half_specs = [
        pl.BlockSpec((NPE, LANES), lambda _: (0, 0)),
        pl.BlockSpec((3, NPE, LANES), lambda _: (0, 0, 0)),
        pl.BlockSpec((NPE, LANES), lambda _: (0, 0)),
        pl.BlockSpec((1, LANES), lambda _: (0, 0)),
    ]
    shared = jnp.transpose(send_nodes, (1, 0, 2))
    send, pos, peer_row, base, node_row = call(
        bind(ghost_diag_body), "ghost_diag", [S, S, *half_specs, V, V],
        [
            ((devices, 1, LANES), f32), ((ROWS, LANES), i32), ((1, LANES), i32), ((peers, 1, slots), i32),
            ((1, peers * slots), i32),
        ],
        (1, 2, 4), grid=(1,),
    )(peer_rank, density, elem_nodes, stiffness, mass, regions, squares, shared)
    recv = exchange(send)
    slots_all = ((vectors, peers * slots), f32)
    edge_count = elem_count // 2
    idx, st_edge, mt_edge, st_inner, mt_inner, own_diag, right_at, diag_at, same = call(
        bind(tables_body), "tables", [S, S] + [V] * 5 + [S, V, V],
        [
            ((elem_count, LANES), i32),
            ((edge_count, 3 * LANES), f32), ((edge_count, LANES), f32),
            ((elem_count - edge_count, 3 * LANES), f32), ((elem_count - edge_count, LANES), f32),
            square, slots_all, slots_all, ((peers * slots, peers * slots), jnp.bfloat16),
        ],
        (0, 1, 2, 5, 6, 7, 8),
        [
            pltpu.VMEM((LANES, elem_count), i32), pltpu.VMEM((LANES, elem_count), f32),
            pltpu.VMEM((elem_count, LANES), f32),
        ],
        (8,),
    )(peer_rank, density, elem_nodes, stiffness, mass, regions, squares, base, node_row, right_side)

    send_shape = ((devices, ROWS, LANES), f32)
    send, inverse_at = call(
        bind(start_body), "start", [V] * 5, [send_shape, slots_all], (1,), (), range(5)
    )(peer_row, recv, right_at, diag_at, same)
    diag_recv = recv
    recv = exchange(send)
    inverse, z, energy = call(
        bind(first_fields_body), "first_fields", [V] * 5, [square, field, tile], range(3), (), range(5),
    )(peer_row, node_row, diag_recv, own_diag, right_side)

    weight_rows = [
        pltpu.VMEM((2 * LANES, 6 * LANES), jnp.bfloat16), pltpu.VMEM((6 * LANES, 2 * LANES), jnp.bfloat16)
    ]

    def inner_part(z):
        return call(
            bind(inner_body), "inner", [V] * 6, [half_rows, tile], range(2),
            [pltpu.VMEM(*half_rows), *weight_rows], (0, 1, 4, 5),
        )(z, idx, st_inner, mt_inner, weights1, weights2)

    def edge_part(recv, z, energy, curve):
        return call(
            bind(edge_body), "edge", [V] * 11,
            [half_rows, ((devices * (ROWS + 1), 1, LANES), f32)], (0,),
            [pltpu.VMEM(*half_rows), pltpu.VMEM((peers, ROWS, LANES), f32), *weight_rows], range(11),
        )(peer_row, recv, z, idx, st_edge, mt_edge, pos, weights1, weights2, energy, curve)

    wide = 2 * peers * slots
    scratch = [
        pltpu.VMEM((vectors * pairs, wide), jnp.bfloat16), pltpu.VMEM((LANES, wide), jnp.bfloat16),
        pltpu.VMEM(*field), pltpu.VMEM(*field),
        pltpu.SemaphoreType.DMA((2,)),
    ]
    inner, curve = inner_part(z)
    result, send = edge_part(recv, z, energy, curve)
    recv = exchange(send)
    own, image_at = call(
        bind(edge_scatter_pick_body), "edge_scatter_pick", [S] + [V] * 4, [field, slots_all], (1,), (),
        (1, 2, 3, 4),
    )(base, node_row, result, idx, inner)
    send, coefs = call(
        bind(step_body), "step", [V] * 6, [send_shape, ((2, ROWS, LANES), f32)], (1,), (),
        range(6),
    )(peer_row, recv, right_at, inverse_at, image_at, same)
    sum_recv = recv
    recv = exchange(send)
    w, z, energy = call(
        bind(next_fields_body), "next_fields", [V] * 3 + [hbm(), hbm()] + [V] * 2, [field, field, tile], (1, 2), scratch,
        (0, 1, 2, 5, 6),
    )(peer_row, node_row, sum_recv, own, right_side, inverse, coefs)
    inner, curve = inner_part(z)
    result, send = edge_part(recv, z, energy, curve)
    recv = exchange(send)
    (own,) = call(bind(edge_scatter_body), "edge_scatter", [V] * 3, [field], (0,), (), range(3))(
        result, idx, inner
    )
    return call(
        bind(last_body), "last", [V] * 4 + [hbm(), V, hbm()] + [V] * 2, [field, field], (),
        scratch + [
            pltpu.VMEM(*field), pltpu.VMEM(*field), pltpu.SemaphoreType.DMA((pairs // LAST_STEP, 2)),
        ],
        (0, 1, 2, 3, 5, 7, 8), out_specs=(hbm(), hbm()),
    )(peer_row, node_row, recv, own, right_side, inverse, w, z, coefs)


def solution(mesh):
    placed = (
        P(None, "dom"),
        P(None, None, "dom"),
        P(None, "dom"),
        P("dom"),
        P(),
        P(None, "dom"),
        P("dom", None),
        P("dom", None, None),
    )
    return jax.shard_map(
        on_device,
        mesh=mesh,
        in_specs=placed,
        out_specs=(P(None, "dom"), P(None, "dom")),
        check_vma=False,
    )
```

```python
import functools

import jax
import jax.numpy as jnp
import numpy as np
from jax import lax
from jax.experimental import pallas as pl
from jax.experimental.pallas import tpu as pltpu
from jax.sharding import PartitionSpec as P

ITERS = 2
LANES = 128
ROWS = 8
NONE = 255
SIDE = 5
NPE = SIDE**3


def gll_matrix():
    points = np.array([-1.0, -np.sqrt(3.0 / 7.0), 0.0, np.sqrt(3.0 / 7.0), 1.0])
    weights = np.array(
        [
            1.0 / np.prod([points[column] - points[other] for other in range(5) if other != column])
            for column in range(5)
        ]
    )
    matrix = np.zeros((5, 5))
    for row_index in range(5):
        for column in range(5):
            if row_index != column:
                matrix[row_index, column] = (
                    weights[column] / weights[row_index] / (points[row_index] - points[column])
                )
        matrix[row_index, row_index] = -np.sum(matrix[row_index])
    return matrix


def direction_matrices():
    base = np.asarray(gll_matrix(), np.float32)
    eye = np.eye(SIDE, dtype=np.float32)
    return [
        np.einsum("ai,bj,ck->abcijk", *factors).reshape(NPE, NPE)
        for factors in ((base, eye, eye), (eye, base, eye), (eye, eye, base))
    ]


def split_np(values):
    high = values.astype(jnp.bfloat16)
    low = (values - high.astype(np.float32)).astype(jnp.bfloat16)
    return high, low


def constant_operands():
    mats = direction_matrices()
    grad = np.zeros((LANES, 3 * LANES), np.float32)
    for d in range(3):
        grad[:NPE, d * LANES : d * LANES + NPE] = mats[d].T
    high, low = split_np(grad)
    first = np.concatenate([high, low], axis=1)
    second = np.concatenate([high.T, low.T], axis=1)
    squares = np.stack(split_np(np.stack([m.T * m.T for m in mats])))
    return jnp.asarray(first), jnp.asarray(second), jnp.asarray(squares)


def take(values, index):
    numbers = lax.GatherDimensionNumbers(
        offset_dims=(),
        collapsed_slice_dims=(1,),
        start_index_map=(1,),
        operand_batching_dims=(0,),
        start_indices_batching_dims=(0,),
    )
    return lax.gather(
        values, index[..., None], numbers, (1, 1), mode=lax.GatherScatterMode.PROMISE_IN_BOUNDS
    )


def iota(shape, axis):
    return lax.broadcasted_iota(jnp.int32, shape, axis)


def spread(row, rows=ROWS):
    return jnp.broadcast_to(row, (rows, row.shape[-1]))


def codes_of(nodes, lane_offset, peer_ref, own_count, peer_count, window):
    pair = (iota(nodes.shape, 1) + lane_offset) >> 1
    own = nodes - pair * window
    ref = nodes - own_count
    sender = ref // LANES
    slot = jnp.zeros_like(ref)
    for p in range(1, peer_count):
        slot = jnp.where(sender == peer_ref[0, p], p, slot)
    return jnp.where(ref >= 0, window + slot * LANES + (ref & (LANES - 1)), own)


def vmem():
    return pl.BlockSpec(memory_space=pltpu.VMEM)


def smem():
    return pl.BlockSpec(memory_space=pltpu.SMEM)


def hbm():
    return pl.BlockSpec(memory_space=pltpu.HBM)


def call(body, name, in_specs, outs, stay, scratch=(), resident=(), grid=(), out_specs=None):
    kernel = pl.pallas_call(
        body,
        name=name,
        grid=grid,
        in_specs=in_specs,
        out_specs=out_specs or tuple(vmem() for _ in outs),
        out_shape=tuple(
            (pltpu.VMEM if k in stay else pltpu.HBM)(shape, dtype)
            for k, (shape, dtype) in enumerate(outs)
        ),
        scratch_shapes=list(scratch),
        compiler_params=pltpu.CompilerParams(vmem_limit_bytes=24 << 20),
    )

    def run(*operands):
        return kernel(
            *[
                pltpu.with_memory_space_constraint(operand, pltpu.VMEM if k in resident else pltpu.HBM)
                for k, operand in enumerate(operands)
            ]
        )

    return run


def element_sums(mass, region, density, stiff, squares):
    dens = jnp.where(region == 0, density[0], jnp.where(region == 1, density[1], density[2]))
    term = mass * dens
    total = term
    for d in range(3):
        high = stiff[d].astype(jnp.bfloat16)
        low = (stiff[d] - high.astype(jnp.float32)).astype(jnp.bfloat16)
        for weight, part in ((squares[0, d], high), (squares[0, d], low), (squares[1, d], high)):
            total = total + jnp.dot(weight, part, preferred_element_type=jnp.float32)
    return term, total


def ghost_diag_body(
    cfg, peer, density, nodes, stiff, mass, region, squares, shared, send, pos, peer_row, base, node_row
):
    lanes = iota((1, LANES), 1)
    row = jnp.zeros((1, LANES), jnp.int32)
    for p in range(cfg["peers"]):
        row = jnp.where(lanes == p, peer[0, p], row)
        base[p] = shared[p] & (-LANES)
        node_row[:, p * LANES : (p + 1) * LANES] = shared[p]
    peer_row[...] = row
    run = cfg["run"]
    _, edge = element_sums(mass[...], region[...], density, stiff, squares)
    code = codes_of(nodes[...], 0, peer, cfg["own"], cfg["peers"], cfg["window"])
    lane = iota(code.shape, 1)
    base = code - (cfg["window"] + run * (lane >> 1))
    place = iota(code.shape, 0) + LANES * (lane & 1)
    flat = iota((ROWS, LANES), 0) * LANES + iota((ROWS, LANES), 1)
    pair = (flat * cfg["magic"]) >> 16
    hop = flat - pair * run
    pair_lane = jnp.minimum(2 * pair, LANES - 1)
    got = jnp.zeros((ROWS, LANES), jnp.float32)
    where_at = jnp.zeros((ROWS, LANES), jnp.int32)
    for h in range(run):
        hit = base == h
        position = jnp.sum(jnp.where(hit, place, 0), axis=0, keepdims=True)
        value = jnp.sum(jnp.where(hit, edge, 0.0), axis=0, keepdims=True)
        position, value = spread(position), spread(value)
        position = position + pltpu.roll(position, LANES - 1, 1)
        value = value + pltpu.roll(value, LANES - 1, 1)
        got = jnp.where(hop == h, take(value, pair_lane), got)
        where_at = jnp.where(hop == h, take(position, pair_lane), where_at)
    pos[...] = where_at
    send[...] = jnp.zeros(send.shape, jnp.float32)
    for p in range(cfg["peers"]):
        send[peer[0, p]] = got[p : p + 1]


def tables_body(
    cfg, peer, density, nodes, stiff, mass, region, squares, base_s, node_row, right,
    idx, mt_edge, mt_inner, own_diag, right_at, diag_at, same,
    code_pad, value_pad, rows,
):
    code_pad[...] = jnp.full(code_pad.shape, NONE, jnp.int32)
    value_pad[...] = jnp.zeros(value_pad.shape, jnp.float32)

    def turned(ref):
        return jnp.concatenate([ref[:, :LANES].T, ref[:, LANES:].T], axis=0)

    for b in range(2):
        cols = slice(b * LANES, (b + 1) * LANES)
        code_pad[:NPE, cols] = codes_of(
            nodes[:, cols], b * LANES, peer, cfg["own"], cfg["peers"], cfg["window"]
        )
    idx[...] = turned(code_pad)
    term, diag = element_sums(mass[...], region[...], density, stiff, squares)
    value_pad[:NPE] = diag
    rows[...] = turned(value_pad)
    for g in range(0, cfg["pairs"], 2):
        lines = [
            spread(jnp.concatenate([rows[2 * k : 2 * k + 1, :], rows[2 * k + 1 : 2 * k + 2, :]], axis=1))
            for k in (g, g + 1)
        ]
        for k, sums in enumerate(scatter_pairs(lines, idx, g)):
            own_diag[g + k : g + k + 1, :] = sums[:1]
    pick(cfg, right, base_s, node_row, right_at)
    value_pad[:NPE] = term
    mt_edge[...] = value_pad[:, :LANES].T
    mt_inner[...] = value_pad[:, LANES:].T
    node = node_row[...]
    wide = node.shape[1]
    hot = jnp.where(iota((LANES, wide), 0) == (node & (LANES - 1)), 1.0, 0.0).astype(jnp.bfloat16)
    here = iota((LANES, wide), 0) == (node >> 7)
    at_slots = jnp.zeros((1, wide), jnp.float32)
    for part in reversed(parts_of(own_diag[...], 3)):
        seen = jnp.dot(part.astype(jnp.bfloat16), hot, preferred_element_type=jnp.float32)
        at_slots = at_slots + jnp.sum(jnp.where(here, seen, 0.0), axis=0, keepdims=True)
    diag_at[...] = spread(at_slots)
    for p in range(cfg["peers"]):
        column = jnp.broadcast_to(node[:, p * LANES : (p + 1) * LANES], (LANES, LANES)).T
        for q in range(cfg["peers"]):
            same[p * LANES : (p + 1) * LANES, q * LANES : (q + 1) * LANES] = jnp.where(
                column == node[:, q * LANES : (q + 1) * LANES], 1.0, 0.0
            ).astype(jnp.bfloat16)


def scatter_rows(rows, idx, g):
    node = iota((LANES, LANES), 0)
    spots = jnp.concatenate(
        [jnp.where(node == idx[2 * g + k : 2 * g + k + 1, :], 1.0, 0.0) for k in range(2)], axis=1
    ).astype(jnp.bfloat16)
    high = rows.astype(jnp.bfloat16).astype(jnp.float32)
    both = jnp.concatenate([high, rows - high], axis=0).astype(jnp.bfloat16)
    sums = lax.dot_general(both, spots, (((1,), (1,)), ((), ())), preferred_element_type=jnp.float32)
    return sums[:ROWS] + sums[ROWS:]


def scatter_pairs(rows, idx, g):
    node = iota((LANES, LANES), 0)
    spots = [
        jnp.concatenate(
            [jnp.where(node == idx[e : e + 1, :], 1.0, 0.0) for e in (2 * pair, 2 * pair + 1)], axis=1
        ).astype(jnp.bfloat16)
        for pair in (g, g + 1)
    ]
    parts = []
    for values in rows:
        high = values.astype(jnp.bfloat16).astype(jnp.float32)
        parts += [high, values - high]
    sums = nt_dot(jnp.concatenate(parts, axis=0).astype(jnp.bfloat16), jnp.concatenate(spots, axis=0))
    own = (sums[: 2 * ROWS, :LANES], sums[2 * ROWS :, LANES:])
    return [x[:ROWS] + x[ROWS:] for x in own]


def peers_of(cfg, peer_row):
    lane = iota((1, LANES), 1)
    return [jnp.max(jnp.where(lane == p, peer_row[...], 0)) for p in range(cfg["peers"])]


def pick(cfg, field, base_s, node_row, out):
    lane = iota((ROWS, LANES), 1)
    for p in range(cfg["peers"]):
        low = spread(node_row[:, p * LANES : (p + 1) * LANES] & (LANES - 1))
        got = jnp.zeros((ROWS, LANES), jnp.float32)
        for c in range(LANES):
            base = pl.multiple_of(base_s[p, 0, c], LANES)
            got = jnp.where(lane == c, take(field[:, pl.ds(base, LANES)], low), got)
        out[:, p * LANES : (p + 1) * LANES] = got


def nt_dot(left, right):
    return lax.dot_general(left, right, (((1,), (1,)), ((), ())), preferred_element_type=jnp.float32)


def parts_of(values, count):
    parts = []
    for _ in range(count):
        part = values.astype(jnp.bfloat16).astype(jnp.float32)
        parts.append(part)
        values = values - part
    return parts


def received_diag(cfg, peer, recv):
    return jnp.concatenate([recv[peer[p]] for p in range(cfg["peers"])], axis=1)


def received_rows(cfg, peer, recv):
    blocks = []
    for p in range(cfg["peers"]):
        first = peer[p] * (ROWS + 1)
        blocks.append(jnp.concatenate([recv[first + v] for v in range(ROWS)], axis=0))
    return jnp.concatenate(blocks, axis=1)


def put_slots(cfg, peer, values, out):
    for p in range(cfg["peers"]):
        out[peer[p]] = values[:, p * LANES : (p + 1) * LANES]


def start_body(cfg, peer_row, recv, right_at, diag_at, same, out, inverse_at):
    peer = peers_of(cfg, peer_row)
    got = spread(received_diag(cfg, peer, recv))
    top, middle, bottom = parts_of(got, 3)
    both = jnp.concatenate([top, middle], axis=0).astype(jnp.bfloat16)
    more = jnp.concatenate([bottom, bottom], axis=0).astype(jnp.bfloat16)
    first = nt_dot(both, same[...])
    total = diag_at[...] + (first[:ROWS] + (first[ROWS:] + nt_dot(more, same[...])[:ROWS]))
    inverse = 1.0 / total
    inverse_at[...] = inverse
    out[...] = jnp.zeros(out.shape, jnp.float32)
    put_slots(cfg, peer, right_at[...] * inverse, out)


def first_fields_body(
    cfg, peer_row, node_row, recv, own_diag, right, stiff_hbm, inverse, z, energy, st_edge, st_inner,
    stiff, value_pad, arrived,
):
    fetch = pltpu.make_async_copy(stiff_hbm, stiff, arrived)
    fetch.start()
    value_pad[...] = jnp.zeros(value_pad.shape, jnp.float32)
    peer = peers_of(cfg, peer_row)
    windows = cfg["pairs"]
    node, got = node_row[...], received_diag(cfg, peer, recv)
    here = iota((windows, got.shape[1]), 0) == (node >> 7)
    hot = jnp.where(iota((LANES, got.shape[1]), 0) == (node & (LANES - 1)), 1.0, 0.0).astype(jnp.bfloat16)
    total = own_diag[...]
    for part in parts_of(got, 3):
        total = total + nt_dot(jnp.where(here, spread(part, windows), 0.0).astype(jnp.bfloat16), hot)
    inverse[...] = 1.0 / total
    acc = jnp.zeros((ROWS, LANES), jnp.float32)
    for g in range(windows):
        cols = slice(g * LANES, (g + 1) * LANES)
        scaled = right[:, cols] * spread(inverse[g : g + 1, :])
        z[:, cols] = scaled
        acc = acc + right[:, cols] * scaled
    energy[...] = acc
    fetch.wait()
    for d in range(3):
        value_pad[:NPE] = stiff[d]
        cols = slice(d * LANES, (d + 1) * LANES)
        st_edge[:, cols] = value_pad[:, :LANES].T
        st_inner[:, cols] = value_pad[:, LANES:].T


def apply_rows(values, st, mt, weights1, weights2):
    count = values.shape[0] // ROWS

    def halves(x):
        high = x.astype(jnp.bfloat16)
        return jnp.concatenate([high, (x - high.astype(jnp.float32)).astype(jnp.bfloat16)], axis=1)

    both = jnp.dot(halves(values), weights1[...], preferred_element_type=jnp.float32)
    wide = 3 * LANES
    grad = (both[:, :wide] + both[:, wide:]).reshape(count, ROWS, wide)
    flux = (grad * st[:, None, :]).reshape(count * ROWS, wide)
    both = jnp.dot(halves(flux), weights2[...], preferred_element_type=jnp.float32)
    lumped = (values.reshape(count, ROWS, LANES) * mt[:, None, :]).reshape(count * ROWS, LANES)
    return both[:, :LANES] + both[:, LANES:] + lumped


def fill_weights(weights1, weights2, both1, both2):
    wide = 3 * LANES
    both1[:LANES] = weights1[...]
    both1[LANES:, :wide] = weights1[:, :wide]
    both1[LANES:, wide:] = jnp.zeros((LANES, wide), jnp.bfloat16)
    both2[:wide] = weights2[...]
    both2[wide:] = weights2[...]


CHUNK = 16


def apply_half(values, result, st, mt, weights1, weights2):
    acc = jnp.zeros((ROWS, LANES), jnp.float32)
    for c in range(values.shape[0] // (ROWS * CHUNK)):
        rows = slice(c * CHUNK * ROWS, (c + 1) * CHUNK * ROWS)
        elems = slice(c * CHUNK, (c + 1) * CHUNK)
        v = values[rows]
        r = apply_rows(v, st[elems], mt[elems], weights1, weights2)
        result[rows] = r
        acc = acc + jnp.sum((v * r).reshape(CHUNK, ROWS, LANES), axis=0)
    return acc


def scatter_half(edge, inner, idx, out):
    count = edge.shape[0] // (2 * ROWS)
    for g in range(idx.shape[0] // 2):
        half, e = (edge, 2 * g * ROWS) if g < count else (inner, 2 * (g - count) * ROWS)
        rows = jnp.concatenate([half[e : e + ROWS], half[e + ROWS : e + 2 * ROWS]], axis=1)
        out[:, g * LANES : (g + 1) * LANES] = scatter_rows(rows, idx, g)


def inner_body(cfg, z, idx, st, mt, w1, w2, result, curve, values, both1, both2):
    fill_weights(w1, w2, both1, both2)
    edge, pairs = cfg["edge_pairs"], cfg["pairs"]
    for g in range(edge, pairs):
        window = z[:, g * LANES : (g + 1) * LANES]
        for parity in range(2):
            e = 2 * g + parity
            at = (e - 2 * edge) * ROWS
            values[at : at + ROWS] = take(window, spread(idx[e : e + 1, :] & (LANES - 1)))
    curve[...] = apply_half(values, result, st, mt, both1, both2)


def edge_body(
    cfg, peer_row, recv, z, idx, st, mt, pos, w1, w2, energy, curve, result, out, values, ghosts, both1, both2
):
    peer = peers_of(cfg, peer_row)
    fill_weights(w1, w2, both1, both2)
    run, edge, peers = cfg["run"], cfg["edge_pairs"], cfg["peers"]
    for p in range(peers):
        ghosts[p] = recv[peer[p]]
    spans = []
    for g in range(edge):
        low, high = run * g // LANES, (run * (g + 1) - 1) // LANES
        spans.append((low, high))
        window = z[:, g * LANES : (g + 1) * LANES]
        for parity in range(2):
            e = 2 * g + parity
            code = spread(idx[e : e + 1, :])
            at = code & (LANES - 1)
            got = take(ghosts[low], at)
            if high > low:
                got = jnp.where(code < LANES * (high + 1), got, take(ghosts[high], at))
            values[e * ROWS : (e + 1) * ROWS] = jnp.where(code < LANES, take(window, at), got)
    acc = apply_half(values, result, st, mt, both1, both2) + curve[...]
    lane = iota((ROWS, LANES), 1)
    sums = [jnp.zeros((ROWS, LANES), jnp.float32) for _ in range(peers)]
    for g in range(edge):
        for p in range(spans[g][0], spans[g][1] + 1):
            place = spread(pos[p : p + 1, :])
            at = place & (LANES - 1)
            e = 2 * g * ROWS
            value = jnp.where(
                place < LANES, take(result[e : e + ROWS], at), take(result[e + ROWS : e + 2 * ROWS], at)
            )
            begin, end = run * g - p * LANES, run * (g + 1) - p * LANES
            sums[p] = jnp.where((lane >= begin) & (lane < end), value, sums[p])
    row = iota((ROWS, LANES), 0)
    dots = jnp.where(lane == row, jnp.sum(energy[...], axis=1, keepdims=True), 0.0)
    dots = jnp.where(lane == row + ROWS, jnp.sum(acc, axis=1, keepdims=True), dots)
    dots = jnp.sum(dots, axis=0, keepdims=True)
    out[...] = jnp.zeros(out.shape, jnp.float32)
    for n in range(out.shape[0] // (ROWS + 1)):
        out[n * (ROWS + 1) + ROWS] = dots
    for p in range(peers):
        for v in range(ROWS):
            out[peer[p] * (ROWS + 1) + v] = sums[p][v : v + 1]


def edge_scatter_body(cfg, result, idx, inner, out):
    scatter_half(result, inner, idx, out)


def edge_scatter_pick_body(cfg, base_s, node_row, result, idx, inner, out, at_slots):
    edge_scatter_body(cfg, result, idx, inner, out)
    pick(cfg, out, base_s, node_row, at_slots)


RETURN_STEP = 32


def returned_sums(cfg, peer, node_row, recv, left, hot):
    windows = cfg["pairs"]
    node, value = node_row[...], received_rows(cfg, peer, recv)
    wide = node.shape[1]
    high, low = parts_of(value, 2)
    lanes = jnp.where(iota((LANES, wide), 0) == (node & (LANES - 1)), 1.0, 0.0).astype(jnp.bfloat16)
    hot[:, :wide] = lanes
    hot[:, wide:] = lanes
    block = spread(node >> 7)
    for start in range(0, windows, RETURN_STEP):
        for g in range(start, start + RETURN_STEP, 2):
            rows = slice(g * ROWS, (g + 2) * ROWS)
            even, odd = block == g, block == g + 1
            left[rows, :wide] = jnp.concatenate(
                [jnp.where(even, high, 0.0), jnp.where(odd, high, 0.0)], axis=0
            ).astype(jnp.bfloat16)
            left[rows, wide:] = jnp.concatenate(
                [jnp.where(even, low, 0.0), jnp.where(odd, low, 0.0)], axis=0
            ).astype(jnp.bfloat16)
        yield start, nt_dot(left[start * ROWS : (start + RETURN_STEP) * ROWS], hot[...])


def dot_totals(recv):
    total = recv[ROWS]
    for n in range(1, recv.shape[0] // (ROWS + 1)):
        total = total + recv[n * (ROWS + 1) + ROWS]
    total = spread(total)
    lane, row = iota((ROWS, LANES), 1), iota((ROWS, LANES), 0)
    return [
        jnp.broadcast_to(
            jnp.sum(jnp.where(lane == row + k * ROWS, total, 0.0), axis=1, keepdims=True), (ROWS, LANES)
        )
        for k in range(2)
    ]


def step_body(cfg, peer_row, recv, right_at, inverse_at, image_at, same, out, coefs):
    peer = peers_of(cfg, peer_row)
    energy_now, curve_now = dot_totals(recv)
    alpha = energy_now / curve_now
    coefs[0] = alpha
    coefs[1] = energy_now
    both = jnp.concatenate(parts_of(received_rows(cfg, peer, recv), 2), axis=0).astype(jnp.bfloat16)
    got = nt_dot(both, same[...])
    image = image_at[...] + (got[:ROWS] + got[ROWS:])
    left_over = right_at[...] - spread_lanes(alpha, image.shape[1]) * image
    out[...] = jnp.zeros(out.shape, jnp.float32)
    put_slots(cfg, peer, left_over * inverse_at[...], out)


def spread_lanes(tile, wide):
    return jnp.concatenate([tile] * (wide // LANES), axis=1)


def window_sums(*operands):
    for start, sums in returned_sums(*operands):
        for k in range(RETURN_STEP):
            yield start + k, sums[k * ROWS : (k + 1) * ROWS]


def next_fields_body(
    cfg, peer_row, node_row, recv, own_hbm, right_hbm, inverse, coefs, w, z1, energy, left, hot, right, own, arrived
):
    fetches = [
        pltpu.make_async_copy(there, here, arrived.at[k]) for k, (there, here) in enumerate(((right_hbm, right), (own_hbm, own)))
    ]
    for fetch in fetches:
        fetch.start()
    peer = peers_of(cfg, peer_row)
    alpha = coefs[0]
    acc = jnp.zeros((ROWS, LANES), jnp.float32)
    for g, sums in window_sums(cfg, peer, node_row, recv, left, hot):
        if g == 0:
            for fetch in fetches:
                fetch.wait()
        cols = slice(g * LANES, (g + 1) * LANES)
        image = own[:, cols] + sums
        w[:, cols] = image
        left_over = right[:, cols] - alpha * image
        scaled = left_over * spread(inverse[g : g + 1, :])
        z1[:, cols] = scaled
        acc = acc + left_over * scaled
    energy[...] = acc


LAST_STEP = 32


def last_body(
    cfg, peer_row, node_row, recv, own, right_hbm, inverse, w_hbm, z1, coefs,
    solution_hbm, residual_hbm, left, hot, right, w, arrived, solution, residual, sent,
):
    fetches = [
        pltpu.make_async_copy(there, here, arrived.at[k]) for k, (there, here) in enumerate(((right_hbm, right), (w_hbm, w)))
    ]
    for fetch in fetches:
        fetch.start()
    peer = peers_of(cfg, peer_row)
    windows = cfg["pairs"]
    energy_next, curve_next = dot_totals(recv)
    alpha, energy_now = coefs[0], coefs[1]
    beta = energy_next / energy_now
    step = energy_next / (curve_next - beta * energy_next / alpha)
    copies = []
    for fetch in fetches:
        fetch.wait()
    for g, sums in window_sums(cfg, peer, node_row, recv, left, hot):
        cols = slice(g * LANES, (g + 1) * LANES)
        image = own[:, cols] + sums
        start, before = right[:, cols], w[:, cols]
        z0 = start * spread(inverse[g : g + 1, :])
        residual[:, cols] = (start - alpha * before) - step * (image + beta * before)
        solution[:, cols] = alpha * z0 + step * (z1[:, cols] + beta * z0)
        if (g + 1) % LAST_STEP == 0:
            done = slice((g + 1 - LAST_STEP) * LANES, (g + 1) * LANES)
            for k, (here, there) in enumerate(((solution, solution_hbm), (residual, residual_hbm))):
                copies.append(
                    pltpu.make_async_copy(here.at[:, done], there.at[:, done], sent.at[g // LAST_STEP, k])
                )
                copies[-1].start()
    for copy in copies:
        copy.wait()


def on_device(right_side, stiffness, mass, region, density, elem_nodes, peer_rank, send_nodes):
    vectors, own_count = right_side.shape
    elem_count = elem_nodes.shape[1]
    pairs = elem_count // 2
    edge_pairs = pairs // 2
    peers, slots = send_nodes.shape[1], send_nodes.shape[2]
    devices = lax.axis_size("dom")
    run = peers * slots // edge_pairs
    magic = (1 << 16) // run + 1
    flat = np.arange(ROWS * LANES)
    if (
        vectors != ROWS or own_count != pairs * LANES or slots != LANES or pairs != LANES
        or peers * slots != run * edge_pairs or peers > ROWS or run > LANES
        or ((flat * magic) >> 16 != flat // run).any()
    ):
        raise ValueError("unsupported sizes")
    cfg = dict(
        own=own_count, pairs=pairs, edge_pairs=edge_pairs, peers=peers, run=run, magic=magic,
        window=own_count // pairs,
    )
    f32, i32 = jnp.float32, jnp.int32
    weights1, weights2, squares = constant_operands()
    V, S = vmem(), smem()
    field = ((vectors, own_count), f32)
    tile = ((ROWS, LANES), f32)
    square = ((LANES, LANES), f32)
    half_rows = ((elem_count // 2 * ROWS, LANES), f32)

    def bind(body):
        return functools.partial(body, cfg)

    def exchange(values):
        return lax.all_to_all(values, "dom", split_axis=0, concat_axis=0, tiled=True)

    regions = region.reshape(1, elem_count)
    half_specs = [
        pl.BlockSpec((NPE, LANES), lambda _: (0, 0)),
        pl.BlockSpec((3, NPE, LANES), lambda _: (0, 0, 0)),
        pl.BlockSpec((NPE, LANES), lambda _: (0, 0)),
        pl.BlockSpec((1, LANES), lambda _: (0, 0)),
    ]
    shared = jnp.transpose(send_nodes, (1, 0, 2))
    send, pos, peer_row, base, node_row = call(
        bind(ghost_diag_body), "ghost_diag", [S, S, *half_specs, V, V],
        [
            ((devices, 1, LANES), f32), ((ROWS, LANES), i32), ((1, LANES), i32), ((peers, 1, slots), i32),
            ((1, peers * slots), i32),
        ],
        (1, 2, 4), grid=(1,),
    )(peer_rank, density, elem_nodes, stiffness, mass, regions, squares, shared)
    recv = exchange(send)
    slots_all = ((vectors, peers * slots), f32)
    edge_count = elem_count // 2
    idx, mt_edge, mt_inner, own_diag, right_at, diag_at, same = call(
        bind(tables_body), "tables", [S, S] + [V] * 5 + [S, V, V],
        [
            ((elem_count, LANES), i32),
            ((edge_count, LANES), f32), ((elem_count - edge_count, LANES), f32),
            square, slots_all, slots_all, ((peers * slots, peers * slots), jnp.bfloat16),
        ],
        (0, 1, 3, 4, 5, 6),
        [
            pltpu.VMEM((LANES, elem_count), i32), pltpu.VMEM((LANES, elem_count), f32),
            pltpu.VMEM((elem_count, LANES), f32),
        ],
        (8,),
    )(peer_rank, density, elem_nodes, stiffness, mass, regions, squares, base, node_row, right_side)

    send_shape = ((devices, ROWS, LANES), f32)
    send, inverse_at = call(
        bind(start_body), "start", [V] * 5, [send_shape, slots_all], (1,), (), range(5)
    )(peer_row, recv, right_at, diag_at, same)
    diag_recv = recv
    recv = exchange(send)
    inverse, z, energy, st_edge, st_inner = call(
        bind(first_fields_body), "first_fields", [V] * 5 + [hbm()],
        [
            square, field, tile, ((edge_count, 3 * LANES), f32), ((elem_count - edge_count, 3 * LANES), f32),
        ],
        range(4),
        [
            pltpu.VMEM(stiffness.shape, f32), pltpu.VMEM((LANES, elem_count), f32),
            pltpu.SemaphoreType.DMA(()),
        ],
        range(5),
    )(peer_row, node_row, diag_recv, own_diag, right_side, stiffness)

    weight_rows = [
        pltpu.VMEM((2 * LANES, 6 * LANES), jnp.bfloat16), pltpu.VMEM((6 * LANES, 2 * LANES), jnp.bfloat16)
    ]

    def inner_part(z):
        return call(
            bind(inner_body), "inner", [V] * 6, [half_rows, tile], range(2),
            [pltpu.VMEM(*half_rows), *weight_rows], (0, 1, 4, 5),
        )(z, idx, st_inner, mt_inner, weights1, weights2)

    def edge_part(recv, z, energy, curve):
        return call(
            bind(edge_body), "edge", [V] * 11,
            [half_rows, ((devices * (ROWS + 1), 1, LANES), f32)], (0,),
            [pltpu.VMEM(*half_rows), pltpu.VMEM((peers, ROWS, LANES), f32), *weight_rows], range(11),
        )(peer_row, recv, z, idx, st_edge, mt_edge, pos, weights1, weights2, energy, curve)

    wide = 2 * peers * slots
    scratch = [
        pltpu.VMEM((vectors * pairs, wide), jnp.bfloat16), pltpu.VMEM((LANES, wide), jnp.bfloat16),
        pltpu.VMEM(*field), pltpu.VMEM(*field),
        pltpu.SemaphoreType.DMA((2,)),
    ]
    inner, curve = inner_part(z)
    result, send = edge_part(recv, z, energy, curve)
    recv = exchange(send)
    own, image_at = call(
        bind(edge_scatter_pick_body), "edge_scatter_pick", [S] + [V] * 4, [field, slots_all], (1,), (),
        (1, 2, 3, 4),
    )(base, node_row, result, idx, inner)
    send, coefs = call(
        bind(step_body), "step", [V] * 6, [send_shape, ((2, ROWS, LANES), f32)], (1,), (),
        range(6),
    )(peer_row, recv, right_at, inverse_at, image_at, same)
    sum_recv = recv
    recv = exchange(send)
    w, z, energy = call(
        bind(next_fields_body), "next_fields", [V] * 3 + [hbm(), hbm()] + [V] * 2, [field, field, tile], (1, 2), scratch,
        (0, 1, 2, 5, 6),
    )(peer_row, node_row, sum_recv, own, right_side, inverse, coefs)
    inner, curve = inner_part(z)
    result, send = edge_part(recv, z, energy, curve)
    recv = exchange(send)
    (own,) = call(bind(edge_scatter_body), "edge_scatter", [V] * 3, [field], (0,), (), range(3))(
        result, idx, inner
    )
    return call(
        bind(last_body), "last", [V] * 4 + [hbm(), V, hbm()] + [V] * 2, [field, field], (),
        scratch + [
            pltpu.VMEM(*field), pltpu.VMEM(*field), pltpu.SemaphoreType.DMA((pairs // LAST_STEP, 2)),
        ],
        (0, 1, 2, 3, 5, 7, 8), out_specs=(hbm(), hbm()),
    )(peer_row, node_row, recv, own, right_side, inverse, w, z, coefs)


def solution(mesh):
    placed = (
        P(None, "dom"),
        P(None, None, "dom"),
        P(None, "dom"),
        P("dom"),
        P(),
        P(None, "dom"),
        P("dom", None),
        P("dom", None, None),
    )
    return jax.shard_map(
        on_device,
        mesh=mesh,
        in_specs=placed,
        out_specs=(P(None, "dom"), P(None, "dom")),
        check_vma=False,
    )
```

```python
import functools

import jax
import jax.numpy as jnp
import numpy as np
from jax import lax
from jax.experimental import pallas as pl
from jax.experimental.pallas import tpu as pltpu
from jax.sharding import PartitionSpec as P

ITERS = 2
LANES = 128
ROWS = 8
NONE = 255
SIDE = 5
NPE = SIDE**3


def gll_matrix():
    points = np.array([-1.0, -np.sqrt(3.0 / 7.0), 0.0, np.sqrt(3.0 / 7.0), 1.0])
    weights = np.array(
        [
            1.0 / np.prod([points[column] - points[other] for other in range(5) if other != column])
            for column in range(5)
        ]
    )
    matrix = np.zeros((5, 5))
    for row_index in range(5):
        for column in range(5):
            if row_index != column:
                matrix[row_index, column] = (
                    weights[column] / weights[row_index] / (points[row_index] - points[column])
                )
        matrix[row_index, row_index] = -np.sum(matrix[row_index])
    return matrix


def direction_matrices():
    base = np.asarray(gll_matrix(), np.float32)
    eye = np.eye(SIDE, dtype=np.float32)
    return [
        np.einsum("ai,bj,ck->abcijk", *factors).reshape(NPE, NPE)
        for factors in ((base, eye, eye), (eye, base, eye), (eye, eye, base))
    ]


def split_np(values):
    high = values.astype(jnp.bfloat16)
    low = (values - high.astype(np.float32)).astype(jnp.bfloat16)
    return high, low


def constant_operands():
    mats = direction_matrices()
    grad = np.zeros((LANES, 3 * LANES), np.float32)
    for d in range(3):
        grad[:NPE, d * LANES : d * LANES + NPE] = mats[d].T
    high, low = split_np(grad)
    first = np.concatenate([high, low], axis=1)
    second = np.concatenate([high.T, low.T], axis=1)
    squares = np.stack(split_np(np.stack([m.T * m.T for m in mats])))
    return jnp.asarray(first), jnp.asarray(second), jnp.asarray(squares)


def take(values, index):
    numbers = lax.GatherDimensionNumbers(
        offset_dims=(),
        collapsed_slice_dims=(1,),
        start_index_map=(1,),
        operand_batching_dims=(0,),
        start_indices_batching_dims=(0,),
    )
    return lax.gather(
        values, index[..., None], numbers, (1, 1), mode=lax.GatherScatterMode.PROMISE_IN_BOUNDS
    )


def iota(shape, axis):
    return lax.broadcasted_iota(jnp.int32, shape, axis)


def spread(row, rows=ROWS):
    return jnp.broadcast_to(row, (rows, row.shape[-1]))


def codes_of(nodes, lane_offset, peer_ref, own_count, peer_count, window):
    pair = (iota(nodes.shape, 1) + lane_offset) >> 1
    own = nodes - pair * window
    ref = nodes - own_count
    sender = ref // LANES
    slot = jnp.zeros_like(ref)
    for p in range(1, peer_count):
        slot = jnp.where(sender == peer_ref[0, p], p, slot)
    return jnp.where(ref >= 0, window + slot * LANES + (ref & (LANES - 1)), own)


def vmem():
    return pl.BlockSpec(memory_space=pltpu.VMEM)


def smem():
    return pl.BlockSpec(memory_space=pltpu.SMEM)


def hbm():
    return pl.BlockSpec(memory_space=pltpu.HBM)


def call(body, name, in_specs, outs, stay, scratch=(), resident=(), grid=(), out_specs=None):
    kernel = pl.pallas_call(
        body,
        name=name,
        grid=grid,
        in_specs=in_specs,
        out_specs=out_specs or tuple(vmem() for _ in outs),
        out_shape=tuple(
            (pltpu.VMEM if k in stay else pltpu.HBM)(shape, dtype)
            for k, (shape, dtype) in enumerate(outs)
        ),
        scratch_shapes=list(scratch),
        compiler_params=pltpu.CompilerParams(vmem_limit_bytes=24 << 20),
    )

    def run(*operands):
        return kernel(
            *[
                pltpu.with_memory_space_constraint(operand, pltpu.VMEM if k in resident else pltpu.HBM)
                for k, operand in enumerate(operands)
            ]
        )

    return run


def element_sums(mass, region, density, stiff, squares):
    dens = jnp.where(region == 0, density[0], jnp.where(region == 1, density[1], density[2]))
    term = mass * dens
    total = term
    for d in range(3):
        high = stiff[d].astype(jnp.bfloat16)
        low = (stiff[d] - high.astype(jnp.float32)).astype(jnp.bfloat16)
        for weight, part in ((squares[0, d], high), (squares[0, d], low), (squares[1, d], high)):
            total = total + jnp.dot(weight, part, preferred_element_type=jnp.float32)
    return term, total


def ghost_diag_body(
    cfg, peer, density, nodes, stiff, mass, region, squares, shared, send, pos, peer_row, base, node_row
):
    lanes = iota((1, LANES), 1)
    row = jnp.zeros((1, LANES), jnp.int32)
    for p in range(cfg["peers"]):
        row = jnp.where(lanes == p, peer[0, p], row)
        base[p] = shared[p] & (-LANES)
        node_row[:, p * LANES : (p + 1) * LANES] = shared[p]
    peer_row[...] = row
    run = cfg["run"]
    _, edge = element_sums(mass[...], region[...], density, stiff, squares)
    code = codes_of(nodes[...], 0, peer, cfg["own"], cfg["peers"], cfg["window"])
    lane = iota(code.shape, 1)
    base = code - (cfg["window"] + run * (lane >> 1))
    place = iota(code.shape, 0) + LANES * (lane & 1)
    flat = iota((ROWS, LANES), 0) * LANES + iota((ROWS, LANES), 1)
    pair = (flat * cfg["magic"]) >> 16
    hop = flat - pair * run
    pair_lane = jnp.minimum(2 * pair, LANES - 1)
    got = jnp.zeros((ROWS, LANES), jnp.float32)
    where_at = jnp.zeros((ROWS, LANES), jnp.int32)
    for h in range(run):
        hit = base == h
        position = jnp.sum(jnp.where(hit, place, 0), axis=0, keepdims=True)
        value = jnp.sum(jnp.where(hit, edge, 0.0), axis=0, keepdims=True)
        position, value = spread(position), spread(value)
        position = position + pltpu.roll(position, LANES - 1, 1)
        value = value + pltpu.roll(value, LANES - 1, 1)
        got = jnp.where(hop == h, take(value, pair_lane), got)
        where_at = jnp.where(hop == h, take(position, pair_lane), where_at)
    pos[...] = where_at
    send[...] = jnp.zeros(send.shape, jnp.float32)
    for p in range(cfg["peers"]):
        send[peer[0, p]] = got[p : p + 1]


def tables_body(
    cfg, peer, density, nodes, stiff, mass, region, squares, base_s, node_row, right,
    idx, st_edge, mt_edge, st_inner, mt_inner, own_diag, right_at, diag_at, same,
    code_pad, value_pad, rows,
):
    code_pad[...] = jnp.full(code_pad.shape, NONE, jnp.int32)
    value_pad[...] = jnp.zeros(value_pad.shape, jnp.float32)

    def turned(ref):
        return jnp.concatenate([ref[:, :LANES].T, ref[:, LANES:].T], axis=0)

    for b in range(2):
        cols = slice(b * LANES, (b + 1) * LANES)
        code_pad[:NPE, cols] = codes_of(
            nodes[:, cols], b * LANES, peer, cfg["own"], cfg["peers"], cfg["window"]
        )
    idx[...] = turned(code_pad)
    term, diag = element_sums(mass[...], region[...], density, stiff, squares)
    value_pad[:NPE] = diag
    rows[...] = turned(value_pad)
    for g in range(0, cfg["pairs"], 2):
        lines = [
            spread(jnp.concatenate([rows[2 * k : 2 * k + 1, :], rows[2 * k + 1 : 2 * k + 2, :]], axis=1))
            for k in (g, g + 1)
        ]
        for k, sums in enumerate(scatter_pairs(lines, idx, g)):
            own_diag[g + k : g + k + 1, :] = sums[:1]
    pick(cfg, right, base_s, node_row, right_at)
    for d in range(3):
        value_pad[:NPE] = stiff[d]
        cols = slice(d * LANES, (d + 1) * LANES)
        st_edge[:, cols] = value_pad[:, :LANES].T
        st_inner[:, cols] = value_pad[:, LANES:].T
    value_pad[:NPE] = term
    mt_edge[...] = value_pad[:, :LANES].T
    mt_inner[...] = value_pad[:, LANES:].T
    node = node_row[...]
    wide = node.shape[1]
    hot = jnp.where(iota((LANES, wide), 0) == (node & (LANES - 1)), 1.0, 0.0).astype(jnp.bfloat16)
    here = iota((LANES, wide), 0) == (node >> 7)
    at_slots = jnp.zeros((1, wide), jnp.float32)
    for part in reversed(parts_of(own_diag[...], 3)):
        seen = jnp.dot(part.astype(jnp.bfloat16), hot, preferred_element_type=jnp.float32)
        at_slots = at_slots + jnp.sum(jnp.where(here, seen, 0.0), axis=0, keepdims=True)
    diag_at[...] = spread(at_slots)
    for p in range(cfg["peers"]):
        column = jnp.broadcast_to(node[:, p * LANES : (p + 1) * LANES], (LANES, LANES)).T
        for q in range(cfg["peers"]):
            same[p * LANES : (p + 1) * LANES, q * LANES : (q + 1) * LANES] = jnp.where(
                column == node[:, q * LANES : (q + 1) * LANES], 1.0, 0.0
            ).astype(jnp.bfloat16)


def scatter_rows(rows, idx, g):
    node = iota((LANES, LANES), 0)
    spots = jnp.concatenate(
        [jnp.where(node == idx[2 * g + k : 2 * g + k + 1, :], 1.0, 0.0) for k in range(2)], axis=1
    ).astype(jnp.bfloat16)
    high = rows.astype(jnp.bfloat16).astype(jnp.float32)
    both = jnp.concatenate([high, rows - high], axis=0).astype(jnp.bfloat16)
    sums = lax.dot_general(both, spots, (((1,), (1,)), ((), ())), preferred_element_type=jnp.float32)
    return sums[:ROWS] + sums[ROWS:]


def scatter_pairs(rows, idx, g):
    node = iota((LANES, LANES), 0)
    spots = [
        jnp.concatenate(
            [jnp.where(node == idx[e : e + 1, :], 1.0, 0.0) for e in (2 * pair, 2 * pair + 1)], axis=1
        ).astype(jnp.bfloat16)
        for pair in (g, g + 1)
    ]
    parts = []
    for values in rows:
        high = values.astype(jnp.bfloat16).astype(jnp.float32)
        parts += [high, values - high]
    sums = nt_dot(jnp.concatenate(parts, axis=0).astype(jnp.bfloat16), jnp.concatenate(spots, axis=0))
    own = (sums[: 2 * ROWS, :LANES], sums[2 * ROWS :, LANES:])
    return [x[:ROWS] + x[ROWS:] for x in own]


def peers_of(cfg, peer_row):
    lane = iota((1, LANES), 1)
    return [jnp.max(jnp.where(lane == p, peer_row[...], 0)) for p in range(cfg["peers"])]


def pick(cfg, field, base_s, node_row, out):
    lane = iota((ROWS, LANES), 1)
    for p in range(cfg["peers"]):
        low = spread(node_row[:, p * LANES : (p + 1) * LANES] & (LANES - 1))
        got = jnp.zeros((ROWS, LANES), jnp.float32)
        for c in range(LANES):
            base = pl.multiple_of(base_s[p, 0, c], LANES)
            got = jnp.where(lane == c, take(field[:, pl.ds(base, LANES)], low), got)
        out[:, p * LANES : (p + 1) * LANES] = got


def nt_dot(left, right):
    return lax.dot_general(left, right, (((1,), (1,)), ((), ())), preferred_element_type=jnp.float32)


def parts_of(values, count):
    parts = []
    for _ in range(count):
        part = values.astype(jnp.bfloat16).astype(jnp.float32)
        parts.append(part)
        values = values - part
    return parts


def received_diag(cfg, peer, recv):
    return jnp.concatenate([recv[peer[p]] for p in range(cfg["peers"])], axis=1)


def received_rows(cfg, peer, recv):
    blocks = []
    for p in range(cfg["peers"]):
        first = peer[p] * (ROWS + 1)
        blocks.append(jnp.concatenate([recv[first + v] for v in range(ROWS)], axis=0))
    return jnp.concatenate(blocks, axis=1)


def put_slots(cfg, peer, values, out):
    for p in range(cfg["peers"]):
        out[peer[p]] = values[:, p * LANES : (p + 1) * LANES]


def start_body(cfg, peer_row, recv, right_at, diag_at, same, out, inverse_at):
    peer = peers_of(cfg, peer_row)
    got = spread(received_diag(cfg, peer, recv))
    top, middle, bottom = parts_of(got, 3)
    both = jnp.concatenate([top, middle], axis=0).astype(jnp.bfloat16)
    more = jnp.concatenate([bottom, bottom], axis=0).astype(jnp.bfloat16)
    first = nt_dot(both, same[...])
    total = diag_at[...] + (first[:ROWS] + (first[ROWS:] + nt_dot(more, same[...])[:ROWS]))
    inverse = 1.0 / total
    inverse_at[...] = inverse
    out[...] = jnp.zeros(out.shape, jnp.float32)
    put_slots(cfg, peer, right_at[...] * inverse, out)


def first_fields_body(cfg, peer_row, node_row, recv, own_diag, right, inverse, z, energy):
    peer = peers_of(cfg, peer_row)
    windows = cfg["pairs"]
    node, got = node_row[...], received_diag(cfg, peer, recv)
    here = iota((windows, got.shape[1]), 0) == (node >> 7)
    hot = jnp.where(iota((LANES, got.shape[1]), 0) == (node & (LANES - 1)), 1.0, 0.0).astype(jnp.bfloat16)
    total = own_diag[...]
    for part in parts_of(got, 3):
        total = total + nt_dot(jnp.where(here, spread(part, windows), 0.0).astype(jnp.bfloat16), hot)
    inverse[...] = 1.0 / total
    acc = jnp.zeros((ROWS, LANES), jnp.float32)
    for g in range(windows):
        cols = slice(g * LANES, (g + 1) * LANES)
        scaled = right[:, cols] * spread(inverse[g : g + 1, :])
        z[:, cols] = scaled
        acc = acc + right[:, cols] * scaled
    energy[...] = acc


def apply_rows(values, st, mt, weights1, weights2):
    count = values.shape[0] // ROWS

    def halves(x):
        high = x.astype(jnp.bfloat16)
        return jnp.concatenate([high, (x - high.astype(jnp.float32)).astype(jnp.bfloat16)], axis=1)

    both = jnp.dot(halves(values), weights1[...], preferred_element_type=jnp.float32)
    wide = 3 * LANES
    grad = (both[:, :wide] + both[:, wide:]).reshape(count, ROWS, wide)
    flux = (grad * st[:, None, :]).reshape(count * ROWS, wide)
    both = jnp.dot(halves(flux), weights2[...], preferred_element_type=jnp.float32)
    lumped = (values.reshape(count, ROWS, LANES) * mt[:, None, :]).reshape(count * ROWS, LANES)
    return both[:, :LANES] + both[:, LANES:] + lumped


def fill_weights(weights1, weights2, both1, both2):
    wide = 3 * LANES
    both1[:LANES] = weights1[...]
    both1[LANES:, :wide] = weights1[:, :wide]
    both1[LANES:, wide:] = jnp.zeros((LANES, wide), jnp.bfloat16)
    both2[:wide] = weights2[...]
    both2[wide:] = weights2[...]


CHUNK = 16


def apply_half(values, result, st, mt, weights1, weights2):
    acc = jnp.zeros((ROWS, LANES), jnp.float32)
    for c in range(values.shape[0] // (ROWS * CHUNK)):
        rows = slice(c * CHUNK * ROWS, (c + 1) * CHUNK * ROWS)
        elems = slice(c * CHUNK, (c + 1) * CHUNK)
        v = values[rows]
        r = apply_rows(v, st[elems], mt[elems], weights1, weights2)
        result[rows] = r
        acc = acc + jnp.sum((v * r).reshape(CHUNK, ROWS, LANES), axis=0)
    return acc


def scatter_half(edge, inner, idx, out):
    count = edge.shape[0] // (2 * ROWS)
    for g in range(idx.shape[0] // 2):
        half, e = (edge, 2 * g * ROWS) if g < count else (inner, 2 * (g - count) * ROWS)
        rows = jnp.concatenate([half[e : e + ROWS], half[e + ROWS : e + 2 * ROWS]], axis=1)
        out[:, g * LANES : (g + 1) * LANES] = scatter_rows(rows, idx, g)


def inner_body(cfg, z, idx, st, mt, w1, w2, result, curve, values, both1, both2):
    fill_weights(w1, w2, both1, both2)
    edge, pairs = cfg["edge_pairs"], cfg["pairs"]
    for g in range(edge, pairs):
        window = z[:, g * LANES : (g + 1) * LANES]
        for parity in range(2):
            e = 2 * g + parity
            at = (e - 2 * edge) * ROWS
            values[at : at + ROWS] = take(window, spread(idx[e : e + 1, :] & (LANES - 1)))
    curve[...] = apply_half(values, result, st, mt, both1, both2)


def edge_body(
    cfg, peer_row, recv, z, idx, st, mt, pos, w1, w2, energy, curve, result, out, values, ghosts, both1, both2
):
    peer = peers_of(cfg, peer_row)
    fill_weights(w1, w2, both1, both2)
    run, edge, peers = cfg["run"], cfg["edge_pairs"], cfg["peers"]
    for p in range(peers):
        ghosts[p] = recv[peer[p]]
    spans = []
    for g in range(edge):
        low, high = run * g // LANES, (run * (g + 1) - 1) // LANES
        spans.append((low, high))
        window = z[:, g * LANES : (g + 1) * LANES]
        for parity in range(2):
            e = 2 * g + parity
            code = spread(idx[e : e + 1, :])
            at = code & (LANES - 1)
            got = take(ghosts[low], at)
            if high > low:
                got = jnp.where(code < LANES * (high + 1), got, take(ghosts[high], at))
            values[e * ROWS : (e + 1) * ROWS] = jnp.where(code < LANES, take(window, at), got)
    acc = apply_half(values, result, st, mt, both1, both2) + curve[...]
    lane = iota((ROWS, LANES), 1)
    sums = [jnp.zeros((ROWS, LANES), jnp.float32) for _ in range(peers)]
    for g in range(edge):
        for p in range(spans[g][0], spans[g][1] + 1):
            place = spread(pos[p : p + 1, :])
            at = place & (LANES - 1)
            e = 2 * g * ROWS
            value = jnp.where(
                place < LANES, take(result[e : e + ROWS], at), take(result[e + ROWS : e + 2 * ROWS], at)
            )
            begin, end = run * g - p * LANES, run * (g + 1) - p * LANES
            sums[p] = jnp.where((lane >= begin) & (lane < end), value, sums[p])
    row = iota((ROWS, LANES), 0)
    dots = jnp.where(lane == row, jnp.sum(energy[...], axis=1, keepdims=True), 0.0)
    dots = jnp.where(lane == row + ROWS, jnp.sum(acc, axis=1, keepdims=True), dots)
    dots = jnp.sum(dots, axis=0, keepdims=True)
    out[...] = jnp.zeros(out.shape, jnp.float32)
    for n in range(out.shape[0] // (ROWS + 1)):
        out[n * (ROWS + 1) + ROWS] = dots
    for p in range(peers):
        for v in range(ROWS):
            out[peer[p] * (ROWS + 1) + v] = sums[p][v : v + 1]


def edge_scatter_body(cfg, result, idx, inner, out):
    scatter_half(result, inner, idx, out)


def edge_scatter_pick_body(cfg, base_s, node_row, result, idx, inner, out, at_slots):
    edge_scatter_body(cfg, result, idx, inner, out)
    pick(cfg, out, base_s, node_row, at_slots)


RETURN_STEP = 32


def returned_sums(cfg, peer, node_row, recv, left, hot, step):
    windows = cfg["pairs"]
    node, value = node_row[...], received_rows(cfg, peer, recv)
    wide = node.shape[1]
    high, low = parts_of(value, 2)
    lanes = jnp.where(iota((LANES, wide), 0) == (node & (LANES - 1)), 1.0, 0.0).astype(jnp.bfloat16)
    hot[:, :wide] = lanes
    hot[:, wide:] = lanes
    block = spread(node >> 7)
    for start in range(0, windows, step):
        for g in range(start, start + step, 2):
            rows = slice(g * ROWS, (g + 2) * ROWS)
            even, odd = block == g, block == g + 1
            left[rows, :wide] = jnp.concatenate(
                [jnp.where(even, high, 0.0), jnp.where(odd, high, 0.0)], axis=0
            ).astype(jnp.bfloat16)
            left[rows, wide:] = jnp.concatenate(
                [jnp.where(even, low, 0.0), jnp.where(odd, low, 0.0)], axis=0
            ).astype(jnp.bfloat16)
        yield start, nt_dot(left[start * ROWS : (start + step) * ROWS], hot[...])


def dot_totals(recv):
    total = recv[ROWS]
    for n in range(1, recv.shape[0] // (ROWS + 1)):
        total = total + recv[n * (ROWS + 1) + ROWS]
    total = spread(total)
    lane, row = iota((ROWS, LANES), 1), iota((ROWS, LANES), 0)
    return [
        jnp.broadcast_to(
            jnp.sum(jnp.where(lane == row + k * ROWS, total, 0.0), axis=1, keepdims=True), (ROWS, LANES)
        )
        for k in range(2)
    ]


def step_body(cfg, peer_row, recv, right_at, inverse_at, image_at, same, out, coefs):
    peer = peers_of(cfg, peer_row)
    energy_now, curve_now = dot_totals(recv)
    alpha = energy_now / curve_now
    coefs[0] = alpha
    coefs[1] = energy_now
    both = jnp.concatenate(parts_of(received_rows(cfg, peer, recv), 2), axis=0).astype(jnp.bfloat16)
    got = nt_dot(both, same[...])
    image = image_at[...] + (got[:ROWS] + got[ROWS:])
    left_over = right_at[...] - spread_lanes(alpha, image.shape[1]) * image
    out[...] = jnp.zeros(out.shape, jnp.float32)
    put_slots(cfg, peer, left_over * inverse_at[...], out)


def spread_lanes(tile, wide):
    return jnp.concatenate([tile] * (wide // LANES), axis=1)


def window_sums(*operands, step):
    for start, sums in returned_sums(*operands, step):
        for k in range(step):
            yield start + k, sums[k * ROWS : (k + 1) * ROWS]


def next_fields_body(
    cfg, peer_row, node_row, recv, own_hbm, right_hbm, inverse, coefs, w, z1, energy, left, hot, right, own, arrived
):
    fetches = [
        pltpu.make_async_copy(there, here, arrived.at[k]) for k, (there, here) in enumerate(((right_hbm, right), (own_hbm, own)))
    ]
    for fetch in fetches:
        fetch.start()
    peer = peers_of(cfg, peer_row)
    alpha = coefs[0]
    acc = jnp.zeros((ROWS, LANES), jnp.float32)
    for g, sums in window_sums(cfg, peer, node_row, recv, left, hot, step=cfg["pairs"]):
        if g == 0:
            for fetch in fetches:
                fetch.wait()
        cols = slice(g * LANES, (g + 1) * LANES)
        image = own[:, cols] + sums
        w[:, cols] = image
        left_over = right[:, cols] - alpha * image
        scaled = left_over * spread(inverse[g : g + 1, :])
        z1[:, cols] = scaled
        acc = acc + left_over * scaled
    energy[...] = acc


LAST_STEP = 32


def last_body(
    cfg, peer_row, node_row, recv, own, right_hbm, inverse, w_hbm, z1, coefs,
    solution_hbm, residual_hbm, left, hot, right, w, arrived, solution, residual, sent,
):
    fetches = [
        pltpu.make_async_copy(there, here, arrived.at[k]) for k, (there, here) in enumerate(((right_hbm, right), (w_hbm, w)))
    ]
    for fetch in fetches:
        fetch.start()
    peer = peers_of(cfg, peer_row)
    windows = cfg["pairs"]
    energy_next, curve_next = dot_totals(recv)
    alpha, energy_now = coefs[0], coefs[1]
    beta = energy_next / energy_now
    step = energy_next / (curve_next - beta * energy_next / alpha)
    copies = []
    for fetch in fetches:
        fetch.wait()
    for g, sums in window_sums(cfg, peer, node_row, recv, left, hot, step=RETURN_STEP):
        cols = slice(g * LANES, (g + 1) * LANES)
        image = own[:, cols] + sums
        start, before = right[:, cols], w[:, cols]
        z0 = start * spread(inverse[g : g + 1, :])
        residual[:, cols] = (start - alpha * before) - step * (image + beta * before)
        solution[:, cols] = alpha * z0 + step * (z1[:, cols] + beta * z0)
        if (g + 1) % LAST_STEP == 0:
            done = slice((g + 1 - LAST_STEP) * LANES, (g + 1) * LANES)
            for k, (here, there) in enumerate(((solution, solution_hbm), (residual, residual_hbm))):
                copies.append(
                    pltpu.make_async_copy(here.at[:, done], there.at[:, done], sent.at[g // LAST_STEP, k])
                )
                copies[-1].start()
    for copy in copies:
        copy.wait()


def on_device(right_side, stiffness, mass, region, density, elem_nodes, peer_rank, send_nodes):
    vectors, own_count = right_side.shape
    elem_count = elem_nodes.shape[1]
    pairs = elem_count // 2
    edge_pairs = pairs // 2
    peers, slots = send_nodes.shape[1], send_nodes.shape[2]
    devices = lax.axis_size("dom")
    run = peers * slots // edge_pairs
    magic = (1 << 16) // run + 1
    flat = np.arange(ROWS * LANES)
    if (
        vectors != ROWS or own_count != pairs * LANES or slots != LANES or pairs != LANES
        or peers * slots != run * edge_pairs or peers > ROWS or run > LANES
        or ((flat * magic) >> 16 != flat // run).any()
    ):
        raise ValueError("unsupported sizes")
    cfg = dict(
        own=own_count, pairs=pairs, edge_pairs=edge_pairs, peers=peers, run=run, magic=magic,
        window=own_count // pairs,
    )
    f32, i32 = jnp.float32, jnp.int32
    weights1, weights2, squares = constant_operands()
    V, S = vmem(), smem()
    field = ((vectors, own_count), f32)
    tile = ((ROWS, LANES), f32)
    square = ((LANES, LANES), f32)
    half_rows = ((elem_count // 2 * ROWS, LANES), f32)

    def bind(body):
        return functools.partial(body, cfg)

    def exchange(values):
        return lax.all_to_all(values, "dom", split_axis=0, concat_axis=0, tiled=True)

    regions = region.reshape(1, elem_count)
    half_specs = [
        pl.BlockSpec((NPE, LANES), lambda _: (0, 0)),
        pl.BlockSpec((3, NPE, LANES), lambda _: (0, 0, 0)),
        pl.BlockSpec((NPE, LANES), lambda _: (0, 0)),
        pl.BlockSpec((1, LANES), lambda _: (0, 0)),
    ]
    shared = jnp.transpose(send_nodes, (1, 0, 2))
    send, pos, peer_row, base, node_row = call(
        bind(ghost_diag_body), "ghost_diag", [S, S, *half_specs, V, V],
        [
            ((devices, 1, LANES), f32), ((ROWS, LANES), i32), ((1, LANES), i32), ((peers, 1, slots), i32),
            ((1, peers * slots), i32),
        ],
        (1, 2, 4), grid=(1,),
    )(peer_rank, density, elem_nodes, stiffness, mass, regions, squares, shared)
    recv = exchange(send)
    slots_all = ((vectors, peers * slots), f32)
    edge_count = elem_count // 2
    idx, st_edge, mt_edge, st_inner, mt_inner, own_diag, right_at, diag_at, same = call(
        bind(tables_body), "tables", [S, S] + [V] * 5 + [S, V, V],
        [
            ((elem_count, LANES), i32),
            ((edge_count, 3 * LANES), f32), ((edge_count, LANES), f32),
            ((elem_count - edge_count, 3 * LANES), f32), ((elem_count - edge_count, LANES), f32),
            square, slots_all, slots_all, ((peers * slots, peers * slots), jnp.bfloat16),
        ],
        (0, 1, 2, 5, 6, 7, 8),
        [
            pltpu.VMEM((LANES, elem_count), i32), pltpu.VMEM((LANES, elem_count), f32),
            pltpu.VMEM((elem_count, LANES), f32),
        ],
        (8,),
    )(peer_rank, density, elem_nodes, stiffness, mass, regions, squares, base, node_row, right_side)

    send_shape = ((devices, ROWS, LANES), f32)
    send, inverse_at = call(
        bind(start_body), "start", [V] * 5, [send_shape, slots_all], (1,), (), range(5)
    )(peer_row, recv, right_at, diag_at, same)
    diag_recv = recv
    recv = exchange(send)
    inverse, z, energy = call(
        bind(first_fields_body), "first_fields", [V] * 5, [square, field, tile], range(3), (), range(5),
    )(peer_row, node_row, diag_recv, own_diag, right_side)

    weight_rows = [
        pltpu.VMEM((2 * LANES, 6 * LANES), jnp.bfloat16), pltpu.VMEM((6 * LANES, 2 * LANES), jnp.bfloat16)
    ]

    def inner_part(z):
        return call(
            bind(inner_body), "inner", [V] * 6, [half_rows, tile], range(2),
            [pltpu.VMEM(*half_rows), *weight_rows], (0, 1, 4, 5),
        )(z, idx, st_inner, mt_inner, weights1, weights2)

    def edge_part(recv, z, energy, curve):
        return call(
            bind(edge_body), "edge", [V] * 11,
            [half_rows, ((devices * (ROWS + 1), 1, LANES), f32)], (0,),
            [pltpu.VMEM(*half_rows), pltpu.VMEM((peers, ROWS, LANES), f32), *weight_rows], range(11),
        )(peer_row, recv, z, idx, st_edge, mt_edge, pos, weights1, weights2, energy, curve)

    wide = 2 * peers * slots
    scratch = [
        pltpu.VMEM((vectors * pairs, wide), jnp.bfloat16), pltpu.VMEM((LANES, wide), jnp.bfloat16),
        pltpu.VMEM(*field), pltpu.VMEM(*field),
        pltpu.SemaphoreType.DMA((2,)),
    ]
    inner, curve = inner_part(z)
    result, send = edge_part(recv, z, energy, curve)
    recv = exchange(send)
    own, image_at = call(
        bind(edge_scatter_pick_body), "edge_scatter_pick", [S] + [V] * 4, [field, slots_all], (1,), (),
        (1, 2, 3, 4),
    )(base, node_row, result, idx, inner)
    send, coefs = call(
        bind(step_body), "step", [V] * 6, [send_shape, ((2, ROWS, LANES), f32)], (1,), (),
        range(6),
    )(peer_row, recv, right_at, inverse_at, image_at, same)
    sum_recv = recv
    recv = exchange(send)
    w, z, energy = call(
        bind(next_fields_body), "next_fields", [V] * 3 + [hbm(), hbm()] + [V] * 2, [field, field, tile], (1, 2), scratch,
        (0, 1, 2, 5, 6),
    )(peer_row, node_row, sum_recv, own, right_side, inverse, coefs)
    inner, curve = inner_part(z)
    result, send = edge_part(recv, z, energy, curve)
    recv = exchange(send)
    (own,) = call(bind(edge_scatter_body), "edge_scatter", [V] * 3, [field], (0,), (), range(3))(
        result, idx, inner
    )
    return call(
        bind(last_body), "last", [V] * 4 + [hbm(), V, hbm()] + [V] * 2, [field, field], (),
        scratch + [
            pltpu.VMEM(*field), pltpu.VMEM(*field), pltpu.SemaphoreType.DMA((pairs // LAST_STEP, 2)),
        ],
        (0, 1, 2, 3, 5, 7, 8), out_specs=(hbm(), hbm()),
    )(peer_row, node_row, recv, own, right_side, inverse, w, z, coefs)


def solution(mesh):
    placed = (
        P(None, "dom"),
        P(None, None, "dom"),
        P(None, "dom"),
        P("dom"),
        P(),
        P(None, "dom"),
        P("dom", None),
        P("dom", None, None),
    )
    return jax.shard_map(
        on_device,
        mesh=mesh,
        in_specs=placed,
        out_specs=(P(None, "dom"), P(None, "dom")),
        check_vma=False,
    )
```

```python
import functools

import jax
import jax.numpy as jnp
import numpy as np
from jax import lax
from jax.experimental import pallas as pl
from jax.experimental.pallas import tpu as pltpu
from jax.sharding import PartitionSpec as P

ITERS = 2
LANES = 128
ROWS = 8
NONE = 255
SIDE = 5
NPE = SIDE**3


def gll_matrix():
    points = np.array([-1.0, -np.sqrt(3.0 / 7.0), 0.0, np.sqrt(3.0 / 7.0), 1.0])
    weights = np.array(
        [
            1.0 / np.prod([points[column] - points[other] for other in range(5) if other != column])
            for column in range(5)
        ]
    )
    matrix = np.zeros((5, 5))
    for row_index in range(5):
        for column in range(5):
            if row_index != column:
                matrix[row_index, column] = (
                    weights[column] / weights[row_index] / (points[row_index] - points[column])
                )
        matrix[row_index, row_index] = -np.sum(matrix[row_index])
    return matrix


def direction_matrices():
    base = np.asarray(gll_matrix(), np.float32)
    eye = np.eye(SIDE, dtype=np.float32)
    return [
        np.einsum("ai,bj,ck->abcijk", *factors).reshape(NPE, NPE)
        for factors in ((base, eye, eye), (eye, base, eye), (eye, eye, base))
    ]


def split_np(values):
    high = values.astype(jnp.bfloat16)
    low = (values - high.astype(np.float32)).astype(jnp.bfloat16)
    return high, low


def constant_operands():
    mats = direction_matrices()
    grad = np.zeros((LANES, 3 * LANES), np.float32)
    for d in range(3):
        grad[:NPE, d * LANES : d * LANES + NPE] = mats[d].T
    high, low = split_np(grad)
    first = np.concatenate([high, low], axis=1)
    second = np.concatenate([high.T, low.T], axis=1)
    squares = np.stack(split_np(np.stack([m.T * m.T for m in mats])))
    return jnp.asarray(first), jnp.asarray(second), jnp.asarray(squares)


def take(values, index):
    numbers = lax.GatherDimensionNumbers(
        offset_dims=(),
        collapsed_slice_dims=(1,),
        start_index_map=(1,),
        operand_batching_dims=(0,),
        start_indices_batching_dims=(0,),
    )
    return lax.gather(
        values, index[..., None], numbers, (1, 1), mode=lax.GatherScatterMode.PROMISE_IN_BOUNDS
    )


def iota(shape, axis):
    return lax.broadcasted_iota(jnp.int32, shape, axis)


def spread(row, rows=ROWS):
    return jnp.broadcast_to(row, (rows, row.shape[-1]))


def codes_of(nodes, lane_offset, peer_ref, own_count, peer_count, window):
    pair = (iota(nodes.shape, 1) + lane_offset) >> 1
    own = nodes - pair * window
    ref = nodes - own_count
    sender = ref // LANES
    slot = jnp.zeros_like(ref)
    for p in range(1, peer_count):
        slot = jnp.where(sender == peer_ref[0, p], p, slot)
    return jnp.where(ref >= 0, window + slot * LANES + (ref & (LANES - 1)), own)


def vmem():
    return pl.BlockSpec(memory_space=pltpu.VMEM)


def smem():
    return pl.BlockSpec(memory_space=pltpu.SMEM)


def hbm():
    return pl.BlockSpec(memory_space=pltpu.HBM)


def call(body, name, in_specs, outs, stay, scratch=(), resident=(), grid=(), out_specs=None):
    kernel = pl.pallas_call(
        body,
        name=name,
        grid=grid,
        in_specs=in_specs,
        out_specs=out_specs or tuple(vmem() for _ in outs),
        out_shape=tuple(
            (pltpu.VMEM if k in stay else pltpu.HBM)(shape, dtype)
            for k, (shape, dtype) in enumerate(outs)
        ),
        scratch_shapes=list(scratch),
        compiler_params=pltpu.CompilerParams(vmem_limit_bytes=24 << 20),
    )

    def run(*operands):
        return kernel(
            *[
                pltpu.with_memory_space_constraint(operand, pltpu.VMEM if k in resident else pltpu.HBM)
                for k, operand in enumerate(operands)
            ]
        )

    return run


def element_sums(mass, region, density, stiff, squares):
    dens = jnp.where(region == 0, density[0], jnp.where(region == 1, density[1], density[2]))
    term = mass * dens
    total = term
    for d in range(3):
        high = stiff[d].astype(jnp.bfloat16)
        low = (stiff[d] - high.astype(jnp.float32)).astype(jnp.bfloat16)
        for weight, part in ((squares[0, d], high), (squares[0, d], low), (squares[1, d], high)):
            total = total + jnp.dot(weight, part, preferred_element_type=jnp.float32)
    return term, total


def ghost_diag_body(
    cfg, peer, density, nodes, stiff, mass, region, squares, shared, send, pos, peer_row, base, node_row
):
    lanes = iota((1, LANES), 1)
    row = jnp.zeros((1, LANES), jnp.int32)
    for p in range(cfg["peers"]):
        row = jnp.where(lanes == p, peer[0, p], row)
        base[p] = shared[p] & (-LANES)
        node_row[:, p * LANES : (p + 1) * LANES] = shared[p]
    peer_row[...] = row
    run = cfg["run"]
    _, edge = element_sums(mass[...], region[...], density, stiff, squares)
    code = codes_of(nodes[...], 0, peer, cfg["own"], cfg["peers"], cfg["window"])
    lane = iota(code.shape, 1)
    base = code - (cfg["window"] + run * (lane >> 1))
    place = iota(code.shape, 0) + LANES * (lane & 1)
    flat = iota((ROWS, LANES), 0) * LANES + iota((ROWS, LANES), 1)
    pair = (flat * cfg["magic"]) >> 16
    hop = flat - pair * run
    pair_lane = jnp.minimum(2 * pair, LANES - 1)
    got = jnp.zeros((ROWS, LANES), jnp.float32)
    where_at = jnp.zeros((ROWS, LANES), jnp.int32)
    for h in range(run):
        hit = base == h
        position = jnp.sum(jnp.where(hit, place, 0), axis=0, keepdims=True)
        value = jnp.sum(jnp.where(hit, edge, 0.0), axis=0, keepdims=True)
        position, value = spread(position), spread(value)
        position = position + pltpu.roll(position, LANES - 1, 1)
        value = value + pltpu.roll(value, LANES - 1, 1)
        got = jnp.where(hop == h, take(value, pair_lane), got)
        where_at = jnp.where(hop == h, take(position, pair_lane), where_at)
    pos[...] = where_at
    send[...] = jnp.zeros(send.shape, jnp.float32)
    for p in range(cfg["peers"]):
        send[peer[0, p]] = got[p : p + 1]


def tables_body(
    cfg, peer, density, nodes, stiff_hbm, mass, region, squares, base_s, node_row, right_hbm,
    idx, st_edge, mt_edge, st_inner, mt_inner, own_diag, right_at, diag_at, same,
    code_pad, value_pad, rows, stiff, right, arrived,
):
    fetches = [
        pltpu.make_async_copy(stiff_hbm, stiff, arrived.at[0]),
        pltpu.make_async_copy(right_hbm, right, arrived.at[1]),
    ]
    for fetch in fetches:
        fetch.start()
    code_pad[...] = jnp.full(code_pad.shape, NONE, jnp.int32)
    value_pad[...] = jnp.zeros(value_pad.shape, jnp.float32)

    def turned(ref):
        return jnp.concatenate([ref[:, :LANES].T, ref[:, LANES:].T], axis=0)

    for b in range(2):
        cols = slice(b * LANES, (b + 1) * LANES)
        code_pad[:NPE, cols] = codes_of(
            nodes[:, cols], b * LANES, peer, cfg["own"], cfg["peers"], cfg["window"]
        )
    idx[...] = turned(code_pad)
    for fetch in fetches:
        fetch.wait()
    term, diag = element_sums(mass[...], region[...], density, stiff, squares)
    value_pad[:NPE] = diag
    rows[...] = turned(value_pad)
    for g in range(0, cfg["pairs"], 2):
        lines = [
            spread(jnp.concatenate([rows[2 * k : 2 * k + 1, :], rows[2 * k + 1 : 2 * k + 2, :]], axis=1))
            for k in (g, g + 1)
        ]
        for k, sums in enumerate(scatter_pairs(lines, idx, g)):
            own_diag[g + k : g + k + 1, :] = sums[:1]
    pick(cfg, right, base_s, node_row, right_at)
    for d in range(3):
        value_pad[:NPE] = stiff[d]
        cols = slice(d * LANES, (d + 1) * LANES)
        st_edge[:, cols] = value_pad[:, :LANES].T
        st_inner[:, cols] = value_pad[:, LANES:].T
    value_pad[:NPE] = term
    mt_edge[...] = value_pad[:, :LANES].T
    mt_inner[...] = value_pad[:, LANES:].T
    node = node_row[...]
    wide = node.shape[1]
    hot = jnp.where(iota((LANES, wide), 0) == (node & (LANES - 1)), 1.0, 0.0).astype(jnp.bfloat16)
    here = iota((LANES, wide), 0) == (node >> 7)
    at_slots = jnp.zeros((1, wide), jnp.float32)
    for part in reversed(parts_of(own_diag[...], 3)):
        seen = jnp.dot(part.astype(jnp.bfloat16), hot, preferred_element_type=jnp.float32)
        at_slots = at_slots + jnp.sum(jnp.where(here, seen, 0.0), axis=0, keepdims=True)
    diag_at[...] = spread(at_slots)
    for p in range(cfg["peers"]):
        column = jnp.broadcast_to(node[:, p * LANES : (p + 1) * LANES], (LANES, LANES)).T
        for q in range(cfg["peers"]):
            same[p * LANES : (p + 1) * LANES, q * LANES : (q + 1) * LANES] = jnp.where(
                column == node[:, q * LANES : (q + 1) * LANES], 1.0, 0.0
            ).astype(jnp.bfloat16)


def scatter_rows(rows, idx, g):
    node = iota((LANES, LANES), 0)
    spots = jnp.concatenate(
        [jnp.where(node == idx[2 * g + k : 2 * g + k + 1, :], 1.0, 0.0) for k in range(2)], axis=1
    ).astype(jnp.bfloat16)
    high = rows.astype(jnp.bfloat16).astype(jnp.float32)
    both = jnp.concatenate([high, rows - high], axis=0).astype(jnp.bfloat16)
    sums = lax.dot_general(both, spots, (((1,), (1,)), ((), ())), preferred_element_type=jnp.float32)
    return sums[:ROWS] + sums[ROWS:]


def scatter_pairs(rows, idx, g):
    node = iota((LANES, LANES), 0)
    spots = [
        jnp.concatenate(
            [jnp.where(node == idx[e : e + 1, :], 1.0, 0.0) for e in (2 * pair, 2 * pair + 1)], axis=1
        ).astype(jnp.bfloat16)
        for pair in (g, g + 1)
    ]
    parts = []
    for values in rows:
        high = values.astype(jnp.bfloat16).astype(jnp.float32)
        parts += [high, values - high]
    sums = nt_dot(jnp.concatenate(parts, axis=0).astype(jnp.bfloat16), jnp.concatenate(spots, axis=0))
    own = (sums[: 2 * ROWS, :LANES], sums[2 * ROWS :, LANES:])
    return [x[:ROWS] + x[ROWS:] for x in own]


def peers_of(cfg, peer_row):
    lane = iota((1, LANES), 1)
    return [jnp.max(jnp.where(lane == p, peer_row[...], 0)) for p in range(cfg["peers"])]


def pick(cfg, field, base_s, node_row, out):
    lane = iota((ROWS, LANES), 1)
    for p in range(cfg["peers"]):
        low = spread(node_row[:, p * LANES : (p + 1) * LANES] & (LANES - 1))
        got = jnp.zeros((ROWS, LANES), jnp.float32)
        for c in range(LANES):
            base = pl.multiple_of(base_s[p, 0, c], LANES)
            got = jnp.where(lane == c, take(field[:, pl.ds(base, LANES)], low), got)
        out[:, p * LANES : (p + 1) * LANES] = got


def nt_dot(left, right):
    return lax.dot_general(left, right, (((1,), (1,)), ((), ())), preferred_element_type=jnp.float32)


def parts_of(values, count):
    parts = []
    for _ in range(count):
        part = values.astype(jnp.bfloat16).astype(jnp.float32)
        parts.append(part)
        values = values - part
    return parts


def received_diag(cfg, peer, recv):
    return jnp.concatenate([recv[peer[p]] for p in range(cfg["peers"])], axis=1)


def received_rows(cfg, peer, recv):
    blocks = []
    for p in range(cfg["peers"]):
        first = peer[p] * (ROWS + 1)
        blocks.append(jnp.concatenate([recv[first + v] for v in range(ROWS)], axis=0))
    return jnp.concatenate(blocks, axis=1)


def put_slots(cfg, peer, values, out):
    for p in range(cfg["peers"]):
        out[peer[p]] = values[:, p * LANES : (p + 1) * LANES]


def start_body(cfg, peer_row, recv, right_at, diag_at, same, out, inverse_at):
    peer = peers_of(cfg, peer_row)
    got = spread(received_diag(cfg, peer, recv))
    top, middle, bottom = parts_of(got, 3)
    both = jnp.concatenate([top, middle], axis=0).astype(jnp.bfloat16)
    more = jnp.concatenate([bottom, bottom], axis=0).astype(jnp.bfloat16)
    first = nt_dot(both, same[...])
    total = diag_at[...] + (first[:ROWS] + (first[ROWS:] + nt_dot(more, same[...])[:ROWS]))
    inverse = 1.0 / total
    inverse_at[...] = inverse
    out[...] = jnp.zeros(out.shape, jnp.float32)
    put_slots(cfg, peer, right_at[...] * inverse, out)


def first_fields_body(cfg, peer_row, node_row, recv, own_diag, right, inverse, z, energy):
    peer = peers_of(cfg, peer_row)
    windows = cfg["pairs"]
    node, got = node_row[...], received_diag(cfg, peer, recv)
    here = iota((windows, got.shape[1]), 0) == (node >> 7)
    hot = jnp.where(iota((LANES, got.shape[1]), 0) == (node & (LANES - 1)), 1.0, 0.0).astype(jnp.bfloat16)
    total = own_diag[...]
    for part in parts_of(got, 3):
        total = total + nt_dot(jnp.where(here, spread(part, windows), 0.0).astype(jnp.bfloat16), hot)
    inverse[...] = 1.0 / total
    acc = jnp.zeros((ROWS, LANES), jnp.float32)
    for g in range(windows):
        cols = slice(g * LANES, (g + 1) * LANES)
        scaled = right[:, cols] * spread(inverse[g : g + 1, :])
        z[:, cols] = scaled
        acc = acc + right[:, cols] * scaled
    energy[...] = acc


def apply_rows(values, st, mt, weights1, weights2):
    count = values.shape[0] // ROWS

    def halves(x):
        high = x.astype(jnp.bfloat16)
        return jnp.concatenate([high, (x - high.astype(jnp.float32)).astype(jnp.bfloat16)], axis=1)

    both = jnp.dot(halves(values), weights1[...], preferred_element_type=jnp.float32)
    wide = 3 * LANES
    grad = (both[:, :wide] + both[:, wide:]).reshape(count, ROWS, wide)
    flux = (grad * st[:, None, :]).reshape(count * ROWS, wide)
    both = jnp.dot(halves(flux), weights2[...], preferred_element_type=jnp.float32)
    lumped = (values.reshape(count, ROWS, LANES) * mt[:, None, :]).reshape(count * ROWS, LANES)
    return both[:, :LANES] + both[:, LANES:] + lumped


def fill_weights(weights1, weights2, both1, both2):
    wide = 3 * LANES
    both1[:LANES] = weights1[...]
    both1[LANES:, :wide] = weights1[:, :wide]
    both1[LANES:, wide:] = jnp.zeros((LANES, wide), jnp.bfloat16)
    both2[:wide] = weights2[...]
    both2[wide:] = weights2[...]


CHUNK = 16


def apply_half(values, result, st, mt, weights1, weights2):
    acc = jnp.zeros((ROWS, LANES), jnp.float32)
    for c in range(values.shape[0] // (ROWS * CHUNK)):
        rows = slice(c * CHUNK * ROWS, (c + 1) * CHUNK * ROWS)
        elems = slice(c * CHUNK, (c + 1) * CHUNK)
        v = values[rows]
        r = apply_rows(v, st[elems], mt[elems], weights1, weights2)
        result[rows] = r
        acc = acc + jnp.sum((v * r).reshape(CHUNK, ROWS, LANES), axis=0)
    return acc


def scatter_half(edge, inner, idx, out):
    count = edge.shape[0] // (2 * ROWS)
    for g in range(idx.shape[0] // 2):
        half, e = (edge, 2 * g * ROWS) if g < count else (inner, 2 * (g - count) * ROWS)
        rows = jnp.concatenate([half[e : e + ROWS], half[e + ROWS : e + 2 * ROWS]], axis=1)
        out[:, g * LANES : (g + 1) * LANES] = scatter_rows(rows, idx, g)


def inner_body(cfg, z, idx, st, mt, w1, w2, result, curve, values, both1, both2):
    fill_weights(w1, w2, both1, both2)
    edge, pairs = cfg["edge_pairs"], cfg["pairs"]
    for g in range(edge, pairs):
        window = z[:, g * LANES : (g + 1) * LANES]
        for parity in range(2):
            e = 2 * g + parity
            at = (e - 2 * edge) * ROWS
            values[at : at + ROWS] = take(window, spread(idx[e : e + 1, :] & (LANES - 1)))
    curve[...] = apply_half(values, result, st, mt, both1, both2)


def edge_body(
    cfg, peer_row, recv, z, idx, st, mt, pos, w1, w2, energy, curve, result, out, values, ghosts, both1, both2
):
    peer = peers_of(cfg, peer_row)
    fill_weights(w1, w2, both1, both2)
    run, edge, peers = cfg["run"], cfg["edge_pairs"], cfg["peers"]
    for p in range(peers):
        ghosts[p] = recv[peer[p]]
    spans = []
    for g in range(edge):
        low, high = run * g // LANES, (run * (g + 1) - 1) // LANES
        spans.append((low, high))
        window = z[:, g * LANES : (g + 1) * LANES]
        for parity in range(2):
            e = 2 * g + parity
            code = spread(idx[e : e + 1, :])
            at = code & (LANES - 1)
            got = take(ghosts[low], at)
            if high > low:
                got = jnp.where(code < LANES * (high + 1), got, take(ghosts[high], at))
            values[e * ROWS : (e + 1) * ROWS] = jnp.where(code < LANES, take(window, at), got)
    acc = apply_half(values, result, st, mt, both1, both2) + curve[...]
    lane = iota((ROWS, LANES), 1)
    sums = [jnp.zeros((ROWS, LANES), jnp.float32) for _ in range(peers)]
    for g in range(edge):
        for p in range(spans[g][0], spans[g][1] + 1):
            place = spread(pos[p : p + 1, :])
            at = place & (LANES - 1)
            e = 2 * g * ROWS
            value = jnp.where(
                place < LANES, take(result[e : e + ROWS], at), take(result[e + ROWS : e + 2 * ROWS], at)
            )
            begin, end = run * g - p * LANES, run * (g + 1) - p * LANES
            sums[p] = jnp.where((lane >= begin) & (lane < end), value, sums[p])
    row = iota((ROWS, LANES), 0)
    dots = jnp.where(lane == row, jnp.sum(energy[...], axis=1, keepdims=True), 0.0)
    dots = jnp.where(lane == row + ROWS, jnp.sum(acc, axis=1, keepdims=True), dots)
    dots = jnp.sum(dots, axis=0, keepdims=True)
    out[...] = jnp.zeros(out.shape, jnp.float32)
    for n in range(out.shape[0] // (ROWS + 1)):
        out[n * (ROWS + 1) + ROWS] = dots
    for p in range(peers):
        for v in range(ROWS):
            out[peer[p] * (ROWS + 1) + v] = sums[p][v : v + 1]


def edge_scatter_body(cfg, result, idx, inner, out):
    scatter_half(result, inner, idx, out)


def edge_scatter_pick_body(cfg, base_s, node_row, result, idx, inner, out, at_slots):
    edge_scatter_body(cfg, result, idx, inner, out)
    pick(cfg, out, base_s, node_row, at_slots)


RETURN_STEP = 32


def returned_sums(cfg, peer, node_row, recv, left, hot, step):
    windows = cfg["pairs"]
    node, value = node_row[...], received_rows(cfg, peer, recv)
    wide = node.shape[1]
    high, low = parts_of(value, 2)
    lanes = jnp.where(iota((LANES, wide), 0) == (node & (LANES - 1)), 1.0, 0.0).astype(jnp.bfloat16)
    hot[:, :wide] = lanes
    hot[:, wide:] = lanes
    block = spread(node >> 7)
    for start in range(0, windows, step):
        for g in range(start, start + step, 2):
            rows = slice(g * ROWS, (g + 2) * ROWS)
            even, odd = block == g, block == g + 1
            left[rows, :wide] = jnp.concatenate(
                [jnp.where(even, high, 0.0), jnp.where(odd, high, 0.0)], axis=0
            ).astype(jnp.bfloat16)
            left[rows, wide:] = jnp.concatenate(
                [jnp.where(even, low, 0.0), jnp.where(odd, low, 0.0)], axis=0
            ).astype(jnp.bfloat16)
        yield start, nt_dot(left[start * ROWS : (start + step) * ROWS], hot[...])


def dot_totals(recv):
    total = recv[ROWS]
    for n in range(1, recv.shape[0] // (ROWS + 1)):
        total = total + recv[n * (ROWS + 1) + ROWS]
    total = spread(total)
    lane, row = iota((ROWS, LANES), 1), iota((ROWS, LANES), 0)
    return [
        jnp.broadcast_to(
            jnp.sum(jnp.where(lane == row + k * ROWS, total, 0.0), axis=1, keepdims=True), (ROWS, LANES)
        )
        for k in range(2)
    ]


def step_body(cfg, peer_row, recv, right_at, inverse_at, image_at, same, out, coefs):
    peer = peers_of(cfg, peer_row)
    energy_now, curve_now = dot_totals(recv)
    alpha = energy_now / curve_now
    coefs[0] = alpha
    coefs[1] = energy_now
    both = jnp.concatenate(parts_of(received_rows(cfg, peer, recv), 2), axis=0).astype(jnp.bfloat16)
    got = nt_dot(both, same[...])
    image = image_at[...] + (got[:ROWS] + got[ROWS:])
    left_over = right_at[...] - spread_lanes(alpha, image.shape[1]) * image
    out[...] = jnp.zeros(out.shape, jnp.float32)
    put_slots(cfg, peer, left_over * inverse_at[...], out)


def spread_lanes(tile, wide):
    return jnp.concatenate([tile] * (wide // LANES), axis=1)


def window_sums(*operands, step):
    for start, sums in returned_sums(*operands, step):
        for k in range(step):
            yield start + k, sums[k * ROWS : (k + 1) * ROWS]


def next_fields_body(
    cfg, peer_row, node_row, recv, own_hbm, right_hbm, inverse, coefs, w, z1, energy, left, hot, right, own, arrived
):
    fetches = [
        pltpu.make_async_copy(there, here, arrived.at[k]) for k, (there, here) in enumerate(((right_hbm, right), (own_hbm, own)))
    ]
    for fetch in fetches:
        fetch.start()
    peer = peers_of(cfg, peer_row)
    alpha = coefs[0]
    acc = jnp.zeros((ROWS, LANES), jnp.float32)
    for g, sums in window_sums(cfg, peer, node_row, recv, left, hot, step=cfg["pairs"]):
        if g == 0:
            for fetch in fetches:
                fetch.wait()
        cols = slice(g * LANES, (g + 1) * LANES)
        image = own[:, cols] + sums
        w[:, cols] = image
        left_over = right[:, cols] - alpha * image
        scaled = left_over * spread(inverse[g : g + 1, :])
        z1[:, cols] = scaled
        acc = acc + left_over * scaled
    energy[...] = acc


LAST_STEP = 32


def last_body(
    cfg, peer_row, node_row, recv, own, right_hbm, inverse, w_hbm, z1, coefs,
    solution_hbm, residual_hbm, left, hot, right, w, arrived, solution, residual, sent,
):
    fetches = [
        pltpu.make_async_copy(there, here, arrived.at[k]) for k, (there, here) in enumerate(((right_hbm, right), (w_hbm, w)))
    ]
    for fetch in fetches:
        fetch.start()
    peer = peers_of(cfg, peer_row)
    windows = cfg["pairs"]
    energy_next, curve_next = dot_totals(recv)
    alpha, energy_now = coefs[0], coefs[1]
    beta = energy_next / energy_now
    step = energy_next / (curve_next - beta * energy_next / alpha)
    copies = []
    for fetch in fetches:
        fetch.wait()
    for g, sums in window_sums(cfg, peer, node_row, recv, left, hot, step=RETURN_STEP):
        cols = slice(g * LANES, (g + 1) * LANES)
        image = own[:, cols] + sums
        start, before = right[:, cols], w[:, cols]
        z0 = start * spread(inverse[g : g + 1, :])
        residual[:, cols] = (start - alpha * before) - step * (image + beta * before)
        solution[:, cols] = alpha * z0 + step * (z1[:, cols] + beta * z0)
        if (g + 1) % LAST_STEP == 0:
            done = slice((g + 1 - LAST_STEP) * LANES, (g + 1) * LANES)
            for k, (here, there) in enumerate(((solution, solution_hbm), (residual, residual_hbm))):
                copies.append(
                    pltpu.make_async_copy(here.at[:, done], there.at[:, done], sent.at[g // LAST_STEP, k])
                )
                copies[-1].start()
    for copy in copies:
        copy.wait()


def on_device(right_side, stiffness, mass, region, density, elem_nodes, peer_rank, send_nodes):
    vectors, own_count = right_side.shape
    elem_count = elem_nodes.shape[1]
    pairs = elem_count // 2
    edge_pairs = pairs // 2
    peers, slots = send_nodes.shape[1], send_nodes.shape[2]
    devices = lax.axis_size("dom")
    run = peers * slots // edge_pairs
    magic = (1 << 16) // run + 1
    flat = np.arange(ROWS * LANES)
    if (
        vectors != ROWS or own_count != pairs * LANES or slots != LANES or pairs != LANES
        or peers * slots != run * edge_pairs or peers > ROWS or run > LANES
        or ((flat * magic) >> 16 != flat // run).any()
    ):
        raise ValueError("unsupported sizes")
    cfg = dict(
        own=own_count, pairs=pairs, edge_pairs=edge_pairs, peers=peers, run=run, magic=magic,
        window=own_count // pairs,
    )
    f32, i32 = jnp.float32, jnp.int32
    weights1, weights2, squares = constant_operands()
    V, S = vmem(), smem()
    field = ((vectors, own_count), f32)
    tile = ((ROWS, LANES), f32)
    square = ((LANES, LANES), f32)
    half_rows = ((elem_count // 2 * ROWS, LANES), f32)

    def bind(body):
        return functools.partial(body, cfg)

    def exchange(values):
        return lax.all_to_all(values, "dom", split_axis=0, concat_axis=0, tiled=True)

    regions = region.reshape(1, elem_count)
    half_specs = [
        pl.BlockSpec((NPE, LANES), lambda _: (0, 0)),
        pl.BlockSpec((3, NPE, LANES), lambda _: (0, 0, 0)),
        pl.BlockSpec((NPE, LANES), lambda _: (0, 0)),
        pl.BlockSpec((1, LANES), lambda _: (0, 0)),
    ]
    shared = jnp.transpose(send_nodes, (1, 0, 2))
    send, pos, peer_row, base, node_row = call(
        bind(ghost_diag_body), "ghost_diag", [S, S, *half_specs, V, V],
        [
            ((devices, 1, LANES), f32), ((ROWS, LANES), i32), ((1, LANES), i32), ((peers, 1, slots), i32),
            ((1, peers * slots), i32),
        ],
        (1, 2, 4), grid=(1,),
    )(peer_rank, density, elem_nodes, stiffness, mass, regions, squares, shared)
    recv = exchange(send)
    slots_all = ((vectors, peers * slots), f32)
    edge_count = elem_count // 2
    idx, st_edge, mt_edge, st_inner, mt_inner, own_diag, right_at, diag_at, same = call(
        bind(tables_body), "tables", [S, S, V, hbm(), V, V, V, S, V, hbm()],
        [
            ((elem_count, LANES), i32),
            ((edge_count, 3 * LANES), f32), ((edge_count, LANES), f32),
            ((elem_count - edge_count, 3 * LANES), f32), ((elem_count - edge_count, LANES), f32),
            square, slots_all, slots_all, ((peers * slots, peers * slots), jnp.bfloat16),
        ],
        (0, 1, 2, 5, 6, 7, 8),
        [
            pltpu.VMEM((LANES, elem_count), i32), pltpu.VMEM((LANES, elem_count), f32),
            pltpu.VMEM((elem_count, LANES), f32), pltpu.VMEM(stiffness.shape, f32), pltpu.VMEM(*field),
            pltpu.SemaphoreType.DMA((2,)),
        ],
        (8,),
    )(peer_rank, density, elem_nodes, stiffness, mass, regions, squares, base, node_row, right_side)

    send_shape = ((devices, ROWS, LANES), f32)
    send, inverse_at = call(
        bind(start_body), "start", [V] * 5, [send_shape, slots_all], (1,), (), range(5)
    )(peer_row, recv, right_at, diag_at, same)
    diag_recv = recv
    recv = exchange(send)
    inverse, z, energy = call(
        bind(first_fields_body), "first_fields", [V] * 5, [square, field, tile], range(3), (), range(5),
    )(peer_row, node_row, diag_recv, own_diag, right_side)

    weight_rows = [
        pltpu.VMEM((2 * LANES, 6 * LANES), jnp.bfloat16), pltpu.VMEM((6 * LANES, 2 * LANES), jnp.bfloat16)
    ]

    def inner_part(z):
        return call(
            bind(inner_body), "inner", [V] * 6, [half_rows, tile], range(2),
            [pltpu.VMEM(*half_rows), *weight_rows], (0, 1, 4, 5),
        )(z, idx, st_inner, mt_inner, weights1, weights2)

    def edge_part(recv, z, energy, curve):
        return call(
            bind(edge_body), "edge", [V] * 11,
            [half_rows, ((devices * (ROWS + 1), 1, LANES), f32)], (0,),
            [pltpu.VMEM(*half_rows), pltpu.VMEM((peers, ROWS, LANES), f32), *weight_rows], range(11),
        )(peer_row, recv, z, idx, st_edge, mt_edge, pos, weights1, weights2, energy, curve)

    wide = 2 * peers * slots
    scratch = [
        pltpu.VMEM((vectors * pairs, wide), jnp.bfloat16), pltpu.VMEM((LANES, wide), jnp.bfloat16),
        pltpu.VMEM(*field), pltpu.VMEM(*field),
        pltpu.SemaphoreType.DMA((2,)),
    ]
    inner, curve = inner_part(z)
    result, send = edge_part(recv, z, energy, curve)
    recv = exchange(send)
    own, image_at = call(
        bind(edge_scatter_pick_body), "edge_scatter_pick", [S] + [V] * 4, [field, slots_all], (1,), (),
        (1, 2, 3, 4),
    )(base, node_row, result, idx, inner)
    send, coefs = call(
        bind(step_body), "step", [V] * 6, [send_shape, ((2, ROWS, LANES), f32)], (1,), (),
        range(6),
    )(peer_row, recv, right_at, inverse_at, image_at, same)
    sum_recv = recv
    recv = exchange(send)
    w, z, energy = call(
        bind(next_fields_body), "next_fields", [V] * 3 + [hbm(), hbm()] + [V] * 2, [field, field, tile], (1, 2), scratch,
        (0, 1, 2, 5, 6),
    )(peer_row, node_row, sum_recv, own, right_side, inverse, coefs)
    inner, curve = inner_part(z)
    result, send = edge_part(recv, z, energy, curve)
    recv = exchange(send)
    (own,) = call(bind(edge_scatter_body), "edge_scatter", [V] * 3, [field], (0,), (), range(3))(
        result, idx, inner
    )
    return call(
        bind(last_body), "last", [V] * 4 + [hbm(), V, hbm()] + [V] * 2, [field, field], (),
        scratch + [
            pltpu.VMEM(*field), pltpu.VMEM(*field), pltpu.SemaphoreType.DMA((pairs // LAST_STEP, 2)),
        ],
        (0, 1, 2, 3, 5, 7, 8), out_specs=(hbm(), hbm()),
    )(peer_row, node_row, recv, own, right_side, inverse, w, z, coefs)


def solution(mesh):
    placed = (
        P(None, "dom"),
        P(None, None, "dom"),
        P(None, "dom"),
        P("dom"),
        P(),
        P(None, "dom"),
        P("dom", None),
        P("dom", None, None),
    )
    return jax.shard_map(
        on_device,
        mesh=mesh,
        in_specs=placed,
        out_specs=(P(None, "dom"), P(None, "dom")),
        check_vma=False,
    )
```

```python
import functools

import jax
import jax.numpy as jnp
import numpy as np
from jax import lax
from jax.experimental import pallas as pl
from jax.experimental.pallas import tpu as pltpu
from jax.sharding import PartitionSpec as P

ITERS = 2
LANES = 128
ROWS = 8
NONE = 255
SIDE = 5
NPE = SIDE**3


def gll_matrix():
    points = np.array([-1.0, -np.sqrt(3.0 / 7.0), 0.0, np.sqrt(3.0 / 7.0), 1.0])
    weights = np.array(
        [
            1.0 / np.prod([points[column] - points[other] for other in range(5) if other != column])
            for column in range(5)
        ]
    )
    matrix = np.zeros((5, 5))
    for row_index in range(5):
        for column in range(5):
            if row_index != column:
                matrix[row_index, column] = (
                    weights[column] / weights[row_index] / (points[row_index] - points[column])
                )
        matrix[row_index, row_index] = -np.sum(matrix[row_index])
    return matrix


def direction_matrices():
    base = np.asarray(gll_matrix(), np.float32)
    eye = np.eye(SIDE, dtype=np.float32)
    return [
        np.einsum("ai,bj,ck->abcijk", *factors).reshape(NPE, NPE)
        for factors in ((base, eye, eye), (eye, base, eye), (eye, eye, base))
    ]


def split_np(values):
    high = values.astype(jnp.bfloat16)
    low = (values - high.astype(np.float32)).astype(jnp.bfloat16)
    return high, low


def constant_operands():
    mats = direction_matrices()
    grad = np.zeros((LANES, 3 * LANES), np.float32)
    for d in range(3):
        grad[:NPE, d * LANES : d * LANES + NPE] = mats[d].T
    high, low = split_np(grad)
    first = np.concatenate([high, low], axis=1)
    second = np.concatenate([high.T, low.T], axis=1)
    squares = np.stack(split_np(np.stack([m.T * m.T for m in mats])))
    return jnp.asarray(first), jnp.asarray(second), jnp.asarray(squares)


def take(values, index):
    numbers = lax.GatherDimensionNumbers(
        offset_dims=(),
        collapsed_slice_dims=(1,),
        start_index_map=(1,),
        operand_batching_dims=(0,),
        start_indices_batching_dims=(0,),
    )
    return lax.gather(
        values, index[..., None], numbers, (1, 1), mode=lax.GatherScatterMode.PROMISE_IN_BOUNDS
    )


def iota(shape, axis):
    return lax.broadcasted_iota(jnp.int32, shape, axis)


def spread(row, rows=ROWS):
    return jnp.broadcast_to(row, (rows, row.shape[-1]))


def codes_of(nodes, lane_offset, peer_ref, own_count, peer_count, window):
    pair = (iota(nodes.shape, 1) + lane_offset) >> 1
    own = nodes - pair * window
    ref = nodes - own_count
    sender = ref // LANES
    slot = jnp.zeros_like(ref)
    for p in range(1, peer_count):
        slot = jnp.where(sender == peer_ref[0, p], p, slot)
    return jnp.where(ref >= 0, window + slot * LANES + (ref & (LANES - 1)), own)


def vmem():
    return pl.BlockSpec(memory_space=pltpu.VMEM)


def smem():
    return pl.BlockSpec(memory_space=pltpu.SMEM)


def hbm():
    return pl.BlockSpec(memory_space=pltpu.HBM)


def call(body, name, in_specs, outs, stay, scratch=(), resident=(), grid=(), out_specs=None):
    kernel = pl.pallas_call(
        body,
        name=name,
        grid=grid,
        in_specs=in_specs,
        out_specs=out_specs or tuple(vmem() for _ in outs),
        out_shape=tuple(
            (pltpu.VMEM if k in stay else pltpu.HBM)(shape, dtype)
            for k, (shape, dtype) in enumerate(outs)
        ),
        scratch_shapes=list(scratch),
        compiler_params=pltpu.CompilerParams(vmem_limit_bytes=24 << 20),
    )

    def run(*operands):
        return kernel(
            *[
                pltpu.with_memory_space_constraint(operand, pltpu.VMEM if k in resident else pltpu.HBM)
                for k, operand in enumerate(operands)
            ]
        )

    return run


def element_sums(mass, region, density, stiff, squares):
    dens = jnp.where(region == 0, density[0], jnp.where(region == 1, density[1], density[2]))
    term = mass * dens
    total = term
    for d in range(3):
        high = stiff[d].astype(jnp.bfloat16)
        low = (stiff[d] - high.astype(jnp.float32)).astype(jnp.bfloat16)
        for weight, part in ((squares[0, d], high), (squares[0, d], low), (squares[1, d], high)):
            total = total + jnp.dot(weight, part, preferred_element_type=jnp.float32)
    return term, total


def ghost_diag_body(
    cfg, peer, density, nodes, stiff, mass, region, squares, shared, send, pos, peer_row, base, node_row
):
    lanes = iota((1, LANES), 1)
    row = jnp.zeros((1, LANES), jnp.int32)
    for p in range(cfg["peers"]):
        row = jnp.where(lanes == p, peer[0, p], row)
        base[p] = shared[p] & (-LANES)
        node_row[:, p * LANES : (p + 1) * LANES] = shared[p]
    peer_row[...] = row
    run = cfg["run"]
    _, edge = element_sums(mass[...], region[...], density, stiff, squares)
    code = codes_of(nodes[...], 0, peer, cfg["own"], cfg["peers"], cfg["window"])
    lane = iota(code.shape, 1)
    base = code - (cfg["window"] + run * (lane >> 1))
    place = iota(code.shape, 0) + LANES * (lane & 1)
    flat = iota((ROWS, LANES), 0) * LANES + iota((ROWS, LANES), 1)
    pair = (flat * cfg["magic"]) >> 16
    hop = flat - pair * run
    pair_lane = jnp.minimum(2 * pair, LANES - 1)
    got = jnp.zeros((ROWS, LANES), jnp.float32)
    where_at = jnp.zeros((ROWS, LANES), jnp.int32)
    for h in range(run):
        hit = base == h
        position = jnp.sum(jnp.where(hit, place, 0), axis=0, keepdims=True)
        value = jnp.sum(jnp.where(hit, edge, 0.0), axis=0, keepdims=True)
        position, value = spread(position), spread(value)
        position = position + pltpu.roll(position, LANES - 1, 1)
        value = value + pltpu.roll(value, LANES - 1, 1)
        got = jnp.where(hop == h, take(value, pair_lane), got)
        where_at = jnp.where(hop == h, take(position, pair_lane), where_at)
    pos[...] = where_at
    send[...] = jnp.zeros(send.shape, jnp.float32)
    for p in range(cfg["peers"]):
        send[peer[0, p]] = got[p : p + 1]


def tables_body(
    cfg, peer, density, nodes, stiff, mass, region, squares, base_s, node_row, right,
    idx, st_edge, mt_edge, st_inner, mt_inner, own_diag, right_at, diag_at, same,
    code_pad, value_pad, rows,
):
    code_pad[...] = jnp.full(code_pad.shape, NONE, jnp.int32)
    value_pad[...] = jnp.zeros(value_pad.shape, jnp.float32)

    def turned(ref):
        return jnp.concatenate([ref[:, :LANES].T, ref[:, LANES:].T], axis=0)

    for b in range(2):
        cols = slice(b * LANES, (b + 1) * LANES)
        code_pad[:NPE, cols] = codes_of(
            nodes[:, cols], b * LANES, peer, cfg["own"], cfg["peers"], cfg["window"]
        )
    idx[...] = turned(code_pad)
    term, diag = element_sums(mass[...], region[...], density, stiff, squares)
    value_pad[:NPE] = diag
    rows[...] = turned(value_pad)
    for g in range(cfg["pairs"]):
        row = jnp.concatenate([rows[2 * g : 2 * g + 1, :], rows[2 * g + 1 : 2 * g + 2, :]], axis=1)
        own_diag[g : g + 1, :] = scatter_rows(spread(row), idx, g)[:1]
    for d in range(3):
        value_pad[:NPE] = stiff[d]
        cols = slice(d * LANES, (d + 1) * LANES)
        st_edge[:, cols] = value_pad[:, :LANES].T
        st_inner[:, cols] = value_pad[:, LANES:].T
    value_pad[:NPE] = term
    mt_edge[...] = value_pad[:, :LANES].T
    mt_inner[...] = value_pad[:, LANES:].T
    pick(cfg, right, base_s, node_row, right_at)
    node = node_row[...]
    wide = node.shape[1]
    hot = jnp.where(iota((LANES, wide), 0) == (node & (LANES - 1)), 1.0, 0.0).astype(jnp.bfloat16)
    here = iota((LANES, wide), 0) == (node >> 7)
    at_slots = jnp.zeros((1, wide), jnp.float32)
    for part in reversed(parts_of(own_diag[...], 3)):
        seen = jnp.dot(part.astype(jnp.bfloat16), hot, preferred_element_type=jnp.float32)
        at_slots = at_slots + jnp.sum(jnp.where(here, seen, 0.0), axis=0, keepdims=True)
    diag_at[...] = spread(at_slots)
    for p in range(cfg["peers"]):
        column = jnp.broadcast_to(node[:, p * LANES : (p + 1) * LANES], (LANES, LANES)).T
        for q in range(cfg["peers"]):
            same[p * LANES : (p + 1) * LANES, q * LANES : (q + 1) * LANES] = jnp.where(
                column == node[:, q * LANES : (q + 1) * LANES], 1.0, 0.0
            ).astype(jnp.bfloat16)


def scatter_rows(rows, idx, g):
    node = iota((LANES, LANES), 0)
    spots = jnp.concatenate(
        [jnp.where(node == idx[2 * g + k : 2 * g + k + 1, :], 1.0, 0.0) for k in range(2)], axis=1
    ).astype(jnp.bfloat16)
    high = rows.astype(jnp.bfloat16).astype(jnp.float32)
    both = jnp.concatenate([high, rows - high], axis=0).astype(jnp.bfloat16)
    sums = lax.dot_general(both, spots, (((1,), (1,)), ((), ())), preferred_element_type=jnp.float32)
    return sums[:ROWS] + sums[ROWS:]


def peers_of(cfg, peer_row):
    lane = iota((1, LANES), 1)
    return [jnp.max(jnp.where(lane == p, peer_row[...], 0)) for p in range(cfg["peers"])]


def pick(cfg, field, base_s, node_row, out):
    lane = iota((ROWS, LANES), 1)
    for p in range(cfg["peers"]):
        low = spread(node_row[:, p * LANES : (p + 1) * LANES] & (LANES - 1))
        got = jnp.zeros((ROWS, LANES), jnp.float32)
        for c in range(LANES):
            base = pl.multiple_of(base_s[p, 0, c], LANES)
            got = jnp.where(lane == c, take(field[:, pl.ds(base, LANES)], low), got)
        out[:, p * LANES : (p + 1) * LANES] = got


def nt_dot(left, right):
    return lax.dot_general(left, right, (((1,), (1,)), ((), ())), preferred_element_type=jnp.float32)


def parts_of(values, count):
    parts = []
    for _ in range(count):
        part = values.astype(jnp.bfloat16).astype(jnp.float32)
        parts.append(part)
        values = values - part
    return parts


def received_diag(cfg, peer, recv):
    return jnp.concatenate([recv[peer[p]] for p in range(cfg["peers"])], axis=1)


def received_rows(cfg, peer, recv):
    blocks = []
    for p in range(cfg["peers"]):
        first = peer[p] * (ROWS + 1)
        blocks.append(jnp.concatenate([recv[first + v] for v in range(ROWS)], axis=0))
    return jnp.concatenate(blocks, axis=1)


def put_slots(cfg, peer, values, out):
    for p in range(cfg["peers"]):
        out[peer[p]] = values[:, p * LANES : (p + 1) * LANES]


def start_body(cfg, peer_row, recv, right_at, diag_at, same, out, inverse_at):
    peer = peers_of(cfg, peer_row)
    got = spread(received_diag(cfg, peer, recv))
    top, middle, bottom = parts_of(got, 3)
    both = jnp.concatenate([top, middle], axis=0).astype(jnp.bfloat16)
    more = jnp.concatenate([bottom, bottom], axis=0).astype(jnp.bfloat16)
    first = nt_dot(both, same[...])
    total = diag_at[...] + (first[:ROWS] + (first[ROWS:] + nt_dot(more, same[...])[:ROWS]))
    inverse = 1.0 / total
    inverse_at[...] = inverse
    out[...] = jnp.zeros(out.shape, jnp.float32)
    put_slots(cfg, peer, right_at[...] * inverse, out)


def first_fields_body(cfg, peer_row, node_row, recv, own_diag, right, inverse, z, energy):
    peer = peers_of(cfg, peer_row)
    windows = cfg["pairs"]
    node, got = node_row[...], received_diag(cfg, peer, recv)
    here = iota((windows, got.shape[1]), 0) == (node >> 7)
    hot = jnp.where(iota((LANES, got.shape[1]), 0) == (node & (LANES - 1)), 1.0, 0.0).astype(jnp.bfloat16)
    total = own_diag[...]
    for part in parts_of(got, 3):
        total = total + nt_dot(jnp.where(here, spread(part, windows), 0.0).astype(jnp.bfloat16), hot)
    inverse[...] = 1.0 / total
    acc = jnp.zeros((ROWS, LANES), jnp.float32)
    for g in range(windows):
        cols = slice(g * LANES, (g + 1) * LANES)
        scaled = right[:, cols] * spread(inverse[g : g + 1, :])
        z[:, cols] = scaled
        acc = acc + right[:, cols] * scaled
    energy[...] = acc


def apply_rows(values, st, mt, weights1, weights2):
    count = values.shape[0] // ROWS

    def halves(x):
        high = x.astype(jnp.bfloat16)
        return jnp.concatenate([high, (x - high.astype(jnp.float32)).astype(jnp.bfloat16)], axis=1)

    both = jnp.dot(halves(values), weights1[...], preferred_element_type=jnp.float32)
    wide = 3 * LANES
    grad = (both[:, :wide] + both[:, wide:]).reshape(count, ROWS, wide)
    flux = (grad * st[:, None, :]).reshape(count * ROWS, wide)
    both = jnp.dot(halves(flux), weights2[...], preferred_element_type=jnp.float32)
    lumped = (values.reshape(count, ROWS, LANES) * mt[:, None, :]).reshape(count * ROWS, LANES)
    return both[:, :LANES] + both[:, LANES:] + lumped


def fill_weights(weights1, weights2, both1, both2):
    wide = 3 * LANES
    both1[:LANES] = weights1[...]
    both1[LANES:, :wide] = weights1[:, :wide]
    both1[LANES:, wide:] = jnp.zeros((LANES, wide), jnp.bfloat16)
    both2[:wide] = weights2[...]
    both2[wide:] = weights2[...]


CHUNK = 16


def apply_half(values, result, st, mt, weights1, weights2):
    acc = jnp.zeros((ROWS, LANES), jnp.float32)
    for c in range(values.shape[0] // (ROWS * CHUNK)):
        rows = slice(c * CHUNK * ROWS, (c + 1) * CHUNK * ROWS)
        elems = slice(c * CHUNK, (c + 1) * CHUNK)
        v = values[rows]
        r = apply_rows(v, st[elems], mt[elems], weights1, weights2)
        result[rows] = r
        acc = acc + jnp.sum((v * r).reshape(CHUNK, ROWS, LANES), axis=0)
    return acc


def scatter_half(edge, inner, idx, out):
    count = edge.shape[0] // (2 * ROWS)
    for g in range(idx.shape[0] // 2):
        half, e = (edge, 2 * g * ROWS) if g < count else (inner, 2 * (g - count) * ROWS)
        rows = jnp.concatenate([half[e : e + ROWS], half[e + ROWS : e + 2 * ROWS]], axis=1)
        out[:, g * LANES : (g + 1) * LANES] = scatter_rows(rows, idx, g)


def inner_body(cfg, z, idx, st, mt, w1, w2, result, curve, values, both1, both2):
    fill_weights(w1, w2, both1, both2)
    edge, pairs = cfg["edge_pairs"], cfg["pairs"]
    for g in range(edge, pairs):
        window = z[:, g * LANES : (g + 1) * LANES]
        for parity in range(2):
            e = 2 * g + parity
            at = (e - 2 * edge) * ROWS
            values[at : at + ROWS] = take(window, spread(idx[e : e + 1, :] & (LANES - 1)))
    curve[...] = apply_half(values, result, st, mt, both1, both2)


def edge_body(
    cfg, peer_row, recv, z, idx, st, mt, pos, w1, w2, energy, curve, result, out, values, ghosts, both1, both2
):
    peer = peers_of(cfg, peer_row)
    fill_weights(w1, w2, both1, both2)
    run, edge, peers = cfg["run"], cfg["edge_pairs"], cfg["peers"]
    for p in range(peers):
        ghosts[p] = recv[peer[p]]
    spans = []
    for g in range(edge):
        low, high = run * g // LANES, (run * (g + 1) - 1) // LANES
        spans.append((low, high))
        window = z[:, g * LANES : (g + 1) * LANES]
        for parity in range(2):
            e = 2 * g + parity
            code = spread(idx[e : e + 1, :])
            at = code & (LANES - 1)
            got = take(ghosts[low], at)
            if high > low:
                got = jnp.where(code < LANES * (high + 1), got, take(ghosts[high], at))
            values[e * ROWS : (e + 1) * ROWS] = jnp.where(code < LANES, take(window, at), got)
    acc = apply_half(values, result, st, mt, both1, both2) + curve[...]
    lane = iota((ROWS, LANES), 1)
    sums = [jnp.zeros((ROWS, LANES), jnp.float32) for _ in range(peers)]
    for g in range(edge):
        for p in range(spans[g][0], spans[g][1] + 1):
            place = spread(pos[p : p + 1, :])
            at = place & (LANES - 1)
            e = 2 * g * ROWS
            value = jnp.where(
                place < LANES, take(result[e : e + ROWS], at), take(result[e + ROWS : e + 2 * ROWS], at)
            )
            begin, end = run * g - p * LANES, run * (g + 1) - p * LANES
            sums[p] = jnp.where((lane >= begin) & (lane < end), value, sums[p])
    row = iota((ROWS, LANES), 0)
    dots = jnp.where(lane == row, jnp.sum(energy[...], axis=1, keepdims=True), 0.0)
    dots = jnp.where(lane == row + ROWS, jnp.sum(acc, axis=1, keepdims=True), dots)
    dots = jnp.sum(dots, axis=0, keepdims=True)
    out[...] = jnp.zeros(out.shape, jnp.float32)
    for n in range(out.shape[0] // (ROWS + 1)):
        out[n * (ROWS + 1) + ROWS] = dots
    for p in range(peers):
        for v in range(ROWS):
            out[peer[p] * (ROWS + 1) + v] = sums[p][v : v + 1]


def edge_scatter_body(cfg, result, idx, inner, out):
    scatter_half(result, inner, idx, out)


def edge_scatter_pick_body(cfg, base_s, node_row, result, idx, inner, out, at_slots):
    edge_scatter_body(cfg, result, idx, inner, out)
    pick(cfg, out, base_s, node_row, at_slots)


RETURN_STEP = 32


def returned_sums(cfg, peer, node_row, recv, left, hot, step):
    windows = cfg["pairs"]
    node, value = node_row[...], received_rows(cfg, peer, recv)
    wide = node.shape[1]
    high, low = parts_of(value, 2)
    lanes = jnp.where(iota((LANES, wide), 0) == (node & (LANES - 1)), 1.0, 0.0).astype(jnp.bfloat16)
    hot[:, :wide] = lanes
    hot[:, wide:] = lanes
    block = spread(node >> 7)
    for start in range(0, windows, step):
        for g in range(start, start + step, 2):
            rows = slice(g * ROWS, (g + 2) * ROWS)
            even, odd = block == g, block == g + 1
            left[rows, :wide] = jnp.concatenate(
                [jnp.where(even, high, 0.0), jnp.where(odd, high, 0.0)], axis=0
            ).astype(jnp.bfloat16)
            left[rows, wide:] = jnp.concatenate(
                [jnp.where(even, low, 0.0), jnp.where(odd, low, 0.0)], axis=0
            ).astype(jnp.bfloat16)
        yield start, nt_dot(left[start * ROWS : (start + step) * ROWS], hot[...])


def dot_totals(recv):
    total = recv[ROWS]
    for n in range(1, recv.shape[0] // (ROWS + 1)):
        total = total + recv[n * (ROWS + 1) + ROWS]
    total = spread(total)
    lane, row = iota((ROWS, LANES), 1), iota((ROWS, LANES), 0)
    return [
        jnp.broadcast_to(
            jnp.sum(jnp.where(lane == row + k * ROWS, total, 0.0), axis=1, keepdims=True), (ROWS, LANES)
        )
        for k in range(2)
    ]


def step_body(cfg, peer_row, recv, right_at, inverse_at, image_at, same, out, coefs):
    peer = peers_of(cfg, peer_row)
    energy_now, curve_now = dot_totals(recv)
    alpha = energy_now / curve_now
    coefs[0] = alpha
    coefs[1] = energy_now
    both = jnp.concatenate(parts_of(received_rows(cfg, peer, recv), 2), axis=0).astype(jnp.bfloat16)
    got = nt_dot(both, same[...])
    image = image_at[...] + (got[:ROWS] + got[ROWS:])
    left_over = right_at[...] - spread_lanes(alpha, image.shape[1]) * image
    out[...] = jnp.zeros(out.shape, jnp.float32)
    put_slots(cfg, peer, left_over * inverse_at[...], out)


def spread_lanes(tile, wide):
    return jnp.concatenate([tile] * (wide // LANES), axis=1)


def window_sums(*operands, step):
    for start, sums in returned_sums(*operands, step):
        for k in range(step):
            yield start + k, sums[k * ROWS : (k + 1) * ROWS]


def next_fields_body(
    cfg, peer_row, node_row, recv, own_hbm, right_hbm, inverse, coefs, w, z1, energy, left, hot, right, own, arrived
):
    fetches = [
        pltpu.make_async_copy(there, here, arrived.at[k]) for k, (there, here) in enumerate(((right_hbm, right), (own_hbm, own)))
    ]
    for fetch in fetches:
        fetch.start()
    peer = peers_of(cfg, peer_row)
    alpha = coefs[0]
    acc = jnp.zeros((ROWS, LANES), jnp.float32)
    for g, sums in window_sums(cfg, peer, node_row, recv, left, hot, step=cfg["pairs"]):
        if g == 0:
            for fetch in fetches:
                fetch.wait()
        cols = slice(g * LANES, (g + 1) * LANES)
        image = own[:, cols] + sums
        w[:, cols] = image
        left_over = right[:, cols] - alpha * image
        scaled = left_over * spread(inverse[g : g + 1, :])
        z1[:, cols] = scaled
        acc = acc + left_over * scaled
    energy[...] = acc


LAST_STEP = 32


def last_body(
    cfg, peer_row, node_row, recv, own, right_hbm, inverse, w_hbm, z1, coefs,
    solution_hbm, residual_hbm, left, hot, right, w, arrived, solution, residual, sent,
):
    fetches = [
        pltpu.make_async_copy(there, here, arrived.at[k]) for k, (there, here) in enumerate(((right_hbm, right), (w_hbm, w)))
    ]
    for fetch in fetches:
        fetch.start()
    peer = peers_of(cfg, peer_row)
    windows = cfg["pairs"]
    energy_next, curve_next = dot_totals(recv)
    alpha, energy_now = coefs[0], coefs[1]
    beta = energy_next / energy_now
    step = energy_next / (curve_next - beta * energy_next / alpha)
    copies = []
    for fetch in fetches:
        fetch.wait()
    for g, sums in window_sums(cfg, peer, node_row, recv, left, hot, step=RETURN_STEP):
        cols = slice(g * LANES, (g + 1) * LANES)
        image = own[:, cols] + sums
        start, before = right[:, cols], w[:, cols]
        z0 = start * spread(inverse[g : g + 1, :])
        residual[:, cols] = (start - alpha * before) - step * (image + beta * before)
        solution[:, cols] = alpha * z0 + step * (z1[:, cols] + beta * z0)
        if (g + 1) % LAST_STEP == 0:
            done = slice((g + 1 - LAST_STEP) * LANES, (g + 1) * LANES)
            for k, (here, there) in enumerate(((solution, solution_hbm), (residual, residual_hbm))):
                copies.append(
                    pltpu.make_async_copy(here.at[:, done], there.at[:, done], sent.at[g // LAST_STEP, k])
                )
                copies[-1].start()
    for copy in copies:
        copy.wait()


def on_device(right_side, stiffness, mass, region, density, elem_nodes, peer_rank, send_nodes):
    vectors, own_count = right_side.shape
    elem_count = elem_nodes.shape[1]
    pairs = elem_count // 2
    edge_pairs = pairs // 2
    peers, slots = send_nodes.shape[1], send_nodes.shape[2]
    devices = lax.axis_size("dom")
    run = peers * slots // edge_pairs
    magic = (1 << 16) // run + 1
    flat = np.arange(ROWS * LANES)
    if (
        vectors != ROWS or own_count != pairs * LANES or slots != LANES or pairs != LANES
        or peers * slots != run * edge_pairs or peers > ROWS or run > LANES
        or ((flat * magic) >> 16 != flat // run).any()
    ):
        raise ValueError("unsupported sizes")
    cfg = dict(
        own=own_count, pairs=pairs, edge_pairs=edge_pairs, peers=peers, run=run, magic=magic,
        window=own_count // pairs,
    )
    f32, i32 = jnp.float32, jnp.int32
    weights1, weights2, squares = constant_operands()
    V, S = vmem(), smem()
    field = ((vectors, own_count), f32)
    tile = ((ROWS, LANES), f32)
    square = ((LANES, LANES), f32)
    half_rows = ((elem_count // 2 * ROWS, LANES), f32)

    def bind(body):
        return functools.partial(body, cfg)

    def exchange(values):
        return lax.all_to_all(values, "dom", split_axis=0, concat_axis=0, tiled=True)

    regions = region.reshape(1, elem_count)
    half_specs = [
        pl.BlockSpec((NPE, LANES), lambda _: (0, 0)),
        pl.BlockSpec((3, NPE, LANES), lambda _: (0, 0, 0)),
        pl.BlockSpec((NPE, LANES), lambda _: (0, 0)),
        pl.BlockSpec((1, LANES), lambda _: (0, 0)),
    ]
    shared = jnp.transpose(send_nodes, (1, 0, 2))
    send, pos, peer_row, base, node_row = call(
        bind(ghost_diag_body), "ghost_diag", [S, S, *half_specs, V, V],
        [
            ((devices, 1, LANES), f32), ((ROWS, LANES), i32), ((1, LANES), i32), ((peers, 1, slots), i32),
            ((1, peers * slots), i32),
        ],
        (1, 2, 4), grid=(1,),
    )(peer_rank, density, elem_nodes, stiffness, mass, regions, squares, shared)
    recv = exchange(send)
    slots_all = ((vectors, peers * slots), f32)
    edge_count = elem_count // 2
    idx, st_edge, mt_edge, st_inner, mt_inner, own_diag, right_at, diag_at, same = call(
        bind(tables_body), "tables", [S, S] + [V] * 5 + [S, V, V],
        [
            ((elem_count, LANES), i32),
            ((edge_count, 3 * LANES), f32), ((edge_count, LANES), f32),
            ((elem_count - edge_count, 3 * LANES), f32), ((elem_count - edge_count, LANES), f32),
            square, slots_all, slots_all, ((peers * slots, peers * slots), jnp.bfloat16),
        ],
        (0, 1, 2, 5, 6, 7, 8),
        [
            pltpu.VMEM((LANES, elem_count), i32), pltpu.VMEM((LANES, elem_count), f32),
            pltpu.VMEM((elem_count, LANES), f32),
        ],
        (8,),
    )(peer_rank, density, elem_nodes, stiffness, mass, regions, squares, base, node_row, right_side)

    send_shape = ((devices, ROWS, LANES), f32)
    send, inverse_at = call(
        bind(start_body), "start", [V] * 5, [send_shape, slots_all], (1,), (), range(5)
    )(peer_row, recv, right_at, diag_at, same)
    diag_recv = recv
    recv = exchange(send)
    inverse, z, energy = call(
        bind(first_fields_body), "first_fields", [V] * 5, [square, field, tile], range(3), (), range(5),
    )(peer_row, node_row, diag_recv, own_diag, right_side)

    weight_rows = [
        pltpu.VMEM((2 * LANES, 6 * LANES), jnp.bfloat16), pltpu.VMEM((6 * LANES, 2 * LANES), jnp.bfloat16)
    ]

    def inner_part(z):
        return call(
            bind(inner_body), "inner", [V] * 6, [half_rows, tile], range(2),
            [pltpu.VMEM(*half_rows), *weight_rows], (0, 1, 4, 5),
        )(z, idx, st_inner, mt_inner, weights1, weights2)

    def edge_part(recv, z, energy, curve):
        return call(
            bind(edge_body), "edge", [V] * 11,
            [half_rows, ((devices * (ROWS + 1), 1, LANES), f32)], (0,),
            [pltpu.VMEM(*half_rows), pltpu.VMEM((peers, ROWS, LANES), f32), *weight_rows], range(11),
        )(peer_row, recv, z, idx, st_edge, mt_edge, pos, weights1, weights2, energy, curve)

    wide = 2 * peers * slots
    scratch = [
        pltpu.VMEM((vectors * pairs, wide), jnp.bfloat16), pltpu.VMEM((LANES, wide), jnp.bfloat16),
        pltpu.VMEM(*field), pltpu.VMEM(*field),
        pltpu.SemaphoreType.DMA((2,)),
    ]
    inner, curve = inner_part(z)
    result, send = edge_part(recv, z, energy, curve)
    recv = exchange(send)
    own, image_at = call(
        bind(edge_scatter_pick_body), "edge_scatter_pick", [S] + [V] * 4, [field, slots_all], (1,), (),
        (1, 2, 3, 4),
    )(base, node_row, result, idx, inner)
    send, coefs = call(
        bind(step_body), "step", [V] * 6, [send_shape, ((2, ROWS, LANES), f32)], (1,), (),
        range(6),
    )(peer_row, recv, right_at, inverse_at, image_at, same)
    sum_recv = recv
    recv = exchange(send)
    w, z, energy = call(
        bind(next_fields_body), "next_fields", [V] * 3 + [hbm(), hbm()] + [V] * 2, [field, field, tile], (1, 2), scratch,
        (0, 1, 2, 5, 6),
    )(peer_row, node_row, sum_recv, own, right_side, inverse, coefs)
    inner, curve = inner_part(z)
    result, send = edge_part(recv, z, energy, curve)
    recv = exchange(send)
    (own,) = call(bind(edge_scatter_body), "edge_scatter", [V] * 3, [field], (0,), (), range(3))(
        result, idx, inner
    )
    return call(
        bind(last_body), "last", [V] * 4 + [hbm(), V, hbm()] + [V] * 2, [field, field], (),
        scratch + [
            pltpu.VMEM(*field), pltpu.VMEM(*field), pltpu.SemaphoreType.DMA((pairs // LAST_STEP, 2)),
        ],
        (0, 1, 2, 3, 5, 7, 8), out_specs=(hbm(), hbm()),
    )(peer_row, node_row, recv, own, right_side, inverse, w, z, coefs)


def solution(mesh):
    placed = (
        P(None, "dom"),
        P(None, None, "dom"),
        P(None, "dom"),
        P("dom"),
        P(),
        P(None, "dom"),
        P("dom", None),
        P("dom", None, None),
    )
    return jax.shard_map(
        on_device,
        mesh=mesh,
        in_specs=placed,
        out_specs=(P(None, "dom"), P(None, "dom")),
        check_vma=False,
    )
```
